32 devices in a mesh: space: 8 (over y, x, core), chan: 4 (over z).
Axes of the slice: x: 2, y: 2, z: 4, core: 2. Of those that a mesh axis runs over, the one named last changes fastest.
Arguments:
- members: bfloat16 [8, 96, 8, 17280], P(None, 'space', 'chan'), may hold values from -400 to 400, as said below
- gain: float32 [768], P('chan'), may hold values from 0.5 to 1.5
- shift: float32 [768], P('chan'), may hold values from -3 to 3
- w_first: bfloat16 [2, 8, 96, 96], P(None, 'chan'), may hold values from -0.4375 to 0.4375
- b_first: float32 [2, 8, 96], P(None, 'chan'), may hold values from -3 to 3
- w_second: bfloat16 [2, 8, 96, 96], P(None, 'chan'), may hold values from -0.4375 to 0.4375
- b_second: float32 [2, 8, 96], P(None, 'chan'), may hold values from -3 to 3
- cotangent: bfloat16 [8, 96, 8, 17280], P(None, 'space', 'chan'), may hold values from -6 to 6
Outputs:
- mixed: bfloat16 [8, 96, 8, 17280], P(None, 'space', 'chan')
- grad_input: bfloat16 [8, 96, 8, 17280], P(None, 'space', 'chan')
- grad_w_first: float32 [2, 8, 96, 96], P(None, 'chan')
- grad_b_first: float32 [2, 8, 96], P(None, 'chan')
- grad_w_second: float32 [2, 8, 96, 96], P(None, 'chan')
- grad_b_second: float32 [2, 8, 96], P(None, 'chan')
- grad_gain: float32 [768], P('chan')
- grad_shift: float32 [768], P('chan')
The draws below stay inside these ranges and needn't reach their ends.
Inputs may be any that keep to these rules, and one draw needn't show every extreme that they name: `members`: real values of varying channel scale.
All inputs are finite; a program needn't handle non-finite values.
Results may differ from the reference program's by a relative error of at most 0.019.
The reference program's roundings to bfloat16 on the way count: a program that leaves them out, or rounds other values in their place, can miss the bound.
Values may be sent and summed in bfloat16 or wider, within the bound.
No kernel may reach another device: no remote copies, remote signals or barrier semaphores. Data moves between devices by JAX's collectives and lax.ppermute only.
A program may use at most 192 MiB of HBM per device.

```python
import math
import jax
import jax.numpy as jnp
from jax import lax

C = 768
NB = 8
H = 96
W = 180
MW = 64
MEMBERS = 8
CB = 96


def stored_layout(tokens):
    split = tokens.reshape((MEMBERS, H, W, NB, C // NB))
    return jnp.transpose(split, (0, 1, 3, 2, 4)).reshape((MEMBERS, H, NB, W * (C // NB)))


def draw_members(key, part):
    key_base, key_rough, key_offset = jax.random.split(key, 3)
    channel_ramp = 3.0 ** (jnp.arange(C, dtype=jnp.float32) / (C - 1))
    channel_rough = jnp.exp(jax.random.uniform(key_rough, (C,), jnp.float32, 0.0, math.log(3.3)))
    channel_offset = jax.random.uniform(key_offset, (C,), jnp.float32, -1.0, 1.0)
    base_draw = jax.random.normal(key_base, (MEMBERS, H, W, C), jnp.float32)
    return stored_layout(0.25 * (base_draw + channel_offset) * channel_ramp * channel_rough).astype(jnp.bfloat16)


def steps_of(stream_key, extent, cuts, low, top_value):
    loudness, own = 1.0, jax.random.fold_in(stream_key, 6)
    for axis_at, shards_of in cuts:
        draws = jnp.exp(jax.random.uniform(jax.random.fold_in(own, axis_at), (shards_of,), jnp.float32, low / len(cuts), top_value / len(cuts)))
        loudness = loudness * jnp.repeat(draws, extent[axis_at] // shards_of).reshape([-1 if axis == axis_at else 1 for axis in range(len(extent))])
    return loudness


def scatter_about(rng, dims, scale, limit, cuts=(), held_as=jnp.bfloat16):
    loudness = steps_of(rng, dims, cuts, -0.22, 0.18) if cuts else 1.0
    entries = jax.random.normal(rng, dims, jnp.float32) * scale * loudness
    return jnp.minimum(jnp.maximum(entries, -limit), limit).astype(held_as)


def setup_inputs(seed: int = 0) -> dict:
    seeds = jax.random.split(jax.random.key(seed), 9)
    return {
        "members": draw_members(jax.random.fold_in(seeds[8], 71), 0),
        "gain": jnp.clip(0.5 + 1.0 * jax.random.uniform(seeds[1], (C,), jnp.float32) ** steps_of(seeds[1], (C,), ((0, 4),), -0.2, 0.2), 0.5, 1.5),
        "shift": scatter_about(seeds[2], (C,), 0.5, 3.0, ((0, 4),), jnp.float32),
        "w_first": scatter_about(seeds[3], (2, NB, CB, CB), (2 * CB) ** -0.5, 0.4375, ((1, 4),)),
        "b_first": scatter_about(seeds[4], (2, NB, CB), 0.5, 3.0, ((1, 4),), jnp.float32),
        "w_second": scatter_about(seeds[5], (2, NB, CB, CB), (2 * CB) ** -0.5, 0.4375, ((1, 4),)),
        "b_second": scatter_about(seeds[6], (2, NB, CB), 0.5, 3.0, ((1, 4),), jnp.float32),
        "cotangent": scatter_about(seeds[7], (MEMBERS, H, NB, W * CB), 1.0, 6.0, ((1, 8), (2, 4))),
    }


shrink_level = 0.05
norm_epsilon = 1e-05
gelu_scale = 0.7978845608
gelu_cubic = 0.044715

def gelu_value(values):
    inner = jnp.tanh(gelu_scale * (values + gelu_cubic * values * values * values))
    return 0.5 * values * (1.0 + inner)

def gelu_slope(values):
    inner = jnp.tanh(gelu_scale * (values + gelu_cubic * values * values * values))
    return 0.5 * (1.0 + inner) + 0.5 * values * (1.0 - inner * inner) * gelu_scale * (1.0 + 3.0 * gelu_cubic * values * values)

def shrink_value(values):
    return values - shrink_level * jnp.tanh(values / shrink_level)

def shrink_slope(values):
    inner = jnp.tanh(values / shrink_level)
    return inner * inner

def twiddle(length, columns):
    row_index = jnp.arange(length, dtype=jnp.int32)[:, None]
    col_index = jnp.arange(columns, dtype=jnp.int32)[None, :]
    angles = (row_index * col_index % length).astype(jnp.float32) * (2.0 * math.pi / length)
    return (jnp.cos(angles).astype(jnp.bfloat16), jnp.sin(angles).astype(jnp.bfloat16))

def product(pattern, first_op, second_op):
    return jnp.einsum(pattern, first_op.astype(jnp.float32), second_op.astype(jnp.float32))

def to_tokens(stored, width):
    lead = stored.shape[:2]
    groups = stored.shape[2]
    columns = stored.shape[3] // width
    split = stored.reshape(lead + (groups, columns, width))
    return jnp.transpose(split, (0, 1, 3, 2, 4)).reshape(lead + (columns, groups * width))

def to_stored(tokens, width):
    lead = tokens.shape[:2]
    columns = tokens.shape[2]
    groups = tokens.shape[3] // width
    split = tokens.reshape(lead + (columns, groups, width))
    return jnp.transpose(split, (0, 1, 3, 2, 4)).reshape(lead + (groups, columns * width))

def latitude_dft(real_part, imag_part, cos_lat, sin_lat, direction):
    factor = 1.0 / math.sqrt(real_part.shape[1])
    pattern = 'kh,bhmc->bkmc'
    out_real = factor * (product(pattern, cos_lat, real_part) - direction * product(pattern, sin_lat, imag_part))
    out_imag = factor * (product(pattern, cos_lat, imag_part) + direction * product(pattern, sin_lat, real_part))
    return (out_real, out_imag)

def as_blocks(values, width):
    return values.reshape(values.shape[:-1] + (values.shape[-1] // width, width))

def from_blocks(values):
    return values.reshape(values.shape[:-2] + (values.shape[-2] * values.shape[-1],))

def complex_apply(real_part, imag_part, weights):
    pattern = 'bkmnc,ncd->bkmnd'
    out_real = product(pattern, real_part, weights[0]) - product(pattern, imag_part, weights[1])
    out_imag = product(pattern, imag_part, weights[0]) + product(pattern, real_part, weights[1])
    return (out_real, out_imag)

def complex_back(real_in, imag_in, grad_real, grad_imag, weights):
    outer = 'bkmnc,bkmnd->ncd'
    grad_weight = jnp.stack([product(outer, real_in, grad_real) + product(outer, imag_in, grad_imag), product(outer, real_in, grad_imag) - product(outer, imag_in, grad_real)])
    grad_bias = jnp.stack([lax.optimization_barrier(jnp.sum(grad_real.astype(jnp.float32), axis=(0, 1, 2))), lax.optimization_barrier(jnp.sum(grad_imag.astype(jnp.float32), axis=(0, 1, 2)))])
    inner = 'bkmnd,ncd->bkmnc'
    back_real = product(inner, grad_real, weights[0]) + product(inner, grad_imag, weights[1])
    back_imag = product(inner, grad_imag, weights[0]) - product(inner, grad_real, weights[1])
    return (grad_weight, grad_bias, back_real, back_imag)

def spectral_forward(lat_real, lat_imag, w_first, b_first, w_second, b_second):
    pre_real, pre_imag = complex_apply(lat_real, lat_imag, w_first)
    pre_real = pre_real + b_first[0]
    pre_imag = pre_imag + b_first[1]
    hidden_real = gelu_value(pre_real).astype(jnp.bfloat16)
    hidden_imag = gelu_value(pre_imag).astype(jnp.bfloat16)
    post_real, post_imag = complex_apply(hidden_real, hidden_imag, w_second)
    post_real = post_real + b_second[0]
    post_imag = post_imag + b_second[1]
    shrunk_real = shrink_value(post_real).astype(jnp.bfloat16)
    shrunk_imag = shrink_value(post_imag).astype(jnp.bfloat16)
    return (shrunk_real, shrunk_imag, (pre_real, pre_imag, hidden_real, hidden_imag, post_real, post_imag))

def spectral_backward(lat_real, lat_imag, saved, grad_real, grad_imag, w_first, w_second):
    pre_real, pre_imag, hidden_real, hidden_imag, post_real, post_imag = saved
    grad_post_real = (grad_real * shrink_slope(post_real)).astype(jnp.bfloat16)
    grad_post_imag = (grad_imag * shrink_slope(post_imag)).astype(jnp.bfloat16)
    grad_w2, grad_b2, grad_hid_real, grad_hid_imag = complex_back(hidden_real, hidden_imag, grad_post_real, grad_post_imag, w_second)
    grad_pre_real = (grad_hid_real * gelu_slope(pre_real)).astype(jnp.bfloat16)
    grad_pre_imag = (grad_hid_imag * gelu_slope(pre_imag)).astype(jnp.bfloat16)
    grad_w1, grad_b1, grad_lat_real, grad_lat_imag = complex_back(lat_real, lat_imag, grad_pre_real, grad_pre_imag, w_first)
    return (grad_w1, grad_b1, grad_w2, grad_b2, grad_lat_real.astype(jnp.bfloat16), grad_lat_imag.astype(jnp.bfloat16))

def reference(members, gain, shift, w_first, b_first, w_second, b_second, cotangent):
    cos_lon, sin_lon = twiddle(W, MW)
    cos_lat, sin_lat = twiddle(H, H)
    lon_factor = 1.0 / math.sqrt(W)
    doubling = jnp.where(jnp.arange(MW) == 0, 1.0, 2.0)
    doubling_half = doubling.astype(jnp.bfloat16)[:, None]
    width = w_first.shape[-1]
    token_members = to_tokens(members, width)
    token_cotangent = to_tokens(cotangent, width)

    def member_step(totals, pair):
        sample, grad_out = pair
        sample = sample[None]
        grad_out = grad_out[None]
        wide = sample.astype(jnp.float32)
        mean_val = lax.optimization_barrier(jnp.sum(wide, -1, keepdims=True)) / C
        square_mean = lax.optimization_barrier(jnp.sum(wide * wide, -1, keepdims=True)) / C
        inv_std = lax.rsqrt(square_mean - mean_val * mean_val + norm_epsilon)
        centred = (wide - mean_val) * inv_std
        normed = (centred * gain + shift).astype(jnp.bfloat16)
        lon_real = (lon_factor * product('bhwc,wm->bhmc', normed, cos_lon)).astype(jnp.bfloat16)
        lon_imag = (-lon_factor * product('bhwc,wm->bhmc', normed, sin_lon)).astype(jnp.bfloat16)
        lat_real, lat_imag = latitude_dft(lon_real, lon_imag, cos_lat, sin_lat, -1.0)
        lat_real = as_blocks(lat_real.astype(jnp.bfloat16), width)
        lat_imag = as_blocks(lat_imag.astype(jnp.bfloat16), width)
        shrunk_real, shrunk_imag, saved = spectral_forward(lat_real, lat_imag, w_first, b_first, w_second, b_second)
        back_real, back_imag = latitude_dft(from_blocks(shrunk_real), from_blocks(shrunk_imag), cos_lat, sin_lat, 1.0)
        rows_real = back_real.astype(jnp.bfloat16) * doubling_half
        rows_imag = back_imag.astype(jnp.bfloat16) * doubling_half
        mixed = (lon_factor * (product('bhmc,wm->bhwc', rows_real, cos_lon) - product('bhmc,wm->bhwc', rows_imag, sin_lon))).astype(jnp.bfloat16)
        grad_back_real = (lon_factor * doubling[:, None] * product('bhwc,wm->bhmc', grad_out, cos_lon)).astype(jnp.bfloat16)
        grad_back_imag = (-lon_factor * doubling[:, None] * product('bhwc,wm->bhmc', grad_out, sin_lon)).astype(jnp.bfloat16)
        grad_shr_real, grad_shr_imag = latitude_dft(grad_back_real, grad_back_imag, cos_lat, sin_lat, -1.0)
        grad_shr_real = as_blocks(grad_shr_real.astype(jnp.bfloat16), width)
        grad_shr_imag = as_blocks(grad_shr_imag.astype(jnp.bfloat16), width)
        grad_w1, grad_b1, grad_w2, grad_b2, grad_lat_real, grad_lat_imag = spectral_backward(lat_real, lat_imag, saved, grad_shr_real, grad_shr_imag, w_first, w_second)
        grad_lon_real, grad_lon_imag = latitude_dft(from_blocks(grad_lat_real), from_blocks(grad_lat_imag), cos_lat, sin_lat, 1.0)
        grad_lon_real = grad_lon_real.astype(jnp.bfloat16)
        grad_lon_imag = grad_lon_imag.astype(jnp.bfloat16)
        grad_normed = lon_factor * (product('bhmc,wm->bhwc', grad_lon_real, cos_lon) - product('bhmc,wm->bhwc', grad_lon_imag, sin_lon))
        grad_gain = lax.optimization_barrier(jnp.sum(grad_normed * centred, axis=(0, 1, 2)))
        grad_shift = lax.optimization_barrier(jnp.sum(grad_normed, axis=(0, 1, 2)))
        grad_centred = grad_normed * gain
        first_mean = lax.optimization_barrier(jnp.sum(grad_centred, -1, keepdims=True)) / C
        second_mean = lax.optimization_barrier(jnp.sum(grad_centred * centred, -1, keepdims=True)) / C
        grad_in = (inv_std * (grad_centred - first_mean - centred * second_mean)).astype(jnp.bfloat16)
        updates = (grad_w1, grad_b1, grad_w2, grad_b2, grad_gain, grad_shift)
        totals = tuple((total + update for total, update in zip(totals, updates)))
        return (totals, (mixed[0], grad_in[0]))
    initial = (jnp.zeros(w_first.shape, jnp.float32), jnp.zeros(b_first.shape, jnp.float32), jnp.zeros(w_second.shape, jnp.float32), jnp.zeros(b_second.shape, jnp.float32), jnp.zeros(gain.shape, jnp.float32), jnp.zeros(shift.shape, jnp.float32))
    totals, outputs = lax.scan(member_step, initial, (token_members, token_cotangent))
    mixed_out = to_stored(outputs[0], width)
    grad_out_stored = to_stored(outputs[1], width)
    return (mixed_out, grad_out_stored, totals[0], totals[1], totals[2], totals[3], totals[4], totals[5])
```

```python
import functools
import math

import jax
import jax.numpy as jnp
import numpy as np
from jax import lax
from jax.experimental import pallas as pl
from jax.experimental.pallas import tpu as pltpu
from jax.sharding import PartitionSpec as P

MW = 64
LANES = 128
PACK = 4

shrink_level = 0.05
norm_epsilon = 1e-05
gelu_scale = 0.7978845608
gelu_cubic = 0.044715

half = jnp.bfloat16
single = jnp.float32
VMEM_LIMIT = 60 * 1024 * 1024
CHUNKS = 2

TN = (((0,), (0,)), ((), ()))
NT = (((1,), (1,)), ((), ()))


def mul(first_op, second_op, dims=(((1,), (0,)), ((), ()))):
    return lax.dot_general(first_op, second_op, dims, preferred_element_type=single)


def trig(length, columns):
    angles = (np.arange(length)[:, None] * np.arange(columns)[None, :] % length).astype(np.float32)
    angles = (angles * np.float32(2.0 * math.pi / length)).astype(np.float64)
    cast = lambda table: table.astype(np.float32).astype(half).astype(np.float32)
    return cast(np.cos(angles)), cast(np.sin(angles))


class Plan:
    def __init__(self, members, width, space, chan):
        self.batch, self.rows, self.groups, self.long = members.shape
        self.width, self.space, self.chan = width, space, chan
        self.lon = self.long // width
        self.lat = self.rows * space
        self.modes = MW // space
        self.stack = PACK // self.groups
        self.packs = self.batch // self.stack
        self.lanes = PACK * width
        self.tiles = self.lanes // LANES
        self.turn = self.lon // PACK
        self.turn_pad = -(-self.turn // 16) * 16
        self.words = self.long // LANES
        self.line = self.rows * self.groups
        self.word_pad = self.tiles * self.turn_pad
        self.channels = self.groups * width * chan


def moved_lanes(p, fetch, from_start, to_start, tile):
    pieces = []
    for slot in range(PACK):
        low = max(to_start(slot), tile * LANES)
        high = min(to_start(slot) + p.width, (tile + 1) * LANES)
        at = low
        while at < high:
            source = at - to_start(slot) + from_start(slot)
            stop = min(high, at + LANES - source % LANES)
            shift = (at - source) % LANES
            pieces.append((stop - tile * LANES, fetch(slot, source // LANES, shift)))
            at = stop
    return pieces


def merged(pieces, lane):
    value = pieces[-1][1]
    for stop, piece in reversed(pieces[:-1]):
        value = jnp.where(lane < stop, piece, value)
    return value


def rolled(value, shift):
    return value if shift == 0 else pltpu.roll(value, shift, 1)


def spread(p, stored_ref, words_ref):
    for s in range(p.stack):
        for t in range(p.words):
            part = stored_ref[s, :, :, t * LANES : (t + 1) * LANES]
            words_ref[s, t * p.line : (t + 1) * p.line, :] = part.reshape(p.line, LANES).astype(single)


def gather_row(p, words_ref, h, put):
    lane = lax.broadcasted_iota(jnp.int32, (p.turn_pad, LANES), 1)
    source = {}
    for q in range(PACK):
        s, n = divmod(q, p.groups)
        for i in range(p.tiles):
            start = i * p.line + h * p.groups + n
            source[q, i] = words_ref[s, pl.ds(start, p.turn_pad, stride=p.tiles * p.line), :]
    for r in range(PACK):
        cache = {}

        def fetch(q, i, shift):
            key = (q, i, shift)
            if key not in cache:
                cache[key] = rolled(source[q, i], shift)
            return cache[key]

        for c in range(p.tiles):
            pieces = moved_lanes(p, fetch, lambda q: r * p.width, lambda q: q * p.width, c)
            put(r, c, merged(pieces, lane))


def scatter_row(p, tokens, words_ref, h):
    lane = lax.broadcasted_iota(jnp.int32, (p.turn_pad, LANES), 1)
    for q in range(PACK):
        s, n = divmod(q, p.groups)

        def fetch(r, c, shift):
            part = tokens[r * p.turn_pad : (r + 1) * p.turn_pad, c * LANES : (c + 1) * LANES]
            return rolled(part, shift)

        for i in range(p.tiles):
            pieces = moved_lanes(p, fetch, lambda r: q * p.width, lambda r: r * p.width, i)
            start = i * p.line + h * p.groups + n
            words_ref[s, pl.ds(start, p.turn_pad, stride=p.tiles * p.line), :] = merged(pieces, lane)


def store_words(p, words_ref, stored_ref):
    for s in range(p.stack):
        for t in range(p.words):
            part = words_ref[s, t * p.line : (t + 1) * p.line, :]
            stored_ref[s, :, :, t * LANES : (t + 1) * LANES] = part.reshape(
                p.rows, p.groups, LANES
            ).astype(half)


def clear_tail(p, words_ref):
    @pl.when(pl.program_id(0) == 0)
    def _():
        tail = (p.word_pad - p.words) * p.line
        words_ref[:, p.words * p.line :, :] = jnp.zeros((p.stack, tail, LANES), single)


def analyse(p, tokens, table, scale, turn_ref, h):
    spectrum = mul(table, tokens) * scale
    for c in range(p.tiles):
        for ri in range(2):
            turn_ref[c, pl.ds(ri * p.rows + h, MW, stride=2 * p.rows), :] = spectrum[
                ri * MW : (ri + 1) * MW, c * LANES : (c + 1) * LANES
            ]


def send_turn(p, turn_ref, out_ref, outer, inner):
    count = outer * inner
    for d in range(p.space):
        for c in range(p.tiles):
            part = turn_ref[c, d * count : (d + 1) * count, :].reshape(outer, inner, LANES)
            out_ref[d, 0, :, :, c * LANES : (c + 1) * LANES] = part.astype(half)


def split_three(value):
    high = value.astype(half).astype(single)
    rest = value - high
    middle = rest.astype(half).astype(single)
    return high, middle, rest - middle


def expand(parts, spread_table):
    stacked = jnp.concatenate(split_three(parts), axis=0).astype(half)
    return mul(stacked, spread_table, TN)


def summed(table, value):
    high = value.astype(half)
    low = (value - high.astype(single)).astype(half)
    return mul(table, high, NT) + mul(table, low, NT)


def cotangent_kernel(p, stored_ref, table_ref, scale_ref, out_ref, words_ref, turn_ref, tokens_ref):
    clear_tail(p, words_ref)
    spread(p, stored_ref, words_ref)

    def row(h, carry):
        def put(r, c, value):
            tokens_ref[r * p.turn_pad : (r + 1) * p.turn_pad, c * LANES : (c + 1) * LANES] = (
                value.astype(half)
            )

        gather_row(p, words_ref, h, put)
        analyse(p, tokens_ref[...], table_ref[...], scale_ref[...], turn_ref, h)
        return carry

    lax.fori_loop(0, p.rows, row, 0)
    send_turn(p, turn_ref, out_ref, p.modes, 2 * p.rows)


def stats_kernel(p, stored_ref, sum_ref, tokens_ref, stat_ref, words_ref, rows_ref):
    clear_tail(p, words_ref)
    spread(p, stored_ref, words_ref)
    count = 2 * p.stack

    def row(h, carry):
        def put(r, c, value):
            tokens_ref[
                0, h, r * p.turn_pad : (r + 1) * p.turn_pad, c * LANES : (c + 1) * LANES
            ] = value.astype(half)

        gather_row(p, words_ref, h, put)
        tokens = tokens_ref[0, h]
        wide = tokens.astype(single)
        plain = mul(sum_ref[0], tokens, NT)
        rows_ref[h] = plain + summed(sum_ref[1], wide * wide)
        return carry

    lax.fori_loop(0, p.rows, row, 0)
    for h in range(p.rows):
        stat_ref[0, h * count : (h + 1) * count, :] = rows_ref[h, :count, :]


def moments(p, stat_refs, rows_ref):
    count = 2 * p.stack
    total = stat_refs[0][0]
    for ref in stat_refs[1:]:
        total = total + ref[0]
    for h in range(p.rows):
        part = total[h * count : (h + 1) * count] * (1.0 / p.channels)
        mean, square = part[: p.stack], part[p.stack :]
        inverse = lax.rsqrt(square - mean * mean + norm_epsilon)
        rows_ref[h, : p.stack, :] = mean
        rows_ref[h, p.stack : count, :] = inverse
        if count < 8:
            rows_ref[h, count:, :] = jnp.zeros((8 - count, p.turn_pad * PACK), single)


def normalise_kernel(p, *refs):
    stat_refs = refs[: p.chan]
    tokens_ref, gain_ref, shift_ref, table_ref, scale_ref, wide_ref = refs[p.chan : p.chan + 6]
    out_ref, rows_ref, turn_ref = refs[p.chan + 6 :]
    moments(p, stat_refs, rows_ref)

    def row(h, carry):
        each = expand(rows_ref[h], wide_ref[...])
        wide = tokens_ref[0, h].astype(single)
        centred = (wide - each[:, : p.lanes]) * each[:, p.lanes :]
        normed = (centred * gain_ref[...] + shift_ref[...]).astype(half)
        analyse(p, normed, table_ref[...], scale_ref[...], turn_ref, h)
        return carry

    lax.fori_loop(0, p.rows, row, 0)
    send_turn(p, turn_ref, out_ref, p.modes, 2 * p.rows)


def gelu_both(values):
    inner = jnp.tanh(gelu_scale * (values + gelu_cubic * values * values * values))
    hidden = 0.5 * values * (1.0 + inner)
    slope = 0.5 * (1.0 + inner) + 0.5 * values * (1.0 - inner * inner) * gelu_scale * (
        1.0 + 3.0 * gelu_cubic * values * values
    )
    return hidden, slope


BAND = 16


def spectral_kernel(
    p,
    step_modes,
    x_ref,
    g_ref,
    there_ref,
    back_ref,
    w1_ref,
    w2_ref,
    bias_ref,
    y_ref,
    dx_ref,
    gw_ref,
    gb_ref,
    lat_ref,
    hid_ref,
    gpost_ref,
    gpre_ref,
    wide_ref,
    slope_ref,
    gsh_ref,
    shr_ref,
    turn_y_ref,
    turn_x_ref,
    acc1_ref,
    acc2_ref,
):
    pack, group = pl.program_id(0), pl.program_id(1)
    count = step_modes * p.lat
    factor = 1.0 / math.sqrt(p.lat)
    base = pl.multiple_of(group * count, count)

    @pl.when((pack == 0) & (group == 0))
    def _():
        gb_ref[...] = jnp.zeros_like(gb_ref)
        acc1_ref[...] = jnp.zeros_like(acc1_ref)
        acc2_ref[...] = jnp.zeros_like(acc2_ref)

    def there(ref, into, offset):
        for m in range(step_modes):
            block = ref[:, 0, m].reshape(2 * p.lat, p.lanes)
            out = (mul(there_ref[...], block) * factor).astype(half)
            at = pl.ds(offset + m * p.lat, p.lat)
            into[at, : p.lanes] = out[: p.lat]
            into[at, p.lanes :] = out[p.lat :]

    def back(value_of, turn_ref):
        for m in range(step_modes):
            rows = slice(m * p.lat, (m + 1) * p.lat)
            both = jnp.concatenate([value_of(rows, 0), value_of(rows, 1)], axis=0)
            out = mul(back_ref[...], both) * factor
            mode = group * step_modes + m
            for ri in range(2):
                for c in range(p.tiles):
                    turn_ref[c, pl.ds(ri * p.modes + mode, p.lat, stride=2 * p.modes), :] = out[
                        ri * p.lat : (ri + 1) * p.lat, c * LANES : (c + 1) * LANES
                    ]

    there(x_ref, lat_ref, base)
    there(g_ref, gsh_ref, 0)
    wide_ref[...] = mul(lat_ref[pl.ds(base, count), :], w1_ref[...])

    def first(i, carry):
        at = pl.ds(pl.multiple_of(i * BAND, BAND), BAND)
        hidden, slope = gelu_both(wide_ref[at, :] + bias_ref[0:1, :])
        hid_ref[pl.ds(pl.multiple_of(base + i * BAND, BAND), BAND), :] = hidden.astype(half)
        slope_ref[at, :] = slope
        return carry

    lax.fori_loop(0, count // BAND, first, 0)
    wide_ref[...] = mul(hid_ref[pl.ds(base, count), :], w2_ref[...])

    def second(i, carry):
        at = pl.ds(pl.multiple_of(i * BAND, BAND), BAND)
        post = wide_ref[at, :] + bias_ref[1:2, :]
        inner = jnp.tanh(post * (1.0 / shrink_level))
        shr_ref[at, :] = (post - shrink_level * inner).astype(half)
        gpost = (gsh_ref[at, :].astype(single) * (inner * inner)).astype(half)
        gpost_ref[pl.ds(pl.multiple_of(base + i * BAND, BAND), BAND), :] = gpost
        gb_ref[8:16, :] += gpost.astype(single).reshape(BAND // 8, 8, 2 * p.lanes).sum(0)
        return carry

    lax.fori_loop(0, count // BAND, second, 0)
    back(lambda rows, ri: shr_ref[rows, ri * p.lanes : (ri + 1) * p.lanes], turn_y_ref)
    wide_ref[...] = mul(gpost_ref[pl.ds(base, count), :], w2_ref[...], NT)

    def third(i, carry):
        at = pl.ds(pl.multiple_of(i * BAND, BAND), BAND)
        gpre = (wide_ref[at, :] * slope_ref[at, :]).astype(half)
        gpre_ref[pl.ds(pl.multiple_of(base + i * BAND, BAND), BAND), :] = gpre
        gb_ref[0:8, :] += gpre.astype(single).reshape(BAND // 8, 8, 2 * p.lanes).sum(0)
        return carry

    lax.fori_loop(0, count // BAND, third, 0)
    shr_ref[...] = mul(gpre_ref[pl.ds(base, count), :], w1_ref[...], NT).astype(half)
    back(lambda rows, ri: shr_ref[rows, ri * p.lanes : (ri + 1) * p.lanes], turn_x_ref)

    @pl.when(group == pl.num_programs(1) - 1)
    def _():
        send_turn(p, turn_y_ref, y_ref, p.rows, 2 * p.modes)
        send_turn(p, turn_x_ref, dx_ref, p.rows, 2 * p.modes)
        acc1_ref[...] += mul(lat_ref[...], gpre_ref[...], TN)
        acc2_ref[...] += mul(hid_ref[...], gpost_ref[...], TN)

    @pl.when((group == pl.num_programs(1) - 1) & (pack == pl.num_programs(0) - 1))
    def _():
        for which, acc in enumerate((acc1_ref, acc2_ref)):
            for n in range(p.groups):
                for part in range(2):
                    total = jnp.zeros((p.width, LANES), single)
                    for s in range(p.stack):
                        q = s * p.groups + n
                        for row_ri, col_ri, sign in (((0, 0, 1), (1, 1, 1)), ((0, 1, 1), (1, 0, -1)))[part]:
                            top = row_ri * p.lanes + q * p.width
                            left = col_ri * p.lanes + q * p.width
                            tile = left // LANES
                            value = rolled(
                                acc[top : top + p.width, tile * LANES : (tile + 1) * LANES],
                                -left % LANES,
                            )
                            if left % LANES + p.width > LANES:
                                nxt = acc[
                                    top : top + p.width, (tile + 1) * LANES : (tile + 2) * LANES
                                ]
                                lane = lax.broadcasted_iota(jnp.int32, (p.width, LANES), 1)
                                value = jnp.where(
                                    lane < LANES - left % LANES, value, rolled(nxt, -left % LANES)
                                )
                            total = total + sign * value
                    gw_ref[which, part, n] = total


def mixed_kernel(p, rows_ref, table_ref, out_ref, words_ref):
    factor = 1.0 / math.sqrt(p.lon)

    def row(h, carry):
        block = rows_ref[:, 0, h].reshape(2 * MW, p.lanes)
        tokens = mul(table_ref[...], block) * factor
        scatter_row(p, tokens, words_ref, h)
        return carry

    lax.fori_loop(0, p.rows, row, 0)
    store_words(p, words_ref, out_ref)


def slope_sums_kernel(p, *refs):
    stat_refs = refs[: p.chan]
    rows_in_ref, tokens_ref, gain_ref, table_ref, wide_ref, sum_ref = refs[p.chan : p.chan + 6]
    sums_ref, param_ref, rows_ref, part_ref = refs[p.chan + 6 :]
    factor = 1.0 / math.sqrt(p.lon)
    count = 2 * p.stack
    moments(p, stat_refs, rows_ref)

    @pl.when(pl.program_id(0) == 0)
    def _():
        param_ref[...] = jnp.zeros_like(param_ref)

    def row(h, carry):
        block = rows_in_ref[:, 0, h].reshape(2 * MW, p.lanes)
        normed_grad = mul(table_ref[...], block) * factor
        each = expand(rows_ref[h], wide_ref[...])
        wide = tokens_ref[0, h].astype(single)
        centred = (wide - each[:, : p.lanes]) * each[:, p.lanes :]
        product = normed_grad * centred
        folds = (PACK * p.turn_pad // 8, 8, p.lanes)
        param_ref[0:8, :] += product.reshape(folds).sum(0)
        param_ref[8:16, :] += normed_grad.reshape(folds).sum(0)
        gain = gain_ref[...]
        part_ref[h] = summed(sum_ref[0], normed_grad * gain) + summed(sum_ref[1], product * gain)
        return carry

    lax.fori_loop(0, p.rows, row, 0)
    for h in range(p.rows):
        sums_ref[0, h * count : (h + 1) * count, :] = part_ref[h, :count, :]


def input_grad_kernel(p, *refs):
    stat_refs, part_refs = refs[: p.chan], refs[p.chan : 2 * p.chan]
    rows_in_ref, tokens_ref, gain_ref, table_ref, wide_ref = refs[2 * p.chan : 2 * p.chan + 5]
    out_ref, rows_ref, part_ref, words_ref = refs[2 * p.chan + 5 :]
    factor = 1.0 / math.sqrt(p.lon)
    count = 2 * p.stack
    moments(p, stat_refs, rows_ref)
    total = part_refs[0][0].astype(single)
    for ref in part_refs[1:]:
        total = total + ref[0].astype(single)
    for h in range(p.rows):
        part_ref[h, :count, :] = total[h * count : (h + 1) * count] * (1.0 / p.channels)
        if count < 8:
            part_ref[h, count:, :] = jnp.zeros((8 - count, p.turn_pad * PACK), single)

    def row(h, carry):
        block = rows_in_ref[:, 0, h].reshape(2 * MW, p.lanes)
        normed_grad = mul(table_ref[...], block) * factor
        each = expand(rows_ref[h], wide_ref[...])
        means = expand(part_ref[h], wide_ref[...])
        inverse = each[:, p.lanes :]
        centred = (tokens_ref[0, h].astype(single) - each[:, : p.lanes]) * inverse
        grad = inverse * (
            normed_grad * gain_ref[...] - means[:, : p.lanes] - centred * means[:, p.lanes :]
        )
        scatter_row(p, grad, words_ref, h)
        return carry

    lax.fori_loop(0, p.rows, row, 0)
    store_words(p, words_ref, out_ref)


def whole_spec(value):
    dims = value.shape
    return pl.BlockSpec(dims, lambda *_: (0,) * len(dims))


def pack_spec(value, offset=0):
    dims = (1,) + value.shape[1:]
    return pl.BlockSpec(dims, lambda b, *_: (b + offset,) + (0,) * (len(dims) - 1))


def peer_spec(value):
    dims = (value.shape[0], 1) + value.shape[2:]
    return pl.BlockSpec(dims, lambda b, *_: (0, b) + (0,) * (len(dims) - 2))


def stored_spec(p, offset):
    return pl.BlockSpec(
        (p.stack, p.rows, p.groups, p.long), lambda b, *_: (b + offset, 0, 0, 0)
    )


def call(p, body, name, grid, ins, in_specs, outs, out_specs, scratch, flops, aliases=None):
    moved = sum(v.size * v.dtype.itemsize for v in ins) + sum(
        math.prod(o.shape) * o.dtype.itemsize for o in outs
    )
    return pl.pallas_call(
        body,
        name=name,
        grid=grid,
        in_specs=in_specs,
        out_specs=out_specs,
        out_shape=outs,
        scratch_shapes=scratch,
        input_output_aliases=aliases or {},
        compiler_params=pltpu.CompilerParams(vmem_limit_bytes=VMEM_LIMIT),
        cost_estimate=pl.CostEstimate(flops=flops, bytes_accessed=moved, transcendentals=0),
    )(*ins)


def lon_tables(p):
    cos_lon, sin_lon = trig(p.lon, MW)
    wave = np.concatenate([cos_lon, -sin_lon], axis=1)
    turned = np.zeros((PACK, p.turn_pad, 2 * MW), np.float32)
    turned[:, : p.turn] = wave.reshape(p.turn, PACK, 2 * MW).transpose(1, 0, 2)
    turned = turned.reshape(PACK * p.turn_pad, 2 * MW)
    doubling = np.where(np.arange(MW) == 0, 1.0, 2.0).astype(np.float32)
    factor = np.float32(1.0 / math.sqrt(p.lon))
    plain_scale = np.full((2 * MW, 1), factor, np.float32)
    double_scale = (factor * np.tile(doubling, 2))[:, None].astype(np.float32)
    owner = turned.reshape(-1, 2, p.space, p.modes).transpose(0, 2, 1, 3).reshape(-1, 2 * MW)
    twice = np.tile(doubling.reshape(p.space, 1, p.modes), (1, 2, 1)).reshape(1, 2 * MW)
    to_half = lambda value: jnp.asarray(value, half)
    return (
        to_half(turned.T),
        jnp.asarray(plain_scale),
        jnp.asarray(double_scale),
        to_half(owner * twice),
        to_half(owner),
    )


def lat_tables(p):
    cos_lat, sin_lat = trig(p.lat, p.lat)
    there = np.block([[cos_lat, sin_lat], [-sin_lat, cos_lat]])
    there = there.reshape(2 * p.lat, 2, p.space, p.rows).transpose(0, 2, 1, 3)
    back = np.block([[cos_lat.T, -sin_lat.T], [sin_lat.T, cos_lat.T]])
    return jnp.asarray(there.reshape(2 * p.lat, 2 * p.lat), half), jnp.asarray(back, half)


def sum_tables(p):
    owner = np.arange(PACK) // p.groups
    lane_owner = np.repeat(owner, p.width)
    sums = np.zeros((2, 8, p.lanes), np.float32)
    wide = np.zeros((3, 8, 2, p.lanes), np.float32)
    for s in range(p.stack):
        sums[0, s] = lane_owner == s
        sums[1, p.stack + s] = lane_owner == s
        wide[:, s, 0] = lane_owner == s
        wide[:, p.stack + s, 1] = lane_owner == s
    return jnp.asarray(sums, half), jnp.asarray(wide.reshape(24, 2 * p.lanes), half)


def block_weights(p, weights):
    each = jnp.tile(weights, (1, p.stack, 1, 1))
    eye = jnp.eye(PACK, dtype=weights.dtype)
    wide = (each[:, :, :, None, :] * eye[None, :, None, :, None]).reshape(2, p.lanes, p.lanes)
    top = jnp.concatenate([wide[0], wide[1]], axis=1)
    bottom = jnp.concatenate([-wide[1], wide[0]], axis=1)
    return jnp.concatenate([top, bottom], axis=0)


def lane_vector(p, vector):
    return jnp.tile(vector, p.stack)[None, :]


def exchange(value):
    return lax.all_to_all(value, "space", 0, 0, tiled=True)


def around(value, axis, size):
    gathered = [value]
    for step in range(1, size):
        gathered.append(
            lax.ppermute(value, axis, [(i, (i + step) % size) for i in range(size)])
        )
    return gathered


def reduced(p, value):
    length = value.shape[0]
    unit = p.space * LANES * 16
    padded = jnp.pad(value, (0, -length % unit)).astype(half).reshape(p.space, -1, LANES)
    part = exchange(padded).astype(single).sum(0)
    every = jnp.broadcast_to(part.astype(half)[None], padded.shape)
    return exchange(every).reshape(-1)[:length].astype(single)


def on_device(space, chan, members, gain, shift, w_first, b_first, w_second, b_second, cotangent):
    p = Plan(members, w_first.shape[-1], space, chan)
    chunks = CHUNKS if p.packs % CHUNKS == 0 else 1
    size = p.packs // chunks
    grid = (size,)
    table, plain_scale, double_scale, mixed_table, slope_table = lon_tables(p)
    there_table, back_table = lat_tables(p)
    sum_table, wide_table = sum_tables(p)
    gain_lanes, shift_lanes = lane_vector(p, gain), lane_vector(p, shift)
    w1, w2 = block_weights(p, w_first), block_weights(p, w_second)
    bias = jnp.stack(
        [jnp.tile(b.reshape(2, -1), (1, p.stack)).reshape(-1) for b in (b_first, b_second)]
    )
    tokens_rows = PACK * p.turn_pad
    dft_flops = 2 * size * p.rows * tokens_rows * 2 * MW * p.lanes
    words = pltpu.VMEM((p.stack, p.word_pad * p.line, LANES), single)
    turn_in = pltpu.VMEM((p.tiles, MW * 2 * p.rows, LANES), single)
    rows_scratch = pltpu.VMEM((p.rows, 8, tokens_rows), single)
    sent = jax.ShapeDtypeStruct((space, size, p.modes, 2 * p.rows, p.lanes), half)
    returned = jax.ShapeDtypeStruct((space, size, p.rows, 2 * p.modes, p.lanes), half)
    count = 2 * p.stack * p.rows
    stored = jax.ShapeDtypeStruct(members.shape, half)

    def cotangent_chunk(c):
        ins = (cotangent, table, double_scale)
        return call(
            p, functools.partial(cotangent_kernel, p), f"cot{c}", grid, ins,
            [stored_spec(p, c * size), whole_spec(table), whole_spec(double_scale)],
            [sent], [peer_spec(sent)],
            [words, turn_in, pltpu.VMEM((tokens_rows, p.lanes), half)], dft_flops,
        )[0]

    def stats_chunk(c):
        ins = (members, sum_table)
        outs = [
            jax.ShapeDtypeStruct((size, p.rows, tokens_rows, p.lanes), half),
            jax.ShapeDtypeStruct((size, count, tokens_rows), single),
        ]
        return call(
            p, functools.partial(stats_kernel, p), f"stats{c}", grid, ins,
            [stored_spec(p, c * size), whole_spec(sum_table)],
            outs, [pack_spec(o) for o in outs], [words, rows_scratch], dft_flops // 4,
        )

    def normalise_chunk(c, stats, tokens):
        tail = (gain_lanes, shift_lanes, table, plain_scale, wide_table)
        return call(
            p, functools.partial(normalise_kernel, p), f"norm{c}", grid, (*stats, tokens, *tail),
            [pack_spec(s) for s in stats] + [pack_spec(tokens)] + [whole_spec(v) for v in tail],
            [sent], [peer_spec(sent)], [rows_scratch, turn_in], dft_flops,
        )[0]

    step_modes = 2 if p.modes % 2 == 0 else 1
    wide_lanes = 2 * p.lanes

    def spectral_chunk(c, x_in, g_in):
        tail = (there_table, back_table, w1, w2, bias)
        mode_spec = pl.BlockSpec(
            (space, 1, step_modes, 2 * p.rows, p.lanes), lambda b, m: (0, b, m, 0, 0)
        )
        grads = jax.ShapeDtypeStruct((2, 2, p.groups, p.width, LANES), single)
        bias_grads = jax.ShapeDtypeStruct((16, wide_lanes), single)
        kept = pltpu.VMEM((p.modes * p.lat, wide_lanes), half)
        held = pltpu.VMEM((step_modes * p.lat, wide_lanes), single)
        brief = pltpu.VMEM((step_modes * p.lat, wide_lanes), half)
        turn_out = pltpu.VMEM((p.tiles, p.lat * 2 * p.modes, LANES), single)
        return call(
            p, functools.partial(spectral_kernel, p, step_modes), f"spec{c}",
            (size, p.modes // step_modes), (x_in, g_in, *tail),
            [mode_spec, mode_spec] + [whole_spec(v) for v in tail],
            [returned, returned, grads, bias_grads],
            [peer_spec(returned), peer_spec(returned), whole_spec(grads), whole_spec(bias_grads)],
            [kept] * 4 + [held] * 2 + [brief] * 2 + [turn_out] * 2
            + [pltpu.VMEM((wide_lanes, wide_lanes), single)] * 2,
            12 * size * p.modes * p.lat * wide_lanes * wide_lanes,
        )

    def with_result(body, before):
        if before is None:
            return body, (), [], {}
        wrapped = lambda n, *refs: body(*refs[:n], *refs[n + 1 :])
        return wrapped, (before,), [pl.BlockSpec(memory_space=pl.ANY)], None

    def out_call(body, name, c, ins, specs, scratch, before, flops):
        ins, specs = list(ins), list(specs)
        aliases = {}
        inner = body
        if before is not None:
            place = len(ins)
            inner = lambda *refs: body(*refs[:place], *refs[place + 1 :])
            ins.append(before)
            specs.append(pl.BlockSpec(memory_space=pl.ANY))
            aliases = {place: 0}
        return call(
            p, inner, name, grid, tuple(ins), specs, [stored], [stored_spec(p, c * size)],
            scratch, flops, aliases,
        )[0]

    def mixed_chunk(c, rows_in, before):
        return out_call(
            functools.partial(mixed_kernel, p), f"mix{c}", c, (rows_in, mixed_table),
            [peer_spec(rows_in), whole_spec(mixed_table)], [words], before, dft_flops,
        )

    def slope_sums_chunk(c, stats, rows_in, tokens):
        tail = (gain_lanes, slope_table, wide_table, sum_table)
        outs = [
            jax.ShapeDtypeStruct((size, count, tokens_rows), single),
            jax.ShapeDtypeStruct((16, p.lanes), single),
        ]
        return call(
            p, functools.partial(slope_sums_kernel, p), f"sums{c}", grid,
            (*stats, rows_in, tokens, *tail),
            [pack_spec(s) for s in stats] + [peer_spec(rows_in), pack_spec(tokens)]
            + [whole_spec(v) for v in tail],
            outs, [pack_spec(outs[0]), whole_spec(outs[1])], [rows_scratch, rows_scratch],
            dft_flops,
        )

    def input_grad_chunk(c, stats, parts, rows_in, tokens, before):
        tail = (gain_lanes, slope_table, wide_table)
        return out_call(
            functools.partial(input_grad_kernel, p), f"grad{c}", c,
            (*stats, *parts, rows_in, tokens, *tail),
            [pack_spec(s) for s in (*stats, *parts)] + [peer_spec(rows_in), pack_spec(tokens)]
            + [whole_spec(v) for v in tail],
            [rows_scratch, rows_scratch, words], before, dft_flops,
        )

    everyone = range(chunks)
    g_in = [exchange(cotangent_chunk(c)) for c in everyone]
    first = [stats_chunk(c) for c in everyone]
    stats = [around(s, "chan", chan) for _, s in first]
    x_in = [exchange(normalise_chunk(c, stats[c], first[c][0])) for c in everyone]
    mixed = grad_input = None
    weight_grads = bias_grads = param_grads = 0.0
    spectra = [spectral_chunk(c, x_in[c], g_in[c]) for c in everyone]
    for c in everyone:
        y_out, dx_out, gw, gb = spectra[c]
        weight_grads, bias_grads = weight_grads + gw, bias_grads + gb
        dx_rows = exchange(dx_out)
        y_rows = exchange(y_out)
        sums, params = slope_sums_chunk(c, stats[c], dx_rows, first[c][0])
        param_grads = param_grads + params
        parts = around(sums.astype(half), "chan", chan)
        grad_input = input_grad_chunk(c, stats[c], parts, dx_rows, first[c][0], grad_input)
        mixed = mixed_chunk(c, y_rows, mixed)

    def by_channel(rows):
        return rows.reshape(-1, p.stack, p.groups * p.width).sum(1)

    flat_bias = bias_grads.reshape(2, 8, 2, p.stack, p.groups * p.width).sum((1, 3))
    flat_params = by_channel(param_grads.reshape(2, 8, p.lanes).sum(1))
    flat = jnp.concatenate([weight_grads[..., : p.width].reshape(-1), flat_bias.reshape(-1)])
    flat = reduced(p, flat)
    size_w = w_first.size
    size_b = b_first.size
    grad_w1 = flat[:size_w].reshape(w_first.shape)
    grad_w2 = flat[size_w : 2 * size_w].reshape(w_first.shape)
    grad_b1 = flat[2 * size_w : 2 * size_w + size_b].reshape(b_first.shape)
    grad_b2 = flat[2 * size_w + size_b : 2 * size_w + 2 * size_b].reshape(b_first.shape)
    both = reduced(p, flat_params.reshape(-1)).reshape(2, -1)
    return (mixed, grad_input, grad_w1, grad_b1, grad_w2, grad_b2, both[0], both[1])


def solution(mesh):
    tokens = P(None, "space", "chan", None)
    weights = P(None, "chan", None, None)
    biases = P(None, "chan", None)
    placed = (tokens, P("chan"), P("chan"), weights, biases, weights, biases, tokens)
    return jax.shard_map(
        functools.partial(on_device, mesh.shape["space"], mesh.shape["chan"]),
        mesh=mesh,
        in_specs=placed,
        out_specs=(tokens, tokens, weights, biases, weights, biases, P("chan"), P("chan")),
        check_vma=False,
    )
```

```python
import functools
import math

import jax
import jax.numpy as jnp
import numpy as np
from jax import lax
from jax.experimental import pallas as pl
from jax.experimental.pallas import tpu as pltpu
from jax.sharding import PartitionSpec as P


MW = 64
LANES = 128
PACK = 4

shrink_level = 0.05
norm_epsilon = 1e-05
gelu_scale = 0.7978845608
gelu_cubic = 0.044715

half = jnp.bfloat16
single = jnp.float32
VMEM_LIMIT = 60 * 1024 * 1024
CHUNKS = 2

TN = (((0,), (0,)), ((), ()))
NT = (((1,), (1,)), ((), ()))


def mul(first_op, second_op, dims=(((1,), (0,)), ((), ()))):
    return lax.dot_general(first_op, second_op, dims, preferred_element_type=single)


def trig(length, columns):
    angles = (np.arange(length)[:, None] * np.arange(columns)[None, :] % length).astype(np.float32)
    angles = (angles * np.float32(2.0 * math.pi / length)).astype(np.float64)
    cast = lambda table: table.astype(np.float32).astype(half).astype(np.float32)
    return cast(np.cos(angles)), cast(np.sin(angles))


class Plan:
    def __init__(self, members, width, space, chan):
        self.batch, self.rows, self.groups, self.long = members.shape
        self.width, self.space, self.chan = width, space, chan
        self.lon = self.long // width
        self.lat = self.rows * space
        self.modes = MW // space
        self.stack = PACK // self.groups
        self.packs = self.batch // self.stack
        self.lanes = PACK * width
        self.tiles = self.lanes // LANES
        self.turn = self.lon // PACK
        self.turn_pad = -(-self.turn // 16) * 16
        self.words = self.long // LANES
        self.line = self.rows * self.groups
        self.word_pad = self.tiles * self.turn_pad
        self.channels = self.groups * width * chan


def moved_lanes(p, fetch, from_start, to_start, tile):
    pieces = []
    for slot in range(PACK):
        low = max(to_start(slot), tile * LANES)
        high = min(to_start(slot) + p.width, (tile + 1) * LANES)
        at = low
        while at < high:
            source = at - to_start(slot) + from_start(slot)
            stop = min(high, at + LANES - source % LANES)
            shift = (at - source) % LANES
            pieces.append((stop - tile * LANES, fetch(slot, source // LANES, shift)))
            at = stop
    return pieces


def merged(pieces, lane):
    value = pieces[-1][1]
    for stop, piece in reversed(pieces[:-1]):
        value = jnp.where(lane < stop, piece, value)
    return value


def rolled(value, shift):
    return value if shift == 0 else pltpu.roll(value, shift, 1)


def spread(p, stored_ref, words_ref):
    for s in range(p.stack):
        for t in range(p.words):
            part = stored_ref[s, :, :, t * LANES : (t + 1) * LANES]
            words_ref[s, t * p.line : (t + 1) * p.line, :] = part.reshape(p.line, LANES).astype(single)


def gather_row(p, words_ref, h, put):
    lane = lax.broadcasted_iota(jnp.int32, (p.turn_pad, LANES), 1)
    source = {}
    for q in range(PACK):
        s, n = divmod(q, p.groups)
        for i in range(p.tiles):
            start = i * p.line + h * p.groups + n
            source[q, i] = words_ref[s, pl.ds(start, p.turn_pad, stride=p.tiles * p.line), :]
    for r in range(PACK):
        cache = {}

        def fetch(q, i, shift):
            key = (q, i, shift)
            if key not in cache:
                cache[key] = rolled(source[q, i], shift)
            return cache[key]

        for c in range(p.tiles):
            pieces = moved_lanes(p, fetch, lambda q: r * p.width, lambda q: q * p.width, c)
            put(r, c, merged(pieces, lane))


def scatter_row(p, tokens, words_ref, h):
    lane = lax.broadcasted_iota(jnp.int32, (p.turn_pad, LANES), 1)
    for q in range(PACK):
        s, n = divmod(q, p.groups)

        def fetch(r, c, shift):
            part = tokens[r * p.turn_pad : (r + 1) * p.turn_pad, c * LANES : (c + 1) * LANES]
            return rolled(part, shift)

        for i in range(p.tiles):
            pieces = moved_lanes(p, fetch, lambda r: q * p.width, lambda r: r * p.width, i)
            start = i * p.line + h * p.groups + n
            words_ref[s, pl.ds(start, p.turn_pad, stride=p.tiles * p.line), :] = merged(pieces, lane)


def store_words(p, words_ref, stored_ref):
    for s in range(p.stack):
        for t in range(p.words):
            part = words_ref[s, t * p.line : (t + 1) * p.line, :]
            stored_ref[s, :, :, t * LANES : (t + 1) * LANES] = part.reshape(
                p.rows, p.groups, LANES
            ).astype(half)


def clear_tail(p, words_ref):
    @pl.when(pl.program_id(0) == 0)
    def _():
        tail = (p.word_pad - p.words) * p.line
        words_ref[:, p.words * p.line :, :] = jnp.zeros((p.stack, tail, LANES), single)


def analyse(p, tokens, table, scale, turn_ref, h):
    spectrum = mul(table, tokens) * scale
    for c in range(p.tiles):
        for ri in range(2):
            turn_ref[c, pl.ds(ri * p.rows + h, MW, stride=2 * p.rows), :] = spectrum[
                ri * MW : (ri + 1) * MW, c * LANES : (c + 1) * LANES
            ]


def send_turn(p, turn_ref, out_ref, outer, inner):
    count = outer * inner
    for d in range(p.space):
        for c in range(p.tiles):
            part = turn_ref[c, d * count : (d + 1) * count, :].reshape(outer, inner, LANES)
            out_ref[d, 0, :, :, c * LANES : (c + 1) * LANES] = part.astype(half)


def split_three(value):
    high = value.astype(half).astype(single)
    rest = value - high
    middle = rest.astype(half).astype(single)
    return high, middle, rest - middle


def expand(parts, spread_table):
    stacked = jnp.concatenate(split_three(parts), axis=0).astype(half)
    return mul(stacked, spread_table, TN)


def summed(table, value):
    high = value.astype(half)
    low = (value - high.astype(single)).astype(half)
    return mul(table, high, NT) + mul(table, low, NT)


def cotangent_kernel(p, stored_ref, table_ref, scale_ref, out_ref, words_ref, turn_ref, tokens_ref):
    clear_tail(p, words_ref)
    spread(p, stored_ref, words_ref)

    def row(h, carry):
        def put(r, c, value):
            tokens_ref[r * p.turn_pad : (r + 1) * p.turn_pad, c * LANES : (c + 1) * LANES] = (
                value.astype(half)
            )

        gather_row(p, words_ref, h, put)
        analyse(p, tokens_ref[...], table_ref[...], scale_ref[...], turn_ref, h)
        return carry

    lax.fori_loop(0, p.rows, row, 0)
    send_turn(p, turn_ref, out_ref, p.modes, 2 * p.rows)


def stats_kernel(p, stored_ref, sum_ref, tokens_ref, stat_ref, words_ref, rows_ref):
    clear_tail(p, words_ref)
    spread(p, stored_ref, words_ref)
    count = 2 * p.stack

    def row(h, carry):
        def put(r, c, value):
            tokens_ref[
                0, h, r * p.turn_pad : (r + 1) * p.turn_pad, c * LANES : (c + 1) * LANES
            ] = value.astype(half)

        gather_row(p, words_ref, h, put)
        tokens = tokens_ref[0, h]
        wide = tokens.astype(single)
        plain = mul(sum_ref[0], tokens, NT)
        rows_ref[h] = plain + summed(sum_ref[1], wide * wide)
        return carry

    lax.fori_loop(0, p.rows, row, 0)
    for h in range(p.rows):
        stat_ref[0, h * count : (h + 1) * count, :] = rows_ref[h, :count, :]


def moments(p, stat_refs, rows_ref):
    count = 2 * p.stack
    total = stat_refs[0][0]
    for ref in stat_refs[1:]:
        total = total + ref[0]
    for h in range(p.rows):
        part = total[h * count : (h + 1) * count] * (1.0 / p.channels)
        mean, square = part[: p.stack], part[p.stack :]
        inverse = lax.rsqrt(square - mean * mean + norm_epsilon)
        rows_ref[h, : p.stack, :] = mean
        rows_ref[h, p.stack : count, :] = inverse
        if count < 8:
            rows_ref[h, count:, :] = jnp.zeros((8 - count, p.turn_pad * PACK), single)


def normalise_kernel(p, *refs):
    stat_refs = refs[: p.chan]
    tokens_ref, gain_ref, shift_ref, table_ref, scale_ref, wide_ref = refs[p.chan : p.chan + 6]
    out_ref, rows_ref, turn_ref = refs[p.chan + 6 :]
    moments(p, stat_refs, rows_ref)

    def row(h, carry):
        each = expand(rows_ref[h], wide_ref[...])
        wide = tokens_ref[0, h].astype(single)
        centred = (wide - each[:, : p.lanes]) * each[:, p.lanes :]
        normed = (centred * gain_ref[...] + shift_ref[...]).astype(half)
        analyse(p, normed, table_ref[...], scale_ref[...], turn_ref, h)
        return carry

    lax.fori_loop(0, p.rows, row, 0)
    send_turn(p, turn_ref, out_ref, p.modes, 2 * p.rows)


def gelu_both(values):
    inner = jnp.tanh(gelu_scale * (values + gelu_cubic * values * values * values))
    hidden = 0.5 * values * (1.0 + inner)
    slope = 0.5 * (1.0 + inner) + 0.5 * values * (1.0 - inner * inner) * gelu_scale * (
        1.0 + 3.0 * gelu_cubic * values * values
    )
    return hidden, slope


BAND = 16


def spectral_kernel(
    p,
    step_modes,
    x_ref,
    g_ref,
    there_ref,
    back_ref,
    w1_ref,
    w2_ref,
    bias_ref,
    y_ref,
    dx_ref,
    gw_ref,
    gb_ref,
    lat_ref,
    hid_ref,
    gpost_ref,
    gpre_ref,
    wide_ref,
    slope_ref,
    gsh_ref,
    shr_ref,
    turn_y_ref,
    turn_x_ref,
    acc1_ref,
    acc2_ref,
):
    pack, group = pl.program_id(0), pl.program_id(1)
    count = step_modes * p.lat
    factor = 1.0 / math.sqrt(p.lat)
    base = pl.multiple_of(group * count, count)

    @pl.when((pack == 0) & (group == 0))
    def _():
        gb_ref[...] = jnp.zeros_like(gb_ref)
        acc1_ref[...] = jnp.zeros_like(acc1_ref)
        acc2_ref[...] = jnp.zeros_like(acc2_ref)

    def there(ref, into, offset):
        for m in range(step_modes):
            block = ref[:, 0, m].reshape(2 * p.lat, p.lanes)
            out = (mul(there_ref[...], block) * factor).astype(half)
            at = pl.ds(offset + m * p.lat, p.lat)
            into[at, : p.lanes] = out[: p.lat]
            into[at, p.lanes :] = out[p.lat :]

    def back(value_of, turn_ref):
        for m in range(step_modes):
            rows = slice(m * p.lat, (m + 1) * p.lat)
            both = jnp.concatenate([value_of(rows, 0), value_of(rows, 1)], axis=0)
            out = mul(back_ref[...], both) * factor
            mode = group * step_modes + m
            for ri in range(2):
                for c in range(p.tiles):
                    turn_ref[c, pl.ds(ri * p.modes + mode, p.lat, stride=2 * p.modes), :] = out[
                        ri * p.lat : (ri + 1) * p.lat, c * LANES : (c + 1) * LANES
                    ]

    there(x_ref, lat_ref, base)
    there(g_ref, gsh_ref, 0)
    wide_ref[...] = mul(lat_ref[pl.ds(base, count), :], w1_ref[...])

    def first(i, carry):
        at = pl.ds(pl.multiple_of(i * BAND, BAND), BAND)
        hidden, slope = gelu_both(wide_ref[at, :] + bias_ref[0:1, :])
        hid_ref[pl.ds(pl.multiple_of(base + i * BAND, BAND), BAND), :] = hidden.astype(half)
        slope_ref[at, :] = slope
        return carry

    lax.fori_loop(0, count // BAND, first, 0)
    wide_ref[...] = mul(hid_ref[pl.ds(base, count), :], w2_ref[...])

    def second(i, carry):
        at = pl.ds(pl.multiple_of(i * BAND, BAND), BAND)
        post = wide_ref[at, :] + bias_ref[1:2, :]
        inner = jnp.tanh(post * (1.0 / shrink_level))
        shr_ref[at, :] = (post - shrink_level * inner).astype(half)
        gpost = (gsh_ref[at, :].astype(single) * (inner * inner)).astype(half)
        gpost_ref[pl.ds(pl.multiple_of(base + i * BAND, BAND), BAND), :] = gpost
        gb_ref[8:16, :] += gpost.astype(single).reshape(BAND // 8, 8, 2 * p.lanes).sum(0)
        return carry

    lax.fori_loop(0, count // BAND, second, 0)
    back(lambda rows, ri: shr_ref[rows, ri * p.lanes : (ri + 1) * p.lanes], turn_y_ref)
    wide_ref[...] = mul(gpost_ref[pl.ds(base, count), :], w2_ref[...], NT)

    def third(i, carry):
        at = pl.ds(pl.multiple_of(i * BAND, BAND), BAND)
        gpre = (wide_ref[at, :] * slope_ref[at, :]).astype(half)
        gpre_ref[pl.ds(pl.multiple_of(base + i * BAND, BAND), BAND), :] = gpre
        gb_ref[0:8, :] += gpre.astype(single).reshape(BAND // 8, 8, 2 * p.lanes).sum(0)
        return carry

    lax.fori_loop(0, count // BAND, third, 0)
    shr_ref[...] = mul(gpre_ref[pl.ds(base, count), :], w1_ref[...], NT).astype(half)
    back(lambda rows, ri: shr_ref[rows, ri * p.lanes : (ri + 1) * p.lanes], turn_x_ref)

    @pl.when(group == pl.num_programs(1) - 1)
    def _():
        send_turn(p, turn_y_ref, y_ref, p.rows, 2 * p.modes)
        send_turn(p, turn_x_ref, dx_ref, p.rows, 2 * p.modes)
        acc1_ref[...] += mul(lat_ref[...], gpre_ref[...], TN)
        acc2_ref[...] += mul(hid_ref[...], gpost_ref[...], TN)

    @pl.when((group == pl.num_programs(1) - 1) & (pack == pl.num_programs(0) - 1))
    def _():
        for which, acc in enumerate((acc1_ref, acc2_ref)):
            for n in range(p.groups):
                for part in range(2):
                    total = jnp.zeros((p.width, LANES), single)
                    for s in range(p.stack):
                        q = s * p.groups + n
                        for row_ri, col_ri, sign in (((0, 0, 1), (1, 1, 1)), ((0, 1, 1), (1, 0, -1)))[part]:
                            top = row_ri * p.lanes + q * p.width
                            left = col_ri * p.lanes + q * p.width
                            tile = left // LANES
                            value = rolled(
                                acc[top : top + p.width, tile * LANES : (tile + 1) * LANES],
                                -left % LANES,
                            )
                            if left % LANES + p.width > LANES:
                                nxt = acc[
                                    top : top + p.width, (tile + 1) * LANES : (tile + 2) * LANES
                                ]
                                lane = lax.broadcasted_iota(jnp.int32, (p.width, LANES), 1)
                                value = jnp.where(
                                    lane < LANES - left % LANES, value, rolled(nxt, -left % LANES)
                                )
                            total = total + sign * value
                    gw_ref[which, part, n] = total


def mixed_kernel(p, rows_ref, table_ref, out_ref, words_ref):
    factor = 1.0 / math.sqrt(p.lon)

    def row(h, carry):
        block = rows_ref[:, 0, h].reshape(2 * MW, p.lanes)
        tokens = mul(table_ref[...], block) * factor
        scatter_row(p, tokens, words_ref, h)
        return carry

    lax.fori_loop(0, p.rows, row, 0)
    store_words(p, words_ref, out_ref)


def slope_sums_kernel(p, *refs):
    stat_refs = refs[: p.chan]
    rows_in_ref, tokens_ref, gain_ref, table_ref, wide_ref, sum_ref = refs[p.chan : p.chan + 6]
    sums_ref, param_ref, rows_ref, part_ref = refs[p.chan + 6 :]
    factor = 1.0 / math.sqrt(p.lon)
    count = 2 * p.stack
    moments(p, stat_refs, rows_ref)

    @pl.when(pl.program_id(0) == 0)
    def _():
        param_ref[...] = jnp.zeros_like(param_ref)

    def row(h, carry):
        block = rows_in_ref[:, 0, h].reshape(2 * MW, p.lanes)
        normed_grad = mul(table_ref[...], block) * factor
        each = expand(rows_ref[h], wide_ref[...])
        wide = tokens_ref[0, h].astype(single)
        centred = (wide - each[:, : p.lanes]) * each[:, p.lanes :]
        product = normed_grad * centred
        folds = (PACK * p.turn_pad // 8, 8, p.lanes)
        param_ref[0:8, :] += product.reshape(folds).sum(0)
        param_ref[8:16, :] += normed_grad.reshape(folds).sum(0)
        gain = gain_ref[...]
        part_ref[h] = summed(sum_ref[0], normed_grad * gain) + summed(sum_ref[1], product * gain)
        return carry

    lax.fori_loop(0, p.rows, row, 0)
    for h in range(p.rows):
        sums_ref[0, h * count : (h + 1) * count, :] = part_ref[h, :count, :]


def input_grad_kernel(p, *refs):
    stat_refs, part_refs = refs[: p.chan], refs[p.chan : 2 * p.chan]
    rows_in_ref, tokens_ref, gain_ref, table_ref, wide_ref = refs[2 * p.chan : 2 * p.chan + 5]
    out_ref, rows_ref, part_ref, words_ref = refs[2 * p.chan + 5 :]
    factor = 1.0 / math.sqrt(p.lon)
    count = 2 * p.stack
    moments(p, stat_refs, rows_ref)
    total = part_refs[0][0].astype(single)
    for ref in part_refs[1:]:
        total = total + ref[0].astype(single)
    for h in range(p.rows):
        part_ref[h, :count, :] = total[h * count : (h + 1) * count] * (1.0 / p.channels)
        if count < 8:
            part_ref[h, count:, :] = jnp.zeros((8 - count, p.turn_pad * PACK), single)

    def row(h, carry):
        block = rows_in_ref[:, 0, h].reshape(2 * MW, p.lanes)
        normed_grad = mul(table_ref[...], block) * factor
        each = expand(rows_ref[h], wide_ref[...])
        means = expand(part_ref[h], wide_ref[...])
        inverse = each[:, p.lanes :]
        centred = (tokens_ref[0, h].astype(single) - each[:, : p.lanes]) * inverse
        grad = inverse * (
            normed_grad * gain_ref[...] - means[:, : p.lanes] - centred * means[:, p.lanes :]
        )
        scatter_row(p, grad, words_ref, h)
        return carry

    lax.fori_loop(0, p.rows, row, 0)
    store_words(p, words_ref, out_ref)


def whole_spec(value):
    dims = value.shape
    return pl.BlockSpec(dims, lambda *_: (0,) * len(dims))


def pack_spec(value, offset=0):
    dims = (1,) + value.shape[1:]
    return pl.BlockSpec(dims, lambda b, *_: (b + offset,) + (0,) * (len(dims) - 1))


def peer_spec(value):
    dims = (value.shape[0], 1) + value.shape[2:]
    return pl.BlockSpec(dims, lambda b, *_: (0, b) + (0,) * (len(dims) - 2))


def stored_spec(p, offset):
    return pl.BlockSpec(
        (p.stack, p.rows, p.groups, p.long), lambda b, *_: (b + offset, 0, 0, 0)
    )


def call(body, grid, ins, in_specs, outs, out_specs, scratch, flops, aliases=None):
    moved = sum(v.size * v.dtype.itemsize for v in ins) + sum(
        math.prod(o.shape) * o.dtype.itemsize for o in outs
    )
    return _call(body, grid, ins, in_specs, outs, out_specs, scratch, flops, moved, aliases)


def _call(body, grid, ins, in_specs, outs, out_specs, scratch, flops, moved, aliases):
    return pl.pallas_call(
        body,
        grid=grid,
        in_specs=in_specs,
        out_specs=out_specs,
        out_shape=outs,
        scratch_shapes=scratch,
        input_output_aliases=aliases or {},
        compiler_params=pltpu.CompilerParams(vmem_limit_bytes=VMEM_LIMIT),
        cost_estimate=pl.CostEstimate(flops=flops, bytes_accessed=moved, transcendentals=0),
    )(*ins)


def lon_tables(p):
    cos_lon, sin_lon = trig(p.lon, MW)
    wave = np.concatenate([cos_lon, -sin_lon], axis=1)
    turned = np.zeros((PACK, p.turn_pad, 2 * MW), np.float32)
    turned[:, : p.turn] = wave.reshape(p.turn, PACK, 2 * MW).transpose(1, 0, 2)
    turned = turned.reshape(PACK * p.turn_pad, 2 * MW)
    doubling = np.where(np.arange(MW) == 0, 1.0, 2.0).astype(np.float32)
    factor = np.float32(1.0 / math.sqrt(p.lon))
    plain_scale = np.full((2 * MW, 1), factor, np.float32)
    double_scale = (factor * np.tile(doubling, 2))[:, None].astype(np.float32)
    owner = turned.reshape(-1, 2, p.space, p.modes).transpose(0, 2, 1, 3).reshape(-1, 2 * MW)
    twice = np.tile(doubling.reshape(p.space, 1, p.modes), (1, 2, 1)).reshape(1, 2 * MW)
    to_half = lambda value: jnp.asarray(value, half)
    return (
        to_half(turned.T),
        jnp.asarray(plain_scale),
        jnp.asarray(double_scale),
        to_half(owner * twice),
        to_half(owner),
    )


def lat_tables(p):
    cos_lat, sin_lat = trig(p.lat, p.lat)
    there = np.block([[cos_lat, sin_lat], [-sin_lat, cos_lat]])
    there = there.reshape(2 * p.lat, 2, p.space, p.rows).transpose(0, 2, 1, 3)
    back = np.block([[cos_lat.T, -sin_lat.T], [sin_lat.T, cos_lat.T]])
    return jnp.asarray(there.reshape(2 * p.lat, 2 * p.lat), half), jnp.asarray(back, half)


def sum_tables(p):
    owner = np.arange(PACK) // p.groups
    lane_owner = np.repeat(owner, p.width)
    sums = np.zeros((2, 8, p.lanes), np.float32)
    wide = np.zeros((3, 8, 2, p.lanes), np.float32)
    for s in range(p.stack):
        sums[0, s] = lane_owner == s
        sums[1, p.stack + s] = lane_owner == s
        wide[:, s, 0] = lane_owner == s
        wide[:, p.stack + s, 1] = lane_owner == s
    return jnp.asarray(sums, half), jnp.asarray(wide.reshape(24, 2 * p.lanes), half)


def block_weights(p, weights):
    each = jnp.tile(weights, (1, p.stack, 1, 1))
    eye = jnp.eye(PACK, dtype=weights.dtype)
    wide = (each[:, :, :, None, :] * eye[None, :, None, :, None]).reshape(2, p.lanes, p.lanes)
    top = jnp.concatenate([wide[0], wide[1]], axis=1)
    bottom = jnp.concatenate([-wide[1], wide[0]], axis=1)
    return jnp.concatenate([top, bottom], axis=0)


def lane_vector(p, vector):
    return jnp.tile(vector, p.stack)[None, :]


def exchange(value):
    return lax.all_to_all(value, "space", 0, 0, tiled=True)


def around(value, axis, size):
    gathered = [value]
    for step in range(1, size):
        gathered.append(
            lax.ppermute(value, axis, [(i, (i + step) % size) for i in range(size)])
        )
    return gathered


def reduced(p, value, kind):
    step = 1
    while step < p.space:
        own = value.astype(kind)
        other = lax.ppermute(own, "space", [(i, i ^ step) for i in range(p.space)])
        value = own.astype(single) + other.astype(single)
        step *= 2
    return value


def on_device(space, chan, members, gain, shift, w_first, b_first, w_second, b_second, cotangent):
    p = Plan(members, w_first.shape[-1], space, chan)
    chunks = CHUNKS if p.packs % CHUNKS == 0 else 1
    size = p.packs // chunks
    grid = (size,)
    table, plain_scale, double_scale, mixed_table, slope_table = lon_tables(p)
    there_table, back_table = lat_tables(p)
    sum_table, wide_table = sum_tables(p)
    gain_lanes, shift_lanes = lane_vector(p, gain), lane_vector(p, shift)
    w1, w2 = block_weights(p, w_first), block_weights(p, w_second)
    bias = jnp.stack(
        [jnp.tile(b.reshape(2, -1), (1, p.stack)).reshape(-1) for b in (b_first, b_second)]
    )
    tokens_rows = PACK * p.turn_pad
    dft_flops = 2 * size * p.rows * tokens_rows * 2 * MW * p.lanes
    words = pltpu.VMEM((p.stack, p.word_pad * p.line, LANES), single)
    turn_in = pltpu.VMEM((p.tiles, MW * 2 * p.rows, LANES), single)
    rows_scratch = pltpu.VMEM((p.rows, 8, tokens_rows), single)
    sent = jax.ShapeDtypeStruct((space, size, p.modes, 2 * p.rows, p.lanes), half)
    returned = jax.ShapeDtypeStruct((space, size, p.rows, 2 * p.modes, p.lanes), half)
    count = 2 * p.stack * p.rows
    stored = jax.ShapeDtypeStruct(members.shape, half)

    def cotangent_chunk(c):
        ins = (cotangent, table, double_scale)
        return call(
            functools.partial(cotangent_kernel, p), grid, ins,
            [stored_spec(p, c * size), whole_spec(table), whole_spec(double_scale)],
            [sent], [peer_spec(sent)],
            [words, turn_in, pltpu.VMEM((tokens_rows, p.lanes), half)], dft_flops,
        )[0]

    def stats_chunk(c):
        ins = (members, sum_table)
        outs = [
            jax.ShapeDtypeStruct((size, p.rows, tokens_rows, p.lanes), half),
            jax.ShapeDtypeStruct((size, count, tokens_rows), single),
        ]
        return call(
            functools.partial(stats_kernel, p), grid, ins,
            [stored_spec(p, c * size), whole_spec(sum_table)],
            outs, [pack_spec(o) for o in outs], [words, rows_scratch], dft_flops // 4,
        )

    def normalise_chunk(stats, tokens):
        tail = (gain_lanes, shift_lanes, table, plain_scale, wide_table)
        return call(
            functools.partial(normalise_kernel, p), grid, (*stats, tokens, *tail),
            [pack_spec(s) for s in stats] + [pack_spec(tokens)] + [whole_spec(v) for v in tail],
            [sent], [peer_spec(sent)], [rows_scratch, turn_in], dft_flops,
        )[0]

    step_modes = 2 if p.modes % 2 == 0 else 1
    wide_lanes = 2 * p.lanes

    def spectral_chunk(x_in, g_in):
        tail = (there_table, back_table, w1, w2, bias)
        mode_spec = pl.BlockSpec(
            (space, 1, step_modes, 2 * p.rows, p.lanes), lambda b, m: (0, b, m, 0, 0)
        )
        grads = jax.ShapeDtypeStruct((2, 2, p.groups, p.width, LANES), single)
        bias_grads = jax.ShapeDtypeStruct((16, wide_lanes), single)
        kept = pltpu.VMEM((p.modes * p.lat, wide_lanes), half)
        held = pltpu.VMEM((step_modes * p.lat, wide_lanes), single)
        brief = pltpu.VMEM((step_modes * p.lat, wide_lanes), half)
        turn_out = pltpu.VMEM((p.tiles, p.lat * 2 * p.modes, LANES), single)
        return call(
            functools.partial(spectral_kernel, p, step_modes),
            (size, p.modes // step_modes), (x_in, g_in, *tail),
            [mode_spec, mode_spec] + [whole_spec(v) for v in tail],
            [returned, returned, grads, bias_grads],
            [peer_spec(returned), peer_spec(returned), whole_spec(grads), whole_spec(bias_grads)],
            [kept] * 4 + [held] * 2 + [brief] * 2 + [turn_out] * 2
            + [pltpu.VMEM((wide_lanes, wide_lanes), single)] * 2,
            12 * size * p.modes * p.lat * wide_lanes * wide_lanes,
        )

    def out_call(body, c, ins, specs, scratch, before, flops):
        ins, specs = list(ins), list(specs)
        aliases = {}
        inner = body
        if before is not None:
            place = len(ins)
            inner = lambda *refs: body(*refs[:place], *refs[place + 1 :])
            ins.append(before)
            specs.append(pl.BlockSpec(memory_space=pl.ANY))
            aliases = {place: 0}
        return call(
            inner, grid, tuple(ins), specs, [stored], [stored_spec(p, c * size)],
            scratch, flops, aliases,
        )[0]

    def mixed_chunk(c, rows_in, before):
        return out_call(
            functools.partial(mixed_kernel, p), c, (rows_in, mixed_table),
            [peer_spec(rows_in), whole_spec(mixed_table)], [words], before, dft_flops,
        )

    def slope_sums_chunk(stats, rows_in, tokens):
        tail = (gain_lanes, slope_table, wide_table, sum_table)
        outs = [
            jax.ShapeDtypeStruct((size, count, tokens_rows), single),
            jax.ShapeDtypeStruct((16, p.lanes), single),
        ]
        return call(
            functools.partial(slope_sums_kernel, p), grid,
            (*stats, rows_in, tokens, *tail),
            [pack_spec(s) for s in stats] + [peer_spec(rows_in), pack_spec(tokens)]
            + [whole_spec(v) for v in tail],
            outs, [pack_spec(outs[0]), whole_spec(outs[1])], [rows_scratch, rows_scratch],
            dft_flops,
        )

    def input_grad_chunk(c, stats, parts, rows_in, tokens, before):
        tail = (gain_lanes, slope_table, wide_table)
        return out_call(
            functools.partial(input_grad_kernel, p), c,
            (*stats, *parts, rows_in, tokens, *tail),
            [pack_spec(s) for s in (*stats, *parts)] + [peer_spec(rows_in), pack_spec(tokens)]
            + [whole_spec(v) for v in tail],
            [rows_scratch, rows_scratch, words], before, dft_flops,
        )

    everyone = range(chunks)
    g_in = [exchange(cotangent_chunk(c)) for c in everyone]
    first = [stats_chunk(c) for c in everyone]
    stats = [around(s, "chan", chan) for _, s in first]
    x_in = [exchange(normalise_chunk(stats[c], first[c][0])) for c in everyone]
    mixed = grad_input = None
    weight_grads = bias_grads = param_grads = 0.0
    spectra = [spectral_chunk(x_in[c], g_in[c]) for c in everyone]
    for c in everyone:
        y_out, dx_out, gw, gb = spectra[c]
        weight_grads, bias_grads = weight_grads + gw, bias_grads + gb
        dx_rows = exchange(dx_out)
        y_rows = exchange(y_out)
        sums, params = slope_sums_chunk(stats[c], dx_rows, first[c][0])
        param_grads = param_grads + params
        parts = around(sums.astype(half), "chan", chan)
        grad_input = input_grad_chunk(c, stats[c], parts, dx_rows, first[c][0], grad_input)
        mixed = mixed_chunk(c, y_rows, mixed)

    def by_channel(rows):
        return rows.reshape(-1, p.stack, p.groups * p.width).sum(1)

    weights = weight_grads.reshape(-1, LANES)
    flat_bias = bias_grads.reshape(2, 8, 2, p.stack, p.groups * p.width).sum((1, 3))
    flat_params = by_channel(param_grads.reshape(2, 8, p.lanes).sum(1))
    grads = reduced(p, weights, half).reshape(weight_grads.shape)[..., : p.width]
    flat_bias = reduced(p, flat_bias, single).reshape((2,) + b_first.shape)
    both = reduced(p, flat_params, single)
    return (mixed, grad_input, grads[0], flat_bias[0], grads[1], flat_bias[1], both[0], both[1])


def solution(mesh):
    tokens = P(None, "space", "chan", None)
    weights = P(None, "chan", None, None)
    biases = P(None, "chan", None)
    placed = (tokens, P("chan"), P("chan"), weights, biases, weights, biases, tokens)
    return jax.shard_map(
        functools.partial(on_device, mesh.shape["space"], mesh.shape["chan"]),
        mesh=mesh,
        in_specs=placed,
        out_specs=(tokens, tokens, weights, biases, weights, biases, P("chan"), P("chan")),
        check_vma=False,
    )
```

```python
import functools
import math

import jax
import jax.numpy as jnp
import numpy as np
from jax import lax
from jax.experimental import pallas as pl
from jax.experimental.pallas import tpu as pltpu
from jax.sharding import PartitionSpec as P


MW = 64
LANES = 128
PACK = 4

shrink_level = 0.05
norm_epsilon = 1e-05
gelu_scale = 0.7978845608
gelu_cubic = 0.044715

half = jnp.bfloat16
single = jnp.float32
VMEM_LIMIT = 36 * 1024 * 1024
SLOTS = 2

TN = (((0,), (0,)), ((), ()))
NT = (((1,), (1,)), ((), ()))


def mul(first_op, second_op, dims=(((1,), (0,)), ((), ()))):
    return lax.dot_general(first_op, second_op, dims, preferred_element_type=single)


def trig(length, columns):
    angles = (np.arange(length)[:, None] * np.arange(columns)[None, :] % length).astype(np.float32)
    angles = (angles * np.float32(2.0 * math.pi / length)).astype(np.float64)
    cast = lambda table: table.astype(np.float32).astype(half).astype(np.float32)
    return cast(np.cos(angles)), cast(np.sin(angles))


class Plan:
    def __init__(self, members, width, space, chan):
        self.batch, self.rows, self.groups, self.long = members.shape
        self.width, self.space, self.chan = width, space, chan
        self.lon = self.long // width
        self.lat = self.rows * space
        self.modes = MW // space
        self.stack = PACK // self.groups
        self.packs = self.batch // self.stack
        self.lanes = PACK * width
        self.tiles = self.lanes // LANES
        self.turn = self.lon // PACK
        self.turn_pad = -(-self.turn // 16) * 16
        self.words = self.long // LANES
        self.word_pad = self.tiles * self.turn_pad
        self.channels = self.groups * width * chan


def moved_lanes(p, fetch, from_start, to_start, tile):
    pieces = []
    for slot in range(PACK):
        low = max(to_start(slot), tile * LANES)
        high = min(to_start(slot) + p.width, (tile + 1) * LANES)
        at = low
        while at < high:
            source = at - to_start(slot) + from_start(slot)
            stop = min(high, at + LANES - source % LANES)
            shift = (at - source) % LANES
            pieces.append((stop - tile * LANES, fetch(slot, source // LANES, shift)))
            at = stop
    return pieces


def merged(pieces, lane):
    value = pieces[-1][1]
    for stop, piece in reversed(pieces[:-1]):
        value = jnp.where(lane < stop, piece, value)
    return value


def rolled(value, shift):
    return value if shift == 0 else pltpu.roll(value, shift, 1)


def spread(p, stored_ref, words_ref, h):
    for q in range(PACK):
        line = stored_ref[q // p.groups, h, q % p.groups, :]
        words_ref[q, : p.words, :] = line.reshape(p.words, LANES).astype(single)


def gather_row(p, words_ref):
    lane = lax.broadcasted_iota(jnp.int32, (p.turn_pad, LANES), 1)
    source = {}
    for q in range(PACK):
        for i in range(p.tiles):
            source[q, i] = words_ref[q, pl.ds(i, p.turn_pad, stride=p.tiles), :]
    rows = []
    for r in range(PACK):
        cache = {}

        def fetch(q, i, shift):
            key = (q, i, shift)
            if key not in cache:
                cache[key] = rolled(source[q, i], shift)
            return cache[key]

        tiles = []
        for c in range(p.tiles):
            pieces = moved_lanes(p, fetch, lambda q: r * p.width, lambda q: q * p.width, c)
            tiles.append(merged(pieces, lane).astype(half))
        rows.append(jnp.concatenate(tiles, axis=1))
    return jnp.concatenate(rows, axis=0)


def scatter_row(p, tokens, words_ref, stored_ref, h):
    lane = lax.broadcasted_iota(jnp.int32, (p.turn_pad, LANES), 1)
    for q in range(PACK):
        s, n = divmod(q, p.groups)

        def fetch(r, c, shift):
            part = tokens[r * p.turn_pad : (r + 1) * p.turn_pad, c * LANES : (c + 1) * LANES]
            return rolled(part, shift)

        for i in range(p.tiles):
            pieces = moved_lanes(p, fetch, lambda r: q * p.width, lambda r: r * p.width, i)
            at = pl.ds(i * p.groups + n, p.turn_pad, stride=p.tiles * p.groups)
            words_ref[s, at, :] = merged(pieces, lane)
    for s in range(p.stack):
        lines = words_ref[s, : p.words * p.groups, :].astype(half)
        for t in range(p.words):
            stored_ref[s, h, :, t * LANES : (t + 1) * LANES] = lines[
                t * p.groups : (t + 1) * p.groups, :
            ]


def clear_tail(p, words_ref):
    @pl.when(pl.program_id(0) == 0)
    def _():
        tail = p.word_pad - p.words
        words_ref[:, :, p.words :, :] = jnp.zeros(words_ref.shape[:2] + (tail, LANES), single)


def each_row(p, body):
    side = SLOTS if p.rows % SLOTS == 0 else 1

    def step(i, carry):
        for slot in range(side):
            body(i * side + slot, slot)
        return carry

    lax.fori_loop(0, p.rows // side, step, 0)


def analyse(p, tokens, table, scale, turn_ref, h):
    spectrum = mul(table, tokens) * scale
    for c in range(p.tiles):
        for ri in range(2):
            turn_ref[c, pl.ds(ri * p.rows + h, MW, stride=2 * p.rows), :] = spectrum[
                ri * MW : (ri + 1) * MW, c * LANES : (c + 1) * LANES
            ]


def send_turn(p, turn_ref, out_ref, outer, inner, which=0):
    count = outer * inner
    for d in range(p.space):
        for c in range(p.tiles):
            part = turn_ref[c, d * count : (d + 1) * count, :].reshape(outer, inner, LANES)
            out_ref[d, which, 0, :, :, c * LANES : (c + 1) * LANES] = part.astype(half)


def split_three(value):
    high = value.astype(half).astype(single)
    rest = value - high
    middle = rest.astype(half).astype(single)
    return high, middle, rest - middle


def expand(parts, spread_table):
    stacked = jnp.concatenate(split_three(parts), axis=0).astype(half)
    return mul(stacked, spread_table, TN)


def summed(table, value):
    high = value.astype(half)
    low = (value - high.astype(single)).astype(half)
    return mul(table, high, NT) + mul(table, low, NT)


def cotangent_kernel(p, stored_ref, table_ref, scale_ref, out_ref, words_ref, turn_ref):
    clear_tail(p, words_ref)

    def row(h, slot):
        spread(p, stored_ref, words_ref.at[slot], h)
        tokens = gather_row(p, words_ref.at[slot])
        analyse(p, tokens, table_ref[...], scale_ref[...], turn_ref, h)

    each_row(p, row)
    send_turn(p, turn_ref, out_ref, p.modes, 2 * p.rows)


def stats_kernel(p, stored_ref, sum_ref, tokens_ref, stat_ref, words_ref, rows_ref):
    clear_tail(p, words_ref)
    count = 2 * p.stack

    def row(h, slot):
        spread(p, stored_ref, words_ref.at[slot], h)
        tokens = gather_row(p, words_ref.at[slot])
        tokens_ref[0, h] = tokens
        wide = tokens.astype(single)
        rows_ref[h] = mul(sum_ref[0], tokens, NT) + summed(sum_ref[1], wide * wide)

    each_row(p, row)
    for h in range(p.rows):
        stat_ref[0, h * count : (h + 1) * count, :] = rows_ref[h, :count, :]


def moments(p, stat_refs, rows_ref):
    count = 2 * p.stack
    total = stat_refs[0][0]
    for ref in stat_refs[1:]:
        total = total + ref[0]
    for h in range(p.rows):
        part = total[h * count : (h + 1) * count] * (1.0 / p.channels)
        mean, square = part[: p.stack], part[p.stack :]
        inverse = lax.rsqrt(square - mean * mean + norm_epsilon)
        rows_ref[h, : p.stack, :] = mean
        rows_ref[h, p.stack : count, :] = inverse
        if count < 8:
            rows_ref[h, count:, :] = jnp.zeros((8 - count, p.turn_pad * PACK), single)


def normalise_kernel(p, *refs):
    stat_refs = refs[: p.chan]
    tokens_ref, gain_ref, shift_ref, table_ref, scale_ref, wide_ref = refs[p.chan : p.chan + 6]
    out_ref, rows_ref, turn_ref = refs[p.chan + 6 :]
    moments(p, stat_refs, rows_ref)

    def row(h, slot):
        each = expand(rows_ref[h], wide_ref[...])
        wide = tokens_ref[0, h].astype(single)
        centred = (wide - each[:, : p.lanes]) * each[:, p.lanes :]
        normed = (centred * gain_ref[...] + shift_ref[...]).astype(half)
        analyse(p, normed, table_ref[...], scale_ref[...], turn_ref, h)

    each_row(p, row)
    send_turn(p, turn_ref, out_ref, p.modes, 2 * p.rows)


def gelu_both(values):
    square = values * values
    inner = jnp.tanh(values * (gelu_scale + gelu_scale * gelu_cubic * square))
    upper = 0.5 + 0.5 * inner
    hidden = values * upper
    slope = upper + hidden * (1.0 - upper) * (
        2.0 * gelu_scale + 6.0 * gelu_scale * gelu_cubic * square
    )
    return hidden, slope


BAND = 16


def place_weights(p, w_ref, out_refs):
    lane = lax.broadcasted_iota(jnp.int32, (p.width, LANES), 1)
    for which, out_ref in enumerate(out_refs):
        for q in range(PACK):
            at, shift = divmod(q * p.width, LANES)
            for part in range(2):
                value = w_ref[which, part, q % p.groups].astype(single)
                turned = rolled(value, shift)
                tiles = [jnp.zeros_like(value) for _ in range(p.tiles)]
                tiles[at] = jnp.where(lane >= shift, turned, 0.0)
                if shift + p.width > LANES:
                    tiles[at + 1] = jnp.where(lane < shift + p.width - LANES, turned, 0.0)
                wide = jnp.concatenate(tiles, axis=1)
                for row_ri, col_ri, sign in (((0, 0, 1), (1, 1, 1)), ((0, 1, 1), (1, 0, -1)))[part]:
                    top = row_ri * p.lanes + q * p.width
                    out_ref[top : top + p.width, col_ri * p.lanes : (col_ri + 1) * p.lanes] = (
                        sign * wide
                    ).astype(half)


def spectral_kernel(
    p,
    step_modes,
    joined,
    x_ref,
    g_ref,
    there_ref,
    back_ref,
    w_ref,
    bias_ref,
    *refs,
):
    out_refs = refs[: 1 if joined else 2]
    (
    gw_ref,
    gb_ref,
    lat_ref,
    hid_ref,
    gpost_ref,
    gpre_ref,
    wide_ref,
    slope_ref,
    gsh_ref,
    shr_ref,
    turn_y_ref,
    turn_x_ref,
    acc1_ref,
    acc2_ref,
    w1_ref,
    w2_ref,
    ) = refs[len(out_refs) :]
    pack, group = pl.program_id(0), pl.program_id(1)
    count = step_modes * p.lat
    factor = 1.0 / math.sqrt(p.lat)
    base = pl.multiple_of(group * count, count)

    @pl.when((pack == 0) & (group == 0))
    def _():
        place_weights(p, w_ref, (w1_ref, w2_ref))
        gb_ref[...] = jnp.zeros_like(gb_ref)
        acc1_ref[...] = jnp.zeros_like(acc1_ref)
        acc2_ref[...] = jnp.zeros_like(acc2_ref)

    def there(ref, into, offset):
        for m in range(step_modes):
            block = ref[:, 0, 0, m].reshape(2 * p.lat, p.lanes)
            out = (mul(there_ref[...], block) * factor).astype(half)
            at = pl.ds(offset + m * p.lat, p.lat)
            into[at, : p.lanes] = out[: p.lat]
            into[at, p.lanes :] = out[p.lat :]

    def back(value_of, turn_ref):
        for m in range(step_modes):
            rows = slice(m * p.lat, (m + 1) * p.lat)
            both = jnp.concatenate([value_of(rows, 0), value_of(rows, 1)], axis=0)
            out = mul(back_ref[...], both) * factor
            mode = group * step_modes + m
            for ri in range(2):
                for c in range(p.tiles):
                    turn_ref[c, pl.ds(ri * p.modes + mode, p.lat, stride=2 * p.modes), :] = out[
                        ri * p.lat : (ri + 1) * p.lat, c * LANES : (c + 1) * LANES
                    ]

    there(x_ref, lat_ref, base)
    there(g_ref, gsh_ref, 0)
    wide_ref[...] = mul(lat_ref[pl.ds(base, count), :], w1_ref[...])

    def first(i, carry):
        at = pl.ds(pl.multiple_of(i * BAND, BAND), BAND)
        hidden, slope = gelu_both(wide_ref[at, :] + bias_ref[0:1, :])
        hid_ref[pl.ds(pl.multiple_of(base + i * BAND, BAND), BAND), :] = hidden.astype(half)
        slope_ref[at, :] = slope
        return carry

    lax.fori_loop(0, count // BAND, first, 0)
    wide_ref[...] = mul(hid_ref[pl.ds(base, count), :], w2_ref[...])

    def second(i, carry):
        at = pl.ds(pl.multiple_of(i * BAND, BAND), BAND)
        post = wide_ref[at, :] + bias_ref[1:2, :]
        inner = jnp.tanh(post * (1.0 / shrink_level))
        shr_ref[at, :] = (post - shrink_level * inner).astype(half)
        gpost = (gsh_ref[at, :].astype(single) * (inner * inner)).astype(half)
        gpost_ref[pl.ds(pl.multiple_of(base + i * BAND, BAND), BAND), :] = gpost
        gb_ref[8:16, :] += gpost.astype(single).reshape(BAND // 8, 8, 2 * p.lanes).sum(0)
        return carry

    lax.fori_loop(0, count // BAND, second, 0)
    back(lambda rows, ri: shr_ref[rows, ri * p.lanes : (ri + 1) * p.lanes], turn_y_ref)
    wide_ref[...] = mul(gpost_ref[pl.ds(base, count), :], w2_ref[...], NT)

    def third(i, carry):
        at = pl.ds(pl.multiple_of(i * BAND, BAND), BAND)
        gpre = (wide_ref[at, :] * slope_ref[at, :]).astype(half)
        gpre_ref[pl.ds(pl.multiple_of(base + i * BAND, BAND), BAND), :] = gpre
        gb_ref[0:8, :] += gpre.astype(single).reshape(BAND // 8, 8, 2 * p.lanes).sum(0)
        return carry

    lax.fori_loop(0, count // BAND, third, 0)
    shr_ref[...] = mul(gpre_ref[pl.ds(base, count), :], w1_ref[...], NT).astype(half)
    back(lambda rows, ri: shr_ref[rows, ri * p.lanes : (ri + 1) * p.lanes], turn_x_ref)

    @pl.when(group == pl.num_programs(1) - 1)
    def _():
        send_turn(p, turn_y_ref, out_refs[0], p.rows, 2 * p.modes)
        send_turn(p, turn_x_ref, out_refs[-1], p.rows, 2 * p.modes, len(out_refs) % 2)
        acc1_ref[...] += mul(lat_ref[...], gpre_ref[...], TN)
        acc2_ref[...] += mul(hid_ref[...], gpost_ref[...], TN)

    @pl.when((group == pl.num_programs(1) - 1) & (pack == pl.num_programs(0) - 1))
    def _():
        for which, acc in enumerate((acc1_ref, acc2_ref)):
            for n in range(p.groups):
                for part in range(2):
                    total = jnp.zeros((p.width, LANES), single)
                    for s in range(p.stack):
                        q = s * p.groups + n
                        for row_ri, col_ri, sign in (((0, 0, 1), (1, 1, 1)), ((0, 1, 1), (1, 0, -1)))[part]:
                            top = row_ri * p.lanes + q * p.width
                            left = col_ri * p.lanes + q * p.width
                            tile = left // LANES
                            value = rolled(
                                acc[top : top + p.width, tile * LANES : (tile + 1) * LANES],
                                -left % LANES,
                            )
                            if left % LANES + p.width > LANES:
                                nxt = acc[
                                    top : top + p.width, (tile + 1) * LANES : (tile + 2) * LANES
                                ]
                                lane = lax.broadcasted_iota(jnp.int32, (p.width, LANES), 1)
                                value = jnp.where(
                                    lane < LANES - left % LANES, value, rolled(nxt, -left % LANES)
                                )
                            total = total + sign * value
                    gw_ref[which, part, n] = total


def mixed_kernel(p, rows_ref, table_ref, out_ref, words_ref):
    factor = 1.0 / math.sqrt(p.lon)

    def row(h, slot):
        block = rows_ref[:, 0, 0, h].reshape(2 * MW, p.lanes)
        tokens = mul(table_ref[...], block) * factor
        scatter_row(p, tokens, words_ref.at[slot], out_ref, h)

    each_row(p, row)


def slope_sums_kernel(p, *refs):
    stat_refs = refs[: p.chan]
    rows_in_ref, tokens_ref, gain_ref, table_ref, wide_ref, sum_ref = refs[p.chan : p.chan + 6]
    sums_ref, param_ref, rows_ref, part_ref = refs[p.chan + 6 :]
    factor = 1.0 / math.sqrt(p.lon)
    count = 2 * p.stack
    moments(p, stat_refs, rows_ref)

    @pl.when(pl.program_id(0) == 0)
    def _():
        param_ref[...] = jnp.zeros_like(param_ref)

    def row(h, slot):
        block = rows_in_ref[:, 0, 0, h].reshape(2 * MW, p.lanes)
        normed_grad = mul(table_ref[...], block) * factor
        each = expand(rows_ref[h], wide_ref[...])
        wide = tokens_ref[0, h].astype(single)
        centred = (wide - each[:, : p.lanes]) * each[:, p.lanes :]
        product = normed_grad * centred
        folds = (PACK * p.turn_pad // 8, 8, p.lanes)
        param_ref[0:8, :] += product.reshape(folds).sum(0)
        param_ref[8:16, :] += normed_grad.reshape(folds).sum(0)
        gain = gain_ref[...]
        part_ref[h] = summed(sum_ref[0], normed_grad * gain) + summed(sum_ref[1], product * gain)

    each_row(p, row)
    for h in range(p.rows):
        sums_ref[0, h * count : (h + 1) * count, :] = part_ref[h, :count, :]


def input_grad_kernel(p, *refs):
    stat_refs, part_refs = refs[: p.chan], refs[p.chan : 2 * p.chan]
    rows_in_ref, tokens_ref, gain_ref, table_ref, wide_ref = refs[2 * p.chan : 2 * p.chan + 5]
    out_ref, rows_ref, part_ref, words_ref = refs[2 * p.chan + 5 :]
    factor = 1.0 / math.sqrt(p.lon)
    count = 2 * p.stack
    moments(p, stat_refs, rows_ref)
    total = part_refs[0][0].astype(single)
    for ref in part_refs[1:]:
        total = total + ref[0].astype(single)
    for h in range(p.rows):
        part_ref[h, :count, :] = total[h * count : (h + 1) * count] * (1.0 / p.channels)
        if count < 8:
            part_ref[h, count:, :] = jnp.zeros((8 - count, p.turn_pad * PACK), single)

    def row(h, slot):
        block = rows_in_ref[:, 0, 0, h].reshape(2 * MW, p.lanes)
        normed_grad = mul(table_ref[...], block) * factor
        each = expand(rows_ref[h], wide_ref[...])
        means = expand(part_ref[h], wide_ref[...])
        inverse = each[:, p.lanes :]
        centred = (tokens_ref[0, h].astype(single) - each[:, : p.lanes]) * inverse
        grad = inverse * (
            normed_grad * gain_ref[...] - means[:, : p.lanes] - centred * means[:, p.lanes :]
        )
        scatter_row(p, grad, words_ref.at[slot], out_ref, h)

    each_row(p, row)


def whole_spec(value):
    dims = value.shape
    return pl.BlockSpec(dims, lambda *_: (0,) * len(dims))


def pack_spec(value, offset=0):
    dims = (1,) + value.shape[1:]
    return pl.BlockSpec(dims, lambda b, *_: (b + offset,) + (0,) * (len(dims) - 1))


def peer_spec(value, which=0, wide=1):
    dims = (value.shape[0], wide, 1) + value.shape[3:]
    return pl.BlockSpec(dims, lambda b, *_: (0, which, b) + (0,) * (len(dims) - 3))


def stored_spec(p, offset):
    return pl.BlockSpec(
        (p.stack, p.rows, p.groups, p.long), lambda b, *_: (b + offset, 0, 0, 0)
    )


def call(body, grid, ins, in_specs, outs, out_specs, scratch, flops, aliases=None):
    moved = sum(v.size * v.dtype.itemsize for v in ins) + sum(
        math.prod(o.shape) * o.dtype.itemsize for o in outs
    )
    return _call(body, grid, ins, in_specs, outs, out_specs, scratch, flops, moved, aliases)


def _call(body, grid, ins, in_specs, outs, out_specs, scratch, flops, moved, aliases):
    return pl.pallas_call(
        body,
        grid=grid,
        in_specs=in_specs,
        out_specs=out_specs,
        out_shape=outs,
        scratch_shapes=scratch,
        input_output_aliases=aliases or {},
        compiler_params=pltpu.CompilerParams(vmem_limit_bytes=VMEM_LIMIT),
        cost_estimate=pl.CostEstimate(flops=flops, bytes_accessed=moved, transcendentals=0),
    )(*ins)


def lon_tables(p):
    cos_lon, sin_lon = trig(p.lon, MW)
    wave = np.concatenate([cos_lon, -sin_lon], axis=1)
    turned = np.zeros((PACK, p.turn_pad, 2 * MW), np.float32)
    turned[:, : p.turn] = wave.reshape(p.turn, PACK, 2 * MW).transpose(1, 0, 2)
    turned = turned.reshape(PACK * p.turn_pad, 2 * MW)
    doubling = np.where(np.arange(MW) == 0, 1.0, 2.0).astype(np.float32)
    factor = np.float32(1.0 / math.sqrt(p.lon))
    plain_scale = np.full((2 * MW, 1), factor, np.float32)
    double_scale = (factor * np.tile(doubling, 2))[:, None].astype(np.float32)
    owner = turned.reshape(-1, 2, p.space, p.modes).transpose(0, 2, 1, 3).reshape(-1, 2 * MW)
    twice = np.tile(doubling.reshape(p.space, 1, p.modes), (1, 2, 1)).reshape(1, 2 * MW)
    to_half = lambda value: jnp.asarray(value, half)
    return (
        to_half(turned.T),
        jnp.asarray(plain_scale),
        jnp.asarray(double_scale),
        to_half(owner * twice),
        to_half(owner),
    )


def lat_tables(p):
    cos_lat, sin_lat = trig(p.lat, p.lat)
    there = np.block([[cos_lat, sin_lat], [-sin_lat, cos_lat]])
    there = there.reshape(2 * p.lat, 2, p.space, p.rows).transpose(0, 2, 1, 3)
    back = np.block([[cos_lat.T, -sin_lat.T], [sin_lat.T, cos_lat.T]])
    return jnp.asarray(there.reshape(2 * p.lat, 2 * p.lat), half), jnp.asarray(back, half)


def sum_tables(p):
    owner = np.arange(PACK) // p.groups
    lane_owner = np.repeat(owner, p.width)
    sums = np.zeros((2, 8, p.lanes), np.float32)
    wide = np.zeros((3, 8, 2, p.lanes), np.float32)
    for s in range(p.stack):
        sums[0, s] = lane_owner == s
        sums[1, p.stack + s] = lane_owner == s
        wide[:, s, 0] = lane_owner == s
        wide[:, p.stack + s, 1] = lane_owner == s
    return jnp.asarray(sums, half), jnp.asarray(wide.reshape(24, 2 * p.lanes), half)


def lane_vector(p, vector):
    return jnp.tile(vector, p.stack)[None, :]


def exchange(value):
    return lax.all_to_all(value, "space", 0, 0, tiled=True)


def around(value, axis, size):
    gathered = [value]
    for step in range(1, size):
        gathered.append(
            lax.ppermute(value, axis, [(i, (i + step) % size) for i in range(size)])
        )
    return gathered


def reduced(p, value, kind):
    step = 1
    while step < p.space:
        own = value.astype(kind)
        other = lax.ppermute(own, "space", [(i, i ^ step) for i in range(p.space)])
        value = own.astype(single) + other.astype(single)
        step *= 2
    return value


def on_device(space, chan, members, gain, shift, w_first, b_first, w_second, b_second, cotangent):
    p = Plan(members, w_first.shape[-1], space, chan)
    size = p.packs // 2
    grid = (size,)
    table, plain_scale, double_scale, mixed_table, slope_table = lon_tables(p)
    there_table, back_table = lat_tables(p)
    sum_table, wide_table = sum_tables(p)
    gain_lanes, shift_lanes = lane_vector(p, gain), lane_vector(p, shift)
    both_weights = jnp.pad(
        jnp.stack([w_first, w_second]), ((0, 0),) * 4 + ((0, LANES - p.width),)
    )
    bias = jnp.concatenate(
        [b[ri].reshape(-1) for b in (b_first, b_second) for ri in range(2) for _ in range(p.stack)]
    ).reshape(2, 2 * p.lanes)
    tokens_rows = PACK * p.turn_pad
    dft_flops = 2 * size * p.rows * tokens_rows * 2 * MW * p.lanes
    words = pltpu.VMEM((SLOTS, PACK, p.word_pad, LANES), single)
    lines = pltpu.VMEM((SLOTS, p.stack, p.word_pad * p.groups, LANES), single)
    turn_in = pltpu.VMEM((p.tiles, MW * 2 * p.rows, LANES), single)
    rows_scratch = pltpu.VMEM((p.rows, 8, tokens_rows), single)

    def sent(wide):
        return jax.ShapeDtypeStruct((space, wide, size, p.modes, 2 * p.rows, p.lanes), half)

    def returned(wide):
        return jax.ShapeDtypeStruct((space, wide, size, p.rows, 2 * p.modes, p.lanes), half)

    count = 2 * p.stack * p.rows
    stored = jax.ShapeDtypeStruct(members.shape, half)

    def out_call(body, ins, specs, out, out_spec, scratch, flops, before):
        ins, specs = list(ins), list(specs)
        aliases = {}
        inner = body
        if before is not None:
            place = len(ins)
            inner = lambda *refs: body(*refs[:place], *refs[place + 1 :])
            ins.append(before)
            specs.append(pl.BlockSpec(memory_space=pl.ANY))
            aliases = {place: 0}
        return call(inner, grid, tuple(ins), specs, [out], [out_spec], scratch, flops, aliases)[0]

    def cotangent_chunk(c, wide):
        return out_call(
            functools.partial(cotangent_kernel, p), (cotangent, table, double_scale),
            [stored_spec(p, c * size), whole_spec(table), whole_spec(double_scale)],
            sent(wide), peer_spec(sent(wide)), [words, turn_in], dft_flops, None,
        )

    def stats_chunk(c):
        ins = (members, sum_table)
        outs = [
            jax.ShapeDtypeStruct((size, p.rows, tokens_rows, p.lanes), half),
            jax.ShapeDtypeStruct((size, count, tokens_rows), single),
        ]
        return call(
            functools.partial(stats_kernel, p), grid, ins,
            [stored_spec(p, c * size), whole_spec(sum_table)],
            outs, [pack_spec(o) for o in outs], [words, rows_scratch], dft_flops // 4,
        )

    def normalise_chunk(stats, tokens, before):
        tail = (gain_lanes, shift_lanes, table, plain_scale, wide_table)
        out = sent(1 if before is None else 2)
        return out_call(
            functools.partial(normalise_kernel, p), (*stats, tokens, *tail),
            [pack_spec(s) for s in stats] + [pack_spec(tokens)] + [whole_spec(v) for v in tail],
            out, peer_spec(out, out.shape[1] - 1), [rows_scratch, turn_in], dft_flops, before,
        )

    step_modes = 2 if p.modes % 2 == 0 else 1
    wide_lanes = 2 * p.lanes

    def spectral_chunk(x_in, x_which, g_in, joined):
        tail = (there_table, back_table, both_weights, bias)

        def mode_spec(which):
            return pl.BlockSpec(
                (space, 1, 1, step_modes, 2 * p.rows, p.lanes),
                lambda b, m: (0, which, b, m, 0, 0),
            )

        outs = [returned(2)] if joined else [returned(1), returned(1)]
        out_specs = [peer_spec(o, 0, o.shape[1]) for o in outs]
        grads = jax.ShapeDtypeStruct((2, 2, p.groups, p.width, LANES), single)
        bias_grads = jax.ShapeDtypeStruct((16, wide_lanes), single)
        kept = pltpu.VMEM((p.modes * p.lat, wide_lanes), half)
        held = pltpu.VMEM((step_modes * p.lat, wide_lanes), single)
        brief = pltpu.VMEM((step_modes * p.lat, wide_lanes), half)
        turn_out = pltpu.VMEM((p.tiles, p.lat * 2 * p.modes, LANES), single)
        return call(
            functools.partial(spectral_kernel, p, step_modes, joined),
            (size, p.modes // step_modes), (x_in, g_in, *tail),
            [mode_spec(x_which), mode_spec(0)] + [whole_spec(v) for v in tail],
            [*outs, grads, bias_grads],
            [*out_specs, whole_spec(grads), whole_spec(bias_grads)],
            [kept] * 4 + [held] * 2 + [brief] * 2 + [turn_out] * 2
            + [pltpu.VMEM((wide_lanes, wide_lanes), single)] * 2
            + [pltpu.VMEM((wide_lanes, wide_lanes), half)] * 2,
            12 * size * p.modes * p.lat * wide_lanes * wide_lanes,
        )

    def mixed_chunk(c, rows_in, which, before):
        return out_call(
            functools.partial(mixed_kernel, p), (rows_in, mixed_table),
            [peer_spec(rows_in, which), whole_spec(mixed_table)], stored, stored_spec(p, c * size),
            [lines], dft_flops, before,
        )

    def slope_sums_chunk(stats, rows_in, which, tokens):
        tail = (gain_lanes, slope_table, wide_table, sum_table)
        outs = [
            jax.ShapeDtypeStruct((size, count, tokens_rows), single),
            jax.ShapeDtypeStruct((16, p.lanes), single),
        ]
        return call(
            functools.partial(slope_sums_kernel, p), grid,
            (*stats, rows_in, tokens, *tail),
            [pack_spec(s) for s in stats] + [peer_spec(rows_in, which), pack_spec(tokens)]
            + [whole_spec(v) for v in tail],
            outs, [pack_spec(outs[0]), whole_spec(outs[1])], [rows_scratch, rows_scratch],
            dft_flops,
        )

    def input_grad_chunk(c, stats, parts, rows_in, which, tokens, before):
        tail = (gain_lanes, slope_table, wide_table)
        return out_call(
            functools.partial(input_grad_kernel, p),
            (*stats, *parts, rows_in, tokens, *tail),
            [pack_spec(s) for s in (*stats, *parts)]
            + [peer_spec(rows_in, which), pack_spec(tokens)] + [whole_spec(v) for v in tail],
            stored, stored_spec(p, c * size), [rows_scratch, rows_scratch, lines], dft_flops,
            before,
        )

    def channel_sums(value):
        return around(value, "chan", chan)

    g0 = exchange(cotangent_chunk(0, 1))
    tokens0, sums = stats_chunk(0)
    stats0 = channel_sums(sums)
    x0 = exchange(normalise_chunk(stats0, tokens0, None))
    both1 = cotangent_chunk(1, 2)
    tokens1, sums = stats_chunk(1)
    stats1 = channel_sums(sums)
    both1 = exchange(normalise_chunk(stats1, tokens1, both1))
    out0, gw0, gb0 = spectral_chunk(x0, 0, g0, True)
    rows0 = exchange(out0)
    y1, dx1, gw1, gb1 = spectral_chunk(both1, 1, both1, False)
    dx1 = exchange(dx1)
    y1 = exchange(y1)
    sums, params0 = slope_sums_chunk(stats0, rows0, 1, tokens0)
    parts = channel_sums(sums.astype(half))
    grad_input = input_grad_chunk(0, stats0, parts, rows0, 1, tokens0, None)
    mixed = mixed_chunk(0, rows0, 0, None)
    sums, params1 = slope_sums_chunk(stats1, dx1, 0, tokens1)
    parts = channel_sums(sums.astype(half))
    grad_input = input_grad_chunk(1, stats1, parts, dx1, 0, tokens1, grad_input)
    mixed = mixed_chunk(1, y1, 0, mixed)
    weight_grads, bias_grads, param_grads = gw0 + gw1, gb0 + gb1, params0 + params1

    def by_channel(rows):
        return rows.reshape(-1, p.stack, p.groups * p.width).sum(1)

    weights = weight_grads.reshape(-1, LANES)
    flat_bias = bias_grads.reshape(2, 8, 2, p.stack, p.groups * p.width).sum((1, 3))
    flat_params = by_channel(param_grads.reshape(2, 8, p.lanes).sum(1))
    flat = jnp.concatenate([weights, flat_bias.reshape(-1, LANES)])
    flat = reduced(p, flat, half)
    grads = flat[: weights.shape[0]].reshape(weight_grads.shape)[..., : p.width]
    flat_bias = flat[weights.shape[0] :].reshape((2,) + b_first.shape)
    both = reduced(p, flat_params, single)
    return (mixed, grad_input, grads[0], flat_bias[0], grads[1], flat_bias[1], both[0], both[1])


def solution(mesh):
    tokens = P(None, "space", "chan", None)
    weights = P(None, "chan", None, None)
    biases = P(None, "chan", None)
    placed = (tokens, P("chan"), P("chan"), weights, biases, weights, biases, tokens)
    return jax.shard_map(
        functools.partial(on_device, mesh.shape["space"], mesh.shape["chan"]),
        mesh=mesh,
        in_specs=placed,
        out_specs=(tokens, tokens, weights, biases, weights, biases, P("chan"), P("chan")),
        check_vma=False,
    )
```

```python
import functools
import math

import jax
import jax.numpy as jnp
import numpy as np
from jax import lax
from jax.experimental import pallas as pl
from jax.experimental.pallas import tpu as pltpu
from jax.sharding import PartitionSpec as P


MW = 64
LANES = 128
PACK = 4

shrink_level = 0.05
norm_epsilon = 1e-05
gelu_scale = 0.7978845608
gelu_cubic = 0.044715

half = jnp.bfloat16
single = jnp.float32
VMEM_LIMIT = 67043328
SLOTS = 2

TN = (((0,), (0,)), ((), ()))
NT = (((1,), (1,)), ((), ()))


def mul(first_op, second_op, dims=(((1,), (0,)), ((), ()))):
    return lax.dot_general(first_op, second_op, dims, preferred_element_type=single)


def trig(length, columns):
    angles = (np.arange(length)[:, None] * np.arange(columns)[None, :] % length).astype(np.float32)
    angles = (angles * np.float32(2.0 * math.pi / length)).astype(np.float64)
    cast = lambda table: table.astype(np.float32).astype(half).astype(np.float32)
    return cast(np.cos(angles)), cast(np.sin(angles))


class Plan:
    def __init__(self, members, width, space, chan):
        self.batch, self.rows, self.groups, self.long = members.shape
        self.width, self.space, self.chan = width, space, chan
        self.lon = self.long // width
        self.lat = self.rows * space
        self.modes = MW // space
        self.stack = PACK // self.groups
        self.packs = self.batch // self.stack
        self.lanes = PACK * width
        self.tiles = self.lanes // LANES
        self.turn = self.lon // PACK
        self.turn_pad = -(-self.turn // 16) * 16
        self.words = self.long // LANES
        self.word_pad = self.tiles * self.turn_pad
        self.channels = self.groups * width * chan


def moved_lanes(p, fetch, from_start, to_start, tile):
    pieces = []
    for slot in range(PACK):
        low = max(to_start(slot), tile * LANES)
        high = min(to_start(slot) + p.width, (tile + 1) * LANES)
        at = low
        while at < high:
            source = at - to_start(slot) + from_start(slot)
            stop = min(high, at + LANES - source % LANES)
            shift = (at - source) % LANES
            pieces.append((stop - tile * LANES, fetch(slot, source // LANES, shift)))
            at = stop
    return pieces


def merged(pieces, lane):
    value = pieces[-1][1]
    for stop, piece in reversed(pieces[:-1]):
        value = jnp.where(lane < stop, piece, value)
    return value


def rolled(value, shift):
    return value if shift == 0 else pltpu.roll(value, shift, 1)


def spread(p, stored_ref, words_ref, h):
    for q in range(PACK):
        line = stored_ref[q // p.groups, h, q % p.groups, :]
        words_ref[q, : p.words, :] = line.reshape(p.words, LANES).astype(single)


def gather_row(p, words_ref):
    lane = lax.broadcasted_iota(jnp.int32, (p.turn_pad, LANES), 1)
    source = {}
    for q in range(PACK):
        for i in range(p.tiles):
            source[q, i] = words_ref[q, pl.ds(i, p.turn_pad, stride=p.tiles), :]
    rows = []
    for r in range(PACK):
        cache = {}

        def fetch(q, i, shift):
            key = (q, i, shift)
            if key not in cache:
                cache[key] = rolled(source[q, i], shift)
            return cache[key]

        tiles = []
        for c in range(p.tiles):
            pieces = moved_lanes(p, fetch, lambda q: r * p.width, lambda q: q * p.width, c)
            tiles.append(merged(pieces, lane).astype(half))
        rows.append(jnp.concatenate(tiles, axis=1))
    return jnp.concatenate(rows, axis=0)


def scatter_row(p, tokens, words_ref, stored_ref, h):
    lane = lax.broadcasted_iota(jnp.int32, (p.turn_pad, LANES), 1)
    for q in range(PACK):
        s, n = divmod(q, p.groups)

        def fetch(r, c, shift):
            part = tokens[r * p.turn_pad : (r + 1) * p.turn_pad, c * LANES : (c + 1) * LANES]
            return rolled(part, shift)

        for i in range(p.tiles):
            pieces = moved_lanes(p, fetch, lambda r: q * p.width, lambda r: r * p.width, i)
            at = pl.ds(i * p.groups + n, p.turn_pad, stride=p.tiles * p.groups)
            words_ref[s, at, :] = merged(pieces, lane)
    for s in range(p.stack):
        lines = words_ref[s, : p.words * p.groups, :].astype(half)
        for t in range(p.words):
            stored_ref[s, h, :, t * LANES : (t + 1) * LANES] = lines[
                t * p.groups : (t + 1) * p.groups, :
            ]


def clear_tail(p, words_ref):
    @pl.when(pl.program_id(0) == 0)
    def _():
        tail = p.word_pad - p.words
        words_ref[:, :, p.words :, :] = jnp.zeros(words_ref.shape[:2] + (tail, LANES), single)


def each_row(p, body):
    side = SLOTS if p.rows % SLOTS == 0 else 1

    def step(i, carry):
        for slot in range(side):
            body(i * side + slot, slot)
        return carry

    lax.fori_loop(0, p.rows // side, step, 0)


def analyse(p, tokens, table, scale, turn_ref, h):
    spectrum = mul(table, tokens) * scale
    for c in range(p.tiles):
        for ri in range(2):
            turn_ref[c, pl.ds(ri * p.rows + h, MW, stride=2 * p.rows), :] = spectrum[
                ri * MW : (ri + 1) * MW, c * LANES : (c + 1) * LANES
            ]


def send_turn(p, turn_ref, out_ref, outer, inner, which=0):
    count = outer * inner
    for d in range(p.space):
        for c in range(p.tiles):
            part = turn_ref[c, d * count : (d + 1) * count, :].reshape(outer, inner, LANES)
            out_ref[d, which, 0, :, :, c * LANES : (c + 1) * LANES] = part.astype(half)


def split_three(value):
    high = value.astype(half).astype(single)
    rest = value - high
    middle = rest.astype(half).astype(single)
    return high, middle, rest - middle


def expand(parts, spread_table):
    stacked = jnp.concatenate(split_three(parts), axis=0).astype(half)
    return mul(stacked, spread_table, TN)


def summed(table, value):
    high = value.astype(half)
    low = (value - high.astype(single)).astype(half)
    return mul(table, high, NT) + mul(table, low, NT)


def cotangent_kernel(p, stored_ref, table_ref, scale_ref, out_ref, words_ref, turn_ref):
    clear_tail(p, words_ref)

    def row(h, slot):
        spread(p, stored_ref, words_ref.at[slot], h)
        tokens = gather_row(p, words_ref.at[slot])
        analyse(p, tokens, table_ref[...], scale_ref[...], turn_ref, h)

    each_row(p, row)
    send_turn(p, turn_ref, out_ref, p.modes, 2 * p.rows)


def stats_kernel(p, stored_ref, sum_ref, tokens_ref, stat_ref, words_ref, rows_ref):
    clear_tail(p, words_ref)
    count = 2 * p.stack

    def row(h, slot):
        spread(p, stored_ref, words_ref.at[slot], h)
        tokens = gather_row(p, words_ref.at[slot])
        tokens_ref[0, h] = tokens
        wide = tokens.astype(single)
        rows_ref[h] = mul(sum_ref[0], tokens, NT) + summed(sum_ref[1], wide * wide)

    each_row(p, row)
    for h in range(p.rows):
        stat_ref[0, h * count : (h + 1) * count, :] = rows_ref[h, :count, :]


def moments(p, stat_refs, rows_ref):
    count = 2 * p.stack
    total = stat_refs[0][0]
    for ref in stat_refs[1:]:
        total = total + ref[0]
    for h in range(p.rows):
        part = total[h * count : (h + 1) * count] * (1.0 / p.channels)
        mean, square = part[: p.stack], part[p.stack :]
        inverse = lax.rsqrt(square - mean * mean + norm_epsilon)
        rows_ref[h, : p.stack, :] = mean
        rows_ref[h, p.stack : count, :] = inverse
        if count < 8:
            rows_ref[h, count:, :] = jnp.zeros((8 - count, p.turn_pad * PACK), single)


def normalise_kernel(p, *refs):
    stat_refs = refs[: p.chan]
    tokens_ref, affine_ref, table_ref, scale_ref, wide_ref = refs[p.chan : p.chan + 5]
    out_ref, rows_ref, turn_ref = refs[p.chan + 5 :]
    moments(p, stat_refs, rows_ref)

    def row(h, slot):
        each = expand(rows_ref[h], wide_ref[...])
        wide = tokens_ref[0, h].astype(single)
        centred = (wide - each[:, : p.lanes]) * each[:, p.lanes :]
        normed = (centred * affine_ref[0:1, :] + affine_ref[1:2, :]).astype(half)
        analyse(p, normed, table_ref[...], scale_ref[...], turn_ref, h)

    each_row(p, row)
    send_turn(p, turn_ref, out_ref, p.modes, 2 * p.rows)


def gelu_both(values):
    square = values * values
    inner = jnp.tanh(values * (gelu_scale + gelu_scale * gelu_cubic * square))
    upper = 0.5 + 0.5 * inner
    hidden = values * upper
    slope = upper + hidden * (1.0 - upper) * (
        2.0 * gelu_scale + 6.0 * gelu_scale * gelu_cubic * square
    )
    return hidden, slope


BAND = 16


def widened(p, value):
    blank = jnp.zeros((value.shape[0], LANES - p.width), single)
    return jnp.concatenate([value.astype(single), blank], axis=1)


def placed_slot(p, value, q):
    lane = lax.broadcasted_iota(jnp.int32, value.shape, 1)
    at, shift = divmod(q * p.width, LANES)
    turned = rolled(value, shift)
    tiles = [jnp.zeros_like(value) for _ in range(p.tiles)]
    tiles[at] = jnp.where(lane >= shift, turned, 0.0)
    if shift + p.width > LANES:
        tiles[at + 1] = jnp.where(lane < shift + p.width - LANES, turned, 0.0)
    return jnp.concatenate(tiles, axis=1)


def taken_slot(p, read, q):
    at, shift = divmod(q * p.width, LANES)
    value = rolled(read(at), -shift % LANES)
    if shift + p.width > LANES:
        lane = lax.broadcasted_iota(jnp.int32, value.shape, 1)
        value = jnp.where(lane < LANES - shift, value, rolled(read(at + 1), -shift % LANES))
    return value


PARTS = (((0, 0, 1), (1, 1, 1)), ((0, 1, 1), (1, 0, -1)))


def place_weights(p, w_refs, out_refs):
    for w_ref, out_ref in zip(w_refs, out_refs):
        for q in range(PACK):
            for part in range(2):
                wide = placed_slot(p, widened(p, w_ref[part, q % p.groups]), q)
                for row_ri, col_ri, sign in PARTS[part]:
                    top = row_ri * p.lanes + q * p.width
                    out_ref[top : top + p.width, col_ri * p.lanes : (col_ri + 1) * p.lanes] = (
                        sign * wide
                    ).astype(half)


def place_biases(p, b_refs, out_ref):
    for which, b_ref in enumerate(b_refs):
        for ri in range(2):
            row = jnp.zeros((1, p.lanes), single)
            for q in range(PACK):
                n = q % p.groups
                row = row + placed_slot(p, widened(p, b_ref[ri, n : n + 1, :]), q)
            out_ref[which : which + 1, ri * p.lanes : (ri + 1) * p.lanes] = row


def spectral_kernel(
    p,
    step_modes,
    joined,
    x_ref,
    g_ref,
    there_ref,
    back_ref,
    w_first_ref,
    w_second_ref,
    b_first_ref,
    b_second_ref,
    *refs,
):
    before_ref = None
    if not joined:
        before_ref, refs = refs[0], refs[1:]
    out_refs = refs[: 1 if joined else 2]
    (
    total_ref,
    gb_ref,
    bias_ref,
    lat_ref,
    hid_ref,
    gpost_ref,
    gpre_ref,
    wide_ref,
    slope_ref,
    gsh_ref,
    shr_ref,
    turn_y_ref,
    turn_x_ref,
    acc1_ref,
    acc2_ref,
    w1_ref,
    w2_ref,
    ) = refs[len(out_refs) :]
    pack, group = pl.program_id(0), pl.program_id(1)
    count = step_modes * p.lat
    factor = 1.0 / math.sqrt(p.lat)
    base = pl.multiple_of(group * count, count)

    @pl.when((pack == 0) & (group == 0))
    def _():
        place_weights(p, (w_first_ref, w_second_ref), (w1_ref, w2_ref))
        place_biases(p, (b_first_ref, b_second_ref), bias_ref)
        gb_ref[...] = jnp.zeros_like(gb_ref)
        acc1_ref[...] = jnp.zeros_like(acc1_ref)
        acc2_ref[...] = jnp.zeros_like(acc2_ref)

    def there(ref, into, offset):
        for m in range(step_modes):
            block = ref[:, 0, 0, m].reshape(2 * p.lat, p.lanes)
            out = (mul(there_ref[...], block) * factor).astype(half)
            at = pl.ds(offset + m * p.lat, p.lat)
            into[at, : p.lanes] = out[: p.lat]
            into[at, p.lanes :] = out[p.lat :]

    def back(value_of, turn_ref):
        for m in range(step_modes):
            rows = slice(m * p.lat, (m + 1) * p.lat)
            both = jnp.concatenate([value_of(rows, 0), value_of(rows, 1)], axis=0)
            out = mul(back_ref[...], both) * factor
            mode = group * step_modes + m
            for ri in range(2):
                for c in range(p.tiles):
                    turn_ref[c, pl.ds(ri * p.modes + mode, p.lat, stride=2 * p.modes), :] = out[
                        ri * p.lat : (ri + 1) * p.lat, c * LANES : (c + 1) * LANES
                    ]

    there(x_ref, lat_ref, base)
    there(g_ref, gsh_ref, 0)
    wide_ref[...] = mul(lat_ref[pl.ds(base, count), :], w1_ref[...])

    def first(i, carry):
        at = pl.ds(pl.multiple_of(i * BAND, BAND), BAND)
        hidden, slope = gelu_both(wide_ref[at, :] + bias_ref[0:1, :])
        hid_ref[pl.ds(pl.multiple_of(base + i * BAND, BAND), BAND), :] = hidden.astype(half)
        slope_ref[at, :] = slope
        return carry

    lax.fori_loop(0, count // BAND, first, 0)
    wide_ref[...] = mul(hid_ref[pl.ds(base, count), :], w2_ref[...])

    def second(i, carry):
        at = pl.ds(pl.multiple_of(i * BAND, BAND), BAND)
        post = wide_ref[at, :] + bias_ref[1:2, :]
        inner = jnp.tanh(post * (1.0 / shrink_level))
        shr_ref[at, :] = (post - shrink_level * inner).astype(half)
        gpost = (gsh_ref[at, :].astype(single) * (inner * inner)).astype(half)
        gpost_ref[pl.ds(pl.multiple_of(base + i * BAND, BAND), BAND), :] = gpost
        gb_ref[8:16, :] += gpost.astype(single).reshape(BAND // 8, 8, 2 * p.lanes).sum(0)
        return carry

    lax.fori_loop(0, count // BAND, second, 0)
    back(lambda rows, ri: shr_ref[rows, ri * p.lanes : (ri + 1) * p.lanes], turn_y_ref)
    wide_ref[...] = mul(gpost_ref[pl.ds(base, count), :], w2_ref[...], NT)

    def third(i, carry):
        at = pl.ds(pl.multiple_of(i * BAND, BAND), BAND)
        gpre = (wide_ref[at, :] * slope_ref[at, :]).astype(half)
        gpre_ref[pl.ds(pl.multiple_of(base + i * BAND, BAND), BAND), :] = gpre
        gb_ref[0:8, :] += gpre.astype(single).reshape(BAND // 8, 8, 2 * p.lanes).sum(0)
        return carry

    lax.fori_loop(0, count // BAND, third, 0)
    shr_ref[...] = mul(gpre_ref[pl.ds(base, count), :], w1_ref[...], NT).astype(half)
    back(lambda rows, ri: shr_ref[rows, ri * p.lanes : (ri + 1) * p.lanes], turn_x_ref)

    @pl.when(group == pl.num_programs(1) - 1)
    def _():
        send_turn(p, turn_y_ref, out_refs[0], p.rows, 2 * p.modes)
        send_turn(p, turn_x_ref, out_refs[-1], p.rows, 2 * p.modes, len(out_refs) % 2)
        acc1_ref[...] += mul(lat_ref[...], gpre_ref[...], TN)
        acc2_ref[...] += mul(hid_ref[...], gpost_ref[...], TN)

    @pl.when((group == pl.num_programs(1) - 1) & (pack == pl.num_programs(0) - 1))
    def _():
        def keep(top, rows, value):
            at = slice(top, top + rows)
            if before_ref is not None:
                value = value + before_ref[at, :]
            total_ref[at, :] = value.astype(total_ref.dtype)

        place = 0
        for acc in (acc1_ref, acc2_ref):
            for part in range(2):
                for n in range(p.groups):
                    total = jnp.zeros((p.width, LANES), single)
                    for s in range(p.stack):
                        q = s * p.groups + n
                        for row_ri, col_ri, sign in PARTS[part]:
                            rows = slice(row_ri * p.lanes + q * p.width, row_ri * p.lanes + (q + 1) * p.width)

                            def read(tile):
                                left = col_ri * p.lanes + tile * LANES
                                return acc[rows, left : left + LANES]

                            total = total + sign * taken_slot(p, read, q)
                    keep(place, p.width, total)
                    place += p.width
        rows = []
        for which in range(2):
            sums = gb_ref[which * 8 : (which + 1) * 8, :].sum(0, keepdims=True)
            for ri in range(2):
                for n in range(p.groups):
                    row = jnp.zeros((1, LANES), single)
                    for s in range(p.stack):

                        def read(tile):
                            left = ri * p.lanes + tile * LANES
                            return sums[:, left : left + LANES]

                        row = row + taken_slot(p, read, s * p.groups + n)
                    rows.append(row)
        rows += [jnp.zeros((1, LANES), single)] * (-len(rows) % 8)
        keep(place, len(rows), jnp.concatenate(rows, axis=0))


def mixed_kernel(p, rows_ref, table_ref, out_ref, words_ref):
    factor = 1.0 / math.sqrt(p.lon)

    def row(h, slot):
        block = rows_ref[:, 0, 0, h].reshape(2 * MW, p.lanes)
        tokens = mul(table_ref[...], block) * factor
        scatter_row(p, tokens, words_ref.at[slot], out_ref, h)

    each_row(p, row)


def slope_sums_kernel(p, *refs):
    stat_refs = refs[: p.chan]
    rows_in_ref, tokens_ref, affine_ref, table_ref, wide_ref, sum_ref = refs[p.chan : p.chan + 6]
    sums_ref, param_ref, rows_ref, part_ref, dense_ref = refs[p.chan + 6 :]
    factor = 1.0 / math.sqrt(p.lon)
    count = 2 * p.stack
    moments(p, stat_refs, rows_ref)

    @pl.when(pl.program_id(0) == 0)
    def _():
        param_ref[...] = jnp.zeros_like(param_ref)

    def row(h, slot):
        block = rows_in_ref[:, 0, 0, h].reshape(2 * MW, p.lanes)
        normed_grad = mul(table_ref[...], block) * factor
        each = expand(rows_ref[h], wide_ref[...])
        wide = tokens_ref[0, h].astype(single)
        centred = (wide - each[:, : p.lanes]) * each[:, p.lanes :]
        product = normed_grad * centred
        folds = (PACK * p.turn_pad // 8, 8, p.lanes)
        param_ref[0:8, :] += product.reshape(folds).sum(0)
        param_ref[8:16, :] += normed_grad.reshape(folds).sum(0)
        gain = affine_ref[0:1, :]
        part_ref[h] = summed(sum_ref[0], normed_grad * gain) + summed(sum_ref[1], product * gain)

    each_row(p, row)
    for h in range(p.rows):
        dense_ref[h * count : (h + 1) * count, :] = part_ref[h, :count, :]
    sums_ref[0] = dense_ref[...].astype(half)


def input_grad_kernel(p, *refs):
    stat_refs, part_refs = refs[: p.chan], refs[p.chan : 2 * p.chan]
    rows_in_ref, tokens_ref, affine_ref, table_ref, wide_ref = refs[2 * p.chan : 2 * p.chan + 5]
    out_ref, rows_ref, part_ref, words_ref = refs[2 * p.chan + 5 :]
    factor = 1.0 / math.sqrt(p.lon)
    count = 2 * p.stack
    moments(p, stat_refs, rows_ref)
    total = part_refs[0][0].astype(single)
    for ref in part_refs[1:]:
        total = total + ref[0].astype(single)
    for h in range(p.rows):
        part_ref[h, :count, :] = total[h * count : (h + 1) * count] * (1.0 / p.channels)
        if count < 8:
            part_ref[h, count:, :] = jnp.zeros((8 - count, p.turn_pad * PACK), single)

    def row(h, slot):
        block = rows_in_ref[:, 0, 0, h].reshape(2 * MW, p.lanes)
        normed_grad = mul(table_ref[...], block) * factor
        each = expand(rows_ref[h], wide_ref[...])
        means = expand(part_ref[h], wide_ref[...])
        inverse = each[:, p.lanes :]
        centred = (tokens_ref[0, h].astype(single) - each[:, : p.lanes]) * inverse
        grad = inverse * (
            normed_grad * affine_ref[0:1, :] - means[:, : p.lanes] - centred * means[:, p.lanes :]
        )
        scatter_row(p, grad, words_ref.at[slot], out_ref, h)

    each_row(p, row)


def whole_spec(value):
    dims = value.shape
    return pl.BlockSpec(dims, lambda *_: (0,) * len(dims))


def pack_spec(value, offset=0):
    dims = (1,) + value.shape[1:]
    return pl.BlockSpec(dims, lambda b, *_: (b + offset,) + (0,) * (len(dims) - 1))


def peer_spec(value, which=0, wide=1):
    dims = (value.shape[0], wide, 1) + value.shape[3:]
    return pl.BlockSpec(dims, lambda b, *_: (0, which, b) + (0,) * (len(dims) - 3))


def stored_spec(p, offset):
    return pl.BlockSpec(
        (p.stack, p.rows, p.groups, p.long), lambda b, *_: (b + offset, 0, 0, 0)
    )


def call(body, grid, ins, in_specs, outs, out_specs, scratch, flops, aliases=None):
    moved = sum(v.size * v.dtype.itemsize for v in ins) + sum(
        math.prod(o.shape) * o.dtype.itemsize for o in outs
    )
    return _call(body, grid, ins, in_specs, outs, out_specs, scratch, flops, moved, aliases)


def _call(body, grid, ins, in_specs, outs, out_specs, scratch, flops, moved, aliases):
    return pl.pallas_call(
        body,
        grid=grid,
        in_specs=in_specs,
        out_specs=out_specs,
        out_shape=outs,
        scratch_shapes=scratch,
        input_output_aliases=aliases or {},
        compiler_params=pltpu.CompilerParams(vmem_limit_bytes=VMEM_LIMIT),
        cost_estimate=pl.CostEstimate(flops=flops, bytes_accessed=moved, transcendentals=0),
    )(*ins)


def lon_tables(p):
    cos_lon, sin_lon = trig(p.lon, MW)
    wave = np.concatenate([cos_lon, -sin_lon], axis=1)
    turned = np.zeros((PACK, p.turn_pad, 2 * MW), np.float32)
    turned[:, : p.turn] = wave.reshape(p.turn, PACK, 2 * MW).transpose(1, 0, 2)
    turned = turned.reshape(PACK * p.turn_pad, 2 * MW)
    doubling = np.where(np.arange(MW) == 0, 1.0, 2.0).astype(np.float32)
    factor = np.float32(1.0 / math.sqrt(p.lon))
    plain_scale = np.full((2 * MW, 1), factor, np.float32)
    double_scale = (factor * np.tile(doubling, 2))[:, None].astype(np.float32)
    owner = turned.reshape(-1, 2, p.space, p.modes).transpose(0, 2, 1, 3).reshape(-1, 2 * MW)
    twice = np.tile(doubling.reshape(p.space, 1, p.modes), (1, 2, 1)).reshape(1, 2 * MW)
    to_half = lambda value: jnp.asarray(value, half)
    return (
        to_half(turned.T),
        jnp.asarray(plain_scale),
        jnp.asarray(double_scale),
        to_half(owner * twice),
        to_half(owner),
    )


def lat_tables(p):
    cos_lat, sin_lat = trig(p.lat, p.lat)
    there = np.block([[cos_lat, sin_lat], [-sin_lat, cos_lat]])
    there = there.reshape(2 * p.lat, 2, p.space, p.rows).transpose(0, 2, 1, 3)
    back = np.block([[cos_lat.T, -sin_lat.T], [sin_lat.T, cos_lat.T]])
    return jnp.asarray(there.reshape(2 * p.lat, 2 * p.lat), half), jnp.asarray(back, half)


def sum_tables(p):
    owner = np.arange(PACK) // p.groups
    lane_owner = np.repeat(owner, p.width)
    sums = np.zeros((2, 8, p.lanes), np.float32)
    wide = np.zeros((3, 8, 2, p.lanes), np.float32)
    for s in range(p.stack):
        sums[0, s] = lane_owner == s
        sums[1, p.stack + s] = lane_owner == s
        wide[:, s, 0] = lane_owner == s
        wide[:, p.stack + s, 1] = lane_owner == s
    return jnp.asarray(sums, half), jnp.asarray(wide.reshape(24, 2 * p.lanes), half)


def exchange(value):
    return lax.all_to_all(value, "space", 0, 0, tiled=True)


def around(value, axis, size):
    gathered = [value]
    for step in range(1, size):
        gathered.append(
            lax.ppermute(value, axis, [(i, (i + step) % size) for i in range(size)])
        )
    return gathered


def reduced(p, value, kind):
    step = 1
    while step < p.space:
        own = value.astype(kind)
        other = lax.ppermute(own, "space", [(i, i ^ step) for i in range(p.space)])
        value = own.astype(single) + other.astype(single)
        step *= 2
    return value


def on_device(space, chan, members, gain, shift, w_first, b_first, w_second, b_second, cotangent):
    p = Plan(members, w_first.shape[-1], space, chan)
    size = p.packs // 2
    grid = (size,)
    table, plain_scale, double_scale, mixed_table, slope_table = lon_tables(p)
    there_table, back_table = lat_tables(p)
    sum_table, wide_table = sum_tables(p)
    affine = jnp.concatenate([gain] * p.stack + [shift] * p.stack).reshape(2, p.lanes)
    tokens_rows = PACK * p.turn_pad
    dft_flops = 2 * size * p.rows * tokens_rows * 2 * MW * p.lanes
    words = pltpu.VMEM((SLOTS, PACK, p.word_pad, LANES), single)
    lines = pltpu.VMEM((SLOTS, p.stack, p.word_pad * p.groups, LANES), single)
    turn_in = pltpu.VMEM((p.tiles, MW * 2 * p.rows, LANES), single)
    rows_scratch = pltpu.VMEM((p.rows, 8, tokens_rows), single)

    def sent(wide):
        return jax.ShapeDtypeStruct((space, wide, size, p.modes, 2 * p.rows, p.lanes), half)

    def returned(wide):
        return jax.ShapeDtypeStruct((space, wide, size, p.rows, 2 * p.modes, p.lanes), half)

    count = 2 * p.stack * p.rows
    stored = jax.ShapeDtypeStruct(members.shape, half)

    def out_call(body, ins, specs, out, out_spec, scratch, flops, before):
        ins, specs = list(ins), list(specs)
        aliases = {}
        inner = body
        if before is not None:
            place = len(ins)
            inner = lambda *refs: body(*refs[:place], *refs[place + 1 :])
            ins.append(before)
            specs.append(pl.BlockSpec(memory_space=pl.ANY))
            aliases = {place: 0}
        return call(inner, grid, tuple(ins), specs, [out], [out_spec], scratch, flops, aliases)[0]

    def cotangent_chunk(c, wide):
        return out_call(
            functools.partial(cotangent_kernel, p), (cotangent, table, double_scale),
            [stored_spec(p, c * size), whole_spec(table), whole_spec(double_scale)],
            sent(wide), peer_spec(sent(wide)), [words, turn_in], dft_flops, None,
        )

    def stats_chunk(c):
        ins = (members, sum_table)
        outs = [
            jax.ShapeDtypeStruct((size, p.rows, tokens_rows, p.lanes), half),
            jax.ShapeDtypeStruct((size, count, tokens_rows), single),
        ]
        return call(
            functools.partial(stats_kernel, p), grid, ins,
            [stored_spec(p, c * size), whole_spec(sum_table)],
            outs, [pack_spec(o) for o in outs], [words, rows_scratch], dft_flops // 4,
        )

    def normalise_chunk(stats, tokens, before):
        tail = (affine, table, plain_scale, wide_table)
        out = sent(1 if before is None else 2)
        return out_call(
            functools.partial(normalise_kernel, p), (*stats, tokens, *tail),
            [pack_spec(s) for s in stats] + [pack_spec(tokens)] + [whole_spec(v) for v in tail],
            out, peer_spec(out, out.shape[1] - 1), [rows_scratch, turn_in], dft_flops, before,
        )

    step_modes = 2 if p.modes % 2 == 0 else 1
    wide_lanes = 2 * p.lanes

    def spectral_chunk(x_in, x_which, g_in, before):
        joined = before is None
        tail = (there_table, back_table, w_first, w_second, b_first, b_second)
        tail += () if joined else (before,)

        def mode_spec(which):
            return pl.BlockSpec(
                (space, 1, 1, step_modes, 2 * p.rows, p.lanes),
                lambda b, m: (0, which, b, m, 0, 0),
            )

        outs = [returned(2)] if joined else [returned(1), returned(1)]
        out_specs = [peer_spec(o, 0, o.shape[1]) for o in outs]
        bias_rows = -(-4 * p.groups // 8) * 8
        totals = jax.ShapeDtypeStruct(
            (4 * p.groups * p.width + bias_rows, LANES), single if joined else half
        )
        kept = pltpu.VMEM((p.modes * p.lat, wide_lanes), half)
        held = pltpu.VMEM((step_modes * p.lat, wide_lanes), single)
        brief = pltpu.VMEM((step_modes * p.lat, wide_lanes), half)
        turn_out = pltpu.VMEM((p.tiles, p.lat * 2 * p.modes, LANES), single)
        return call(
            functools.partial(spectral_kernel, p, step_modes, joined),
            (size, p.modes // step_modes), (x_in, g_in, *tail),
            [mode_spec(x_which), mode_spec(0)] + [whole_spec(v) for v in tail],
            [*outs, totals],
            [*out_specs, whole_spec(totals)],
            [pltpu.VMEM((16, wide_lanes), single), pltpu.VMEM((2, wide_lanes), single)]
            + [kept] * 4 + [held] * 2 + [brief] * 2 + [turn_out] * 2
            + [pltpu.VMEM((wide_lanes, wide_lanes), single)] * 2
            + [pltpu.VMEM((wide_lanes, wide_lanes), half)] * 2,
            12 * size * p.modes * p.lat * wide_lanes * wide_lanes,
        )

    def mixed_chunk(c, rows_in, which, before):
        return out_call(
            functools.partial(mixed_kernel, p), (rows_in, mixed_table),
            [peer_spec(rows_in, which), whole_spec(mixed_table)], stored, stored_spec(p, c * size),
            [lines], dft_flops, before,
        )

    def slope_sums_chunk(stats, rows_in, which, tokens):
        tail = (affine, slope_table, wide_table, sum_table)
        outs = [
            jax.ShapeDtypeStruct((size, count, tokens_rows), half),
            jax.ShapeDtypeStruct((16, p.lanes), single),
        ]
        return call(
            functools.partial(slope_sums_kernel, p), grid,
            (*stats, rows_in, tokens, *tail),
            [pack_spec(s) for s in stats] + [peer_spec(rows_in, which), pack_spec(tokens)]
            + [whole_spec(v) for v in tail],
            outs, [pack_spec(outs[0]), whole_spec(outs[1])],
            [rows_scratch, rows_scratch, pltpu.VMEM((count, tokens_rows), single)],
            dft_flops,
        )

    def input_grad_chunk(c, stats, parts, rows_in, which, tokens, before):
        tail = (affine, slope_table, wide_table)
        return out_call(
            functools.partial(input_grad_kernel, p),
            (*stats, *parts, rows_in, tokens, *tail),
            [pack_spec(s) for s in (*stats, *parts)]
            + [peer_spec(rows_in, which), pack_spec(tokens)] + [whole_spec(v) for v in tail],
            stored, stored_spec(p, c * size), [rows_scratch, rows_scratch, lines], dft_flops,
            before,
        )

    def channel_sums(value):
        return around(value, "chan", chan)

    g0 = exchange(cotangent_chunk(0, 1))
    tokens0, sums = stats_chunk(0)
    stats0 = channel_sums(sums)
    x0 = exchange(normalise_chunk(stats0, tokens0, None))
    both1 = cotangent_chunk(1, 2)
    tokens1, sums = stats_chunk(1)
    stats1 = channel_sums(sums)
    both1 = exchange(normalise_chunk(stats1, tokens1, both1))
    out0, totals = spectral_chunk(x0, 0, g0, None)
    rows0 = exchange(out0)
    y1, dx1, totals = spectral_chunk(both1, 1, both1, totals)
    dx1 = exchange(dx1)
    y1 = exchange(y1)
    sums, params0 = slope_sums_chunk(stats0, rows0, 1, tokens0)
    parts = channel_sums(sums)
    grad_input = input_grad_chunk(0, stats0, parts, rows0, 1, tokens0, None)
    mixed = mixed_chunk(0, rows0, 0, None)
    sums, params1 = slope_sums_chunk(stats1, dx1, 0, tokens1)
    parts = channel_sums(sums)
    grad_input = input_grad_chunk(1, stats1, parts, dx1, 0, tokens1, grad_input)
    mixed = mixed_chunk(1, y1, 0, mixed)
    size_w = p.groups * p.width
    flat = reduced(p, totals, half)[:, : p.width]
    grads = flat[: 4 * size_w].reshape((2,) + w_first.shape)
    bias_grads = flat[4 * size_w : 4 * size_w + 4 * p.groups].reshape((2,) + b_first.shape)
    params = reduced(p, params0 + params1, single)
    params = params.reshape(2, 8, p.stack, size_w).sum((1, 2))
    return (
        mixed, grad_input, grads[0], bias_grads[0], grads[1], bias_grads[1], params[0], params[1]
    )


def solution(mesh):
    tokens = P(None, "space", "chan", None)
    weights = P(None, "chan", None, None)
    biases = P(None, "chan", None)
    placed = (tokens, P("chan"), P("chan"), weights, biases, weights, biases, tokens)
    return jax.shard_map(
        functools.partial(on_device, mesh.shape["space"], mesh.shape["chan"]),
        mesh=mesh,
        in_specs=placed,
        out_specs=(tokens, tokens, weights, biases, weights, biases, P("chan"), P("chan")),
        check_vma=False,
    )
```

```python
import functools
import math

import jax
import jax.numpy as jnp
import numpy as np
from jax import lax
from jax.experimental import pallas as pl
from jax.experimental.pallas import tpu as pltpu
from jax.sharding import PartitionSpec as P


MW = 64
LANES = 128
PACK = 4

shrink_level = 0.05
norm_epsilon = 1e-05
gelu_scale = 0.7978845608
gelu_cubic = 0.044715

half = jnp.bfloat16
single = jnp.float32
VMEM_LIMIT = 67043328
SLOTS = 4

TN = (((0,), (0,)), ((), ()))
NT = (((1,), (1,)), ((), ()))


def mul(first_op, second_op, dims=(((1,), (0,)), ((), ()))):
    return lax.dot_general(first_op, second_op, dims, preferred_element_type=single)


def trig(length, columns):
    angles = (np.arange(length)[:, None] * np.arange(columns)[None, :] % length).astype(np.float32)
    angles = (angles * np.float32(2.0 * math.pi / length)).astype(np.float64)
    cast = lambda table: table.astype(np.float32).astype(half).astype(np.float32)
    return cast(np.cos(angles)), cast(np.sin(angles))


class Plan:
    def __init__(self, members, width, space, chan):
        self.batch, self.rows, self.groups, self.long = members.shape
        self.width, self.space, self.chan = width, space, chan
        self.lon = self.long // width
        self.lat = self.rows * space
        self.modes = MW // space
        self.stack = PACK // self.groups
        self.packs = self.batch // self.stack
        self.lanes = PACK * width
        self.tiles = self.lanes // LANES
        self.turn = self.lon // PACK
        self.turn_pad = -(-self.turn // 16) * 16
        self.words = self.long // LANES
        self.word_pad = self.tiles * self.turn_pad
        self.channels = self.groups * width * chan


def moved_lanes(p, fetch, from_start, to_start, tile):
    pieces = []
    for slot in range(PACK):
        low = max(to_start(slot), tile * LANES)
        high = min(to_start(slot) + p.width, (tile + 1) * LANES)
        at = low
        while at < high:
            source = at - to_start(slot) + from_start(slot)
            stop = min(high, at + LANES - source % LANES)
            shift = (at - source) % LANES
            pieces.append((stop - tile * LANES, fetch(slot, source // LANES, shift)))
            at = stop
    return pieces


def merged(pieces, lane):
    value = pieces[-1][1]
    for stop, piece in reversed(pieces[:-1]):
        value = jnp.where(lane < stop, piece, value)
    return value


def rolled(value, shift):
    return value if shift == 0 else pltpu.roll(value, shift, 1)


def spread(p, stored_ref, words_ref, h):
    for q in range(PACK):
        line = stored_ref[q // p.groups, h, q % p.groups, :]
        words_ref[q, : p.words, :] = line.reshape(p.words, LANES).astype(single)


def gather_row(p, words_ref):
    lane = lax.broadcasted_iota(jnp.int32, (p.turn_pad, LANES), 1)
    source = {}
    for q in range(PACK):
        for i in range(p.tiles):
            source[q, i] = words_ref[q, pl.ds(i, p.turn_pad, stride=p.tiles), :]
    rows = []
    for r in range(PACK):
        cache = {}

        def fetch(q, i, shift):
            key = (q, i, shift)
            if key not in cache:
                cache[key] = rolled(source[q, i], shift)
            return cache[key]

        tiles = []
        for c in range(p.tiles):
            pieces = moved_lanes(p, fetch, lambda q: r * p.width, lambda q: q * p.width, c)
            tiles.append(merged(pieces, lane).astype(half))
        rows.append(jnp.concatenate(tiles, axis=1))
    return jnp.concatenate(rows, axis=0)


def scatter_row(p, tokens, words_ref, stored_ref, h):
    lane = lax.broadcasted_iota(jnp.int32, (p.turn_pad, LANES), 1)
    for q in range(PACK):
        s, n = divmod(q, p.groups)
        cache = {}

        def fetch(r, c, shift):
            if (r, c, shift) not in cache:
                part = tokens[r * p.turn_pad : (r + 1) * p.turn_pad, c * LANES : (c + 1) * LANES]
                cache[r, c, shift] = rolled(part, shift)
            return cache[r, c, shift]

        for i in range(p.tiles):
            pieces = moved_lanes(p, fetch, lambda r: q * p.width, lambda r: r * p.width, i)
            at = pl.ds(i * p.groups + n, p.turn_pad, stride=p.tiles * p.groups)
            words_ref[s, at, :] = merged(pieces, lane)
    for s in range(p.stack):
        lines = words_ref[s, : p.words * p.groups, :].astype(half)
        for t in range(p.words):
            stored_ref[s, h, :, t * LANES : (t + 1) * LANES] = lines[
                t * p.groups : (t + 1) * p.groups, :
            ]


def clear_tail(p, words_ref):
    @pl.when(pl.program_id(0) == 0)
    def _():
        tail = p.word_pad - p.words
        words_ref[:, :, p.words :, :] = jnp.zeros(words_ref.shape[:2] + (tail, LANES), single)


def each_row(p, body):
    side = SLOTS if p.rows % SLOTS == 0 else 1

    def step(i, carry):
        for slot in range(side):
            body(i * side + slot, slot)
        return carry

    lax.fori_loop(0, p.rows // side, step, 0)


def analyse(p, tokens, table, scale, turn_ref, h):
    spectrum = mul(table, tokens) * scale
    for c in range(p.tiles):
        for ri in range(2):
            turn_ref[c, pl.ds(ri * p.rows + h, MW, stride=2 * p.rows), :] = spectrum[
                ri * MW : (ri + 1) * MW, c * LANES : (c + 1) * LANES
            ]


def send_turn(p, turn_ref, out_ref, outer, inner, which=0):
    count = outer * inner
    for d in range(p.space):
        for c in range(p.tiles):
            part = turn_ref[c, d * count : (d + 1) * count, :].reshape(outer, inner, LANES)
            out_ref[d, which, 0, :, :, c * LANES : (c + 1) * LANES] = part.astype(half)


def split_three(value):
    high = value.astype(half).astype(single)
    rest = value - high
    middle = rest.astype(half).astype(single)
    return high, middle, rest - middle


def expand(p, parts, wide_ref):
    stacked = jnp.concatenate(split_three(parts), axis=0).astype(half)
    pairs = []
    for c in range(p.tiles):
        both = mul(stacked, wide_ref[:, 2 * c * LANES : 2 * (c + 1) * LANES], TN)
        pairs.append((both[:, :LANES], both[:, LANES:]))
    return pairs


def summed(table, value):
    high = value.astype(half)
    low = (value - high.astype(single)).astype(half)
    return mul(table, high, NT) + mul(table, low, NT)


def cotangent_kernel(p, stored_ref, table_ref, scale_ref, out_ref, words_ref, turn_ref):
    clear_tail(p, words_ref)

    def row(h, slot):
        spread(p, stored_ref, words_ref.at[slot], h)
        tokens = gather_row(p, words_ref.at[slot])
        analyse(p, tokens, table_ref[...], scale_ref[...], turn_ref, h)

    each_row(p, row)
    send_turn(p, turn_ref, out_ref, p.modes, 2 * p.rows)


def stats_kernel(p, stored_ref, sum_ref, tokens_ref, stat_ref, words_ref, rows_ref):
    clear_tail(p, words_ref)
    count = 2 * p.stack

    def row(h, slot):
        spread(p, stored_ref, words_ref.at[slot], h)
        tokens = gather_row(p, words_ref.at[slot])
        tokens_ref[0, h] = tokens
        wide = tokens.astype(single)
        rows_ref[h] = mul(sum_ref[0], tokens, NT) + summed(sum_ref[1], wide * wide)

    each_row(p, row)
    for h in range(p.rows):
        stat_ref[0, h * count : (h + 1) * count, :] = rows_ref[h, :count, :]


def moments(p, stat_refs, rows_ref):
    count = 2 * p.stack
    total = stat_refs[0][0]
    for ref in stat_refs[1:]:
        total = total + ref[0]
    for h in range(p.rows):
        part = total[h * count : (h + 1) * count] * (1.0 / p.channels)
        mean, square = part[: p.stack], part[p.stack :]
        inverse = lax.rsqrt(square - mean * mean + norm_epsilon)
        rows_ref[h, : p.stack, :] = mean
        rows_ref[h, p.stack : count, :] = inverse
        if count < 8:
            rows_ref[h, count:, :] = jnp.zeros((8 - count, p.turn_pad * PACK), single)


def normalise_kernel(p, *refs):
    stat_refs = refs[: p.chan]
    tokens_ref, affine_ref, table_ref, scale_ref, wide_ref = refs[p.chan : p.chan + 5]
    out_ref, rows_ref, turn_ref = refs[p.chan + 5 :]
    moments(p, stat_refs, rows_ref)

    def row(h, slot):
        tiles = []
        for c, (mean, inverse) in enumerate(expand(p, rows_ref[h], wide_ref)):
            at = slice(c * LANES, (c + 1) * LANES)
            centred = (tokens_ref[0, h, :, at].astype(single) - mean) * inverse
            tiles.append((centred * affine_ref[0:1, at] + affine_ref[1:2, at]).astype(half))
        normed = jnp.concatenate(tiles, axis=1)
        analyse(p, normed, table_ref[...], scale_ref[...], turn_ref, h)

    each_row(p, row)
    send_turn(p, turn_ref, out_ref, p.modes, 2 * p.rows)


def gelu_both(values):
    square = values * values
    inner = jnp.tanh(values * (gelu_scale + gelu_scale * gelu_cubic * square))
    upper = 0.5 + 0.5 * inner
    hidden = values * upper
    slope = upper + hidden * (1.0 - upper) * (
        2.0 * gelu_scale + 6.0 * gelu_scale * gelu_cubic * square
    )
    return hidden, slope


BAND = 32
COLUMNS = 256


def widened(p, value):
    blank = jnp.zeros((value.shape[0], LANES - p.width), single)
    return jnp.concatenate([value.astype(single), blank], axis=1)


def placed_slot(p, value, q):
    lane = lax.broadcasted_iota(jnp.int32, value.shape, 1)
    at, shift = divmod(q * p.width, LANES)
    turned = rolled(value, shift)
    tiles = [jnp.zeros_like(value) for _ in range(p.tiles)]
    tiles[at] = jnp.where(lane >= shift, turned, 0.0)
    if shift + p.width > LANES:
        tiles[at + 1] = jnp.where(lane < shift + p.width - LANES, turned, 0.0)
    return jnp.concatenate(tiles, axis=1)


def taken_slot(p, read, q):
    at, shift = divmod(q * p.width, LANES)
    value = rolled(read(at), -shift % LANES)
    if shift + p.width > LANES:
        lane = lax.broadcasted_iota(jnp.int32, value.shape, 1)
        value = jnp.where(lane < LANES - shift, value, rolled(read(at + 1), -shift % LANES))
    return value


PARTS = (((0, 0, 1), (1, 1, 1)), ((0, 1, 1), (1, 0, -1)))


def place_weights(p, w_refs, out_refs):
    for w_ref, out_ref in zip(w_refs, out_refs):
        for q in range(PACK):
            for part in range(2):
                wide = placed_slot(p, widened(p, w_ref[part, q % p.groups]), q)
                for row_ri, col_ri, sign in PARTS[part]:
                    top = row_ri * p.lanes + q * p.width
                    out_ref[top : top + p.width, col_ri * p.lanes : (col_ri + 1) * p.lanes] = (
                        sign * wide
                    ).astype(half)


def place_biases(p, b_refs, out_ref):
    for which, b_ref in enumerate(b_refs):
        for ri in range(2):
            row = jnp.zeros((1, p.lanes), single)
            for q in range(PACK):
                n = q % p.groups
                row = row + placed_slot(p, widened(p, b_ref[ri, n : n + 1, :]), q)
            out_ref[which : which + 1, ri * p.lanes : (ri + 1) * p.lanes] = row


def spectral_kernel(
    p,
    step_modes,
    joined,
    x_ref,
    g_ref,
    there_ref,
    back_ref,
    w_first_ref,
    w_second_ref,
    b_first_ref,
    b_second_ref,
    *refs,
):
    before_ref = None
    if not joined:
        before_ref, refs = refs[0], refs[1:]
    out_refs = refs[: 1 if joined else 2]
    (
    total_ref,
    gb_ref,
    bias_ref,
    lat_ref,
    hid_ref,
    gpost_ref,
    gpre_ref,
    slope_ref,
    gsh_ref,
    shr_ref,
    glat_ref,
    turn_y_ref,
    turn_x_ref,
    acc1_ref,
    acc2_ref,
    w1_ref,
    w2_ref,
    ) = refs[len(out_refs) :]
    pack, group = pl.program_id(0), pl.program_id(1)
    count = step_modes * p.lat
    factor = 1.0 / math.sqrt(p.lat)
    base = pl.multiple_of(group * count, count)

    @pl.when((pack == 0) & (group == 0))
    def _():
        place_weights(p, (w_first_ref, w_second_ref), (w1_ref, w2_ref))
        place_biases(p, (b_first_ref, b_second_ref), bias_ref)
        gb_ref[...] = jnp.zeros_like(gb_ref)
        acc1_ref[...] = jnp.zeros_like(acc1_ref)
        acc2_ref[...] = jnp.zeros_like(acc2_ref)

    def there(ref, into, offset):
        for m in range(step_modes):
            block = ref[:, 0, 0, m].reshape(2 * p.lat, p.lanes)
            out = (mul(there_ref[...], block) * factor).astype(half)
            at = pl.ds(offset + m * p.lat, p.lat)
            into[at, : p.lanes] = out[: p.lat]
            into[at, p.lanes :] = out[p.lat :]

    def back(value_of, turn_ref):
        for m in range(step_modes):
            rows = slice(m * p.lat, (m + 1) * p.lat)
            both = jnp.concatenate([value_of(rows, 0), value_of(rows, 1)], axis=0)
            out = mul(back_ref[...], both) * factor
            mode = group * step_modes + m
            for ri in range(2):
                for c in range(p.tiles):
                    turn_ref[c, pl.ds(ri * p.modes + mode, p.lat, stride=2 * p.modes), :] = out[
                        ri * p.lat : (ri + 1) * p.lat, c * LANES : (c + 1) * LANES
                    ]

    def bands(columns, body):
        for low in range(0, count, BAND):
            at = slice(low, low + BAND)
            body(at, pl.ds(pl.multiple_of(base + low, BAND), BAND), columns)

    def folded(value):
        return value.reshape(BAND // 8, 8, value.shape[1]).sum(0)

    there(x_ref, lat_ref, base)
    there(g_ref, gsh_ref, 0)
    every = [slice(low, low + COLUMNS) for low in range(0, 2 * p.lanes, COLUMNS)]
    lat = lat_ref[pl.ds(base, count), :]
    for columns in every:
        pre = mul(lat, w1_ref[:, columns])

        def first(at, kept, columns):
            hidden, slope = gelu_both(pre[at] + bias_ref[0:1, columns])
            hid_ref[kept, columns] = hidden.astype(half)
            slope_ref[at, columns] = slope

        bands(columns, first)
    hid = hid_ref[pl.ds(base, count), :]
    for columns in every:
        part = mul(hid, w2_ref[:, columns])
        sums = [jnp.zeros((8, COLUMNS), single)]

        def second(at, kept, columns):
            post = part[at] + bias_ref[1:2, columns]
            inner = jnp.tanh(post * (1.0 / shrink_level))
            shr_ref[at, columns] = (post - shrink_level * inner).astype(half)
            gpost = (gsh_ref[at, columns].astype(single) * (inner * inner)).astype(half)
            gpost_ref[kept, columns] = gpost
            sums[0] += folded(gpost.astype(single))

        bands(columns, second)
        gb_ref[8:16, columns] += sums[0]
    back(lambda rows, ri: shr_ref[rows, ri * p.lanes : (ri + 1) * p.lanes], turn_y_ref)
    gpost = gpost_ref[pl.ds(base, count), :]
    for columns in every:
        part = mul(gpost, w2_ref[columns, :], NT)
        sums = [jnp.zeros((8, COLUMNS), single)]

        def third(at, kept, columns):
            gpre = (part[at] * slope_ref[at, columns]).astype(half)
            gpre_ref[kept, columns] = gpre
            sums[0] += folded(gpre.astype(single))

        bands(columns, third)
        gb_ref[0:8, columns] += sums[0]
    gpre = gpre_ref[pl.ds(base, count), :]
    for columns in every:
        glat_ref[:, columns] = mul(gpre, w1_ref[columns, :], NT).astype(half)
    back(lambda rows, ri: glat_ref[rows, ri * p.lanes : (ri + 1) * p.lanes], turn_x_ref)

    @pl.when(group == pl.num_programs(1) - 1)
    def _():
        send_turn(p, turn_y_ref, out_refs[0], p.rows, 2 * p.modes)
        send_turn(p, turn_x_ref, out_refs[-1], p.rows, 2 * p.modes, len(out_refs) % 2)
        acc1_ref[...] += mul(lat_ref[...], gpre_ref[...], TN)
        acc2_ref[...] += mul(hid_ref[...], gpost_ref[...], TN)

    @pl.when((group == pl.num_programs(1) - 1) & (pack == pl.num_programs(0) - 1))
    def _():
        def keep(top, rows, value):
            at = slice(top, top + rows)
            if before_ref is not None:
                value = value + before_ref[at, :]
            total_ref[at, :] = value.astype(total_ref.dtype)

        place = 0
        for acc in (acc1_ref, acc2_ref):
            for part in range(2):
                for n in range(p.groups):
                    total = jnp.zeros((p.width, LANES), single)
                    for s in range(p.stack):
                        q = s * p.groups + n
                        for row_ri, col_ri, sign in PARTS[part]:
                            rows = slice(row_ri * p.lanes + q * p.width, row_ri * p.lanes + (q + 1) * p.width)

                            def read(tile):
                                left = col_ri * p.lanes + tile * LANES
                                return acc[rows, left : left + LANES]

                            total = total + sign * taken_slot(p, read, q)
                    keep(place, p.width, total)
                    place += p.width
        rows = []
        for which in range(2):
            sums = gb_ref[which * 8 : (which + 1) * 8, :].sum(0, keepdims=True)
            for ri in range(2):
                for n in range(p.groups):
                    row = jnp.zeros((1, LANES), single)
                    for s in range(p.stack):

                        def read(tile):
                            left = ri * p.lanes + tile * LANES
                            return sums[:, left : left + LANES]

                        row = row + taken_slot(p, read, s * p.groups + n)
                    rows.append(row)
        rows += [jnp.zeros((1, LANES), single)] * (-len(rows) % 8)
        keep(place, len(rows), jnp.concatenate(rows, axis=0))


def mixed_kernel(p, rows_ref, table_ref, out_ref, words_ref):
    factor = 1.0 / math.sqrt(p.lon)

    def row(h, slot):
        block = rows_ref[:, 0, 0, h].reshape(2 * MW, p.lanes)
        tokens = mul(table_ref[...], block) * factor
        scatter_row(p, tokens, words_ref.at[slot], out_ref, h)

    each_row(p, row)


def slope_sums_kernel(p, *refs):
    stat_refs = refs[: p.chan]
    rows_in_ref, tokens_ref, affine_ref, table_ref, wide_ref, sum_ref = refs[p.chan : p.chan + 6]
    sums_ref, total_ref, param_ref, rows_ref, part_ref, dense_ref = refs[p.chan + 6 :]
    factor = 1.0 / math.sqrt(p.lon)
    count = 2 * p.stack
    moments(p, stat_refs, rows_ref)

    @pl.when(pl.program_id(0) == 0)
    def _():
        param_ref[...] = jnp.zeros_like(param_ref)

    def row(h, slot):
        block = rows_in_ref[:, 0, 0, h].reshape(2 * MW, p.lanes)
        folds = (PACK * p.turn_pad // 8, 8, LANES)
        plain, scaled = [], []
        spectrum = mul(table_ref[...], block)
        for c, (mean, inverse) in enumerate(expand(p, rows_ref[h], wide_ref)):
            at = slice(c * LANES, (c + 1) * LANES)
            normed_grad = spectrum[:, at] * factor
            centred = (tokens_ref[0, h, :, at].astype(single) - mean) * inverse
            param_ref[0:8, at] += (normed_grad * centred).reshape(folds).sum(0)
            param_ref[8:16, at] += normed_grad.reshape(folds).sum(0)
            grad = normed_grad * affine_ref[0:1, at]
            plain.append(grad.astype(half))
            scaled.append((grad * centred).astype(half))
        part_ref[h] = mul(sum_ref[0], jnp.concatenate(plain, axis=1), NT) + mul(
            sum_ref[1], jnp.concatenate(scaled, axis=1), NT
        )

    each_row(p, row)
    for h in range(p.rows):
        dense_ref[h * count : (h + 1) * count, :] = part_ref[h, :count, :]
    sums_ref[0] = dense_ref[...].astype(half)

    @pl.when(pl.program_id(0) == pl.num_programs(0) - 1)
    def _():
        for kind in range(2):
            total_ref[kind : kind + 1, :] = param_ref[8 * kind : 8 * kind + 8, :].sum(
                0, keepdims=True
            )


def input_grad_kernel(p, *refs):
    stat_refs, part_refs = refs[: p.chan], refs[p.chan : 2 * p.chan]
    rows_in_ref, tokens_ref, affine_ref, table_ref, wide_ref = refs[2 * p.chan : 2 * p.chan + 5]
    out_ref, rows_ref, part_ref, words_ref = refs[2 * p.chan + 5 :]
    factor = 1.0 / math.sqrt(p.lon)
    count = 2 * p.stack
    moments(p, stat_refs, rows_ref)
    total = part_refs[0][0].astype(single)
    for ref in part_refs[1:]:
        total = total + ref[0].astype(single)
    for h in range(p.rows):
        part_ref[h, :count, :] = total[h * count : (h + 1) * count] * (1.0 / p.channels)
        if count < 8:
            part_ref[h, count:, :] = jnp.zeros((8 - count, p.turn_pad * PACK), single)

    def row(h, slot):
        block = rows_in_ref[:, 0, 0, h].reshape(2 * MW, p.lanes)
        spectrum = mul(table_ref[...], block)
        moment = expand(p, rows_ref[h], wide_ref)
        means = expand(p, part_ref[h], wide_ref)
        tiles = []
        for c in range(p.tiles):
            at = slice(c * LANES, (c + 1) * LANES)
            (mean, inverse), (first, second) = moment[c], means[c]
            centred = (tokens_ref[0, h, :, at].astype(single) - mean) * inverse
            grad = spectrum[:, at] * factor * affine_ref[0:1, at]
            tiles.append(inverse * (grad - first - centred * second))
        grad = jnp.concatenate(tiles, axis=1)
        scatter_row(p, grad, words_ref.at[slot], out_ref, h)

    each_row(p, row)


def whole_spec(value):
    dims = value.shape
    return pl.BlockSpec(dims, lambda *_: (0,) * len(dims))


def pack_spec(value, offset=0):
    dims = (1,) + value.shape[1:]
    return pl.BlockSpec(dims, lambda b, *_: (b + offset,) + (0,) * (len(dims) - 1))


def peer_spec(value, which=0, wide=1):
    dims = (value.shape[0], wide, 1) + value.shape[3:]
    return pl.BlockSpec(dims, lambda b, *_: (0, which, b) + (0,) * (len(dims) - 3))


def stored_spec(p, offset):
    return pl.BlockSpec(
        (p.stack, p.rows, p.groups, p.long), lambda b, *_: (b + offset, 0, 0, 0)
    )


def call(body, grid, ins, in_specs, outs, out_specs, scratch, flops, aliases=None):
    moved = sum(v.size * v.dtype.itemsize for v in ins) + sum(
        math.prod(o.shape) * o.dtype.itemsize for o in outs
    )
    return _call(body, grid, ins, in_specs, outs, out_specs, scratch, flops, moved, aliases)


def _call(body, grid, ins, in_specs, outs, out_specs, scratch, flops, moved, aliases):
    return pl.pallas_call(
        body,
        grid=grid,
        in_specs=in_specs,
        out_specs=out_specs,
        out_shape=outs,
        scratch_shapes=scratch,
        input_output_aliases=aliases or {},
        compiler_params=pltpu.CompilerParams(vmem_limit_bytes=VMEM_LIMIT),
        cost_estimate=pl.CostEstimate(flops=flops, bytes_accessed=moved, transcendentals=0),
    )(*ins)


def lon_tables(p):
    cos_lon, sin_lon = trig(p.lon, MW)
    wave = np.concatenate([cos_lon, -sin_lon], axis=1)
    turned = np.zeros((PACK, p.turn_pad, 2 * MW), np.float32)
    turned[:, : p.turn] = wave.reshape(p.turn, PACK, 2 * MW).transpose(1, 0, 2)
    turned = turned.reshape(PACK * p.turn_pad, 2 * MW)
    doubling = np.where(np.arange(MW) == 0, 1.0, 2.0).astype(np.float32)
    factor = np.float32(1.0 / math.sqrt(p.lon))
    plain_scale = np.full((2 * MW, 1), factor, np.float32)
    double_scale = (factor * np.tile(doubling, 2))[:, None].astype(np.float32)
    owner = turned.reshape(-1, 2, p.space, p.modes).transpose(0, 2, 1, 3).reshape(-1, 2 * MW)
    twice = np.tile(doubling.reshape(p.space, 1, p.modes), (1, 2, 1)).reshape(1, 2 * MW)
    to_half = lambda value: jnp.asarray(value, half)
    return (
        to_half(turned.T),
        jnp.asarray(plain_scale),
        jnp.asarray(double_scale),
        to_half(owner * twice),
        to_half(owner),
    )


def lat_tables(p):
    cos_lat, sin_lat = trig(p.lat, p.lat)
    there = np.block([[cos_lat, sin_lat], [-sin_lat, cos_lat]])
    there = there.reshape(2 * p.lat, 2, p.space, p.rows).transpose(0, 2, 1, 3)
    back = np.block([[cos_lat.T, -sin_lat.T], [sin_lat.T, cos_lat.T]])
    return jnp.asarray(there.reshape(2 * p.lat, 2 * p.lat), half), jnp.asarray(back, half)


def sum_tables(p):
    owner = np.arange(PACK) // p.groups
    lane_owner = np.repeat(owner, p.width)
    sums = np.zeros((2, 8, p.lanes), np.float32)
    wide = np.zeros((3, 8, 2, p.lanes), np.float32)
    for s in range(p.stack):
        sums[0, s] = lane_owner == s
        sums[1, p.stack + s] = lane_owner == s
        wide[:, s, 0] = lane_owner == s
        wide[:, p.stack + s, 1] = lane_owner == s
    wide = wide.reshape(24, 2, p.tiles, LANES).transpose(0, 2, 1, 3)
    return jnp.asarray(sums, half), jnp.asarray(wide.reshape(24, 2 * p.lanes), half)


def exchange(value):
    return lax.all_to_all(value, "space", 0, 0, tiled=True)


def around(value, axis, size):
    gathered = [value]
    for step in range(1, size):
        gathered.append(
            lax.ppermute(value, axis, [(i, (i + step) % size) for i in range(size)])
        )
    return gathered


def reduced(p, value, kind):
    step = 1
    while step < p.space:
        own = value.astype(kind)
        other = lax.ppermute(own, "space", [(i, i ^ step) for i in range(p.space)])
        value = own.astype(single) + other.astype(single)
        step *= 2
    return value


def on_device(space, chan, members, gain, shift, w_first, b_first, w_second, b_second, cotangent):
    p = Plan(members, w_first.shape[-1], space, chan)
    size = p.packs // 2
    grid = (size,)
    table, plain_scale, double_scale, mixed_table, slope_table = lon_tables(p)
    there_table, back_table = lat_tables(p)
    sum_table, wide_table = sum_tables(p)
    affine = jnp.concatenate([gain] * p.stack + [shift] * p.stack).reshape(2, p.lanes)
    tokens_rows = PACK * p.turn_pad
    dft_flops = 2 * size * p.rows * tokens_rows * 2 * MW * p.lanes
    words = pltpu.VMEM((SLOTS, PACK, p.word_pad, LANES), single)
    lines = pltpu.VMEM((SLOTS, p.stack, p.word_pad * p.groups, LANES), single)
    turn_in = pltpu.VMEM((p.tiles, MW * 2 * p.rows, LANES), single)
    rows_scratch = pltpu.VMEM((p.rows, 8, tokens_rows), single)

    def sent(wide):
        return jax.ShapeDtypeStruct((space, wide, size, p.modes, 2 * p.rows, p.lanes), half)

    def returned(wide):
        return jax.ShapeDtypeStruct((space, wide, size, p.rows, 2 * p.modes, p.lanes), half)

    count = 2 * p.stack * p.rows
    stored = jax.ShapeDtypeStruct(members.shape, half)

    def out_call(body, ins, specs, out, out_spec, scratch, flops, before):
        ins, specs = list(ins), list(specs)
        aliases = {}
        inner = body
        if before is not None:
            place = len(ins)
            inner = lambda *refs: body(*refs[:place], *refs[place + 1 :])
            ins.append(before)
            specs.append(pl.BlockSpec(memory_space=pl.ANY))
            aliases = {place: 0}
        return call(inner, grid, tuple(ins), specs, [out], [out_spec], scratch, flops, aliases)[0]

    def cotangent_chunk(c, wide):
        return out_call(
            functools.partial(cotangent_kernel, p), (cotangent, table, double_scale),
            [stored_spec(p, c * size), whole_spec(table), whole_spec(double_scale)],
            sent(wide), peer_spec(sent(wide)), [words, turn_in], dft_flops, None,
        )

    def stats_chunk(c):
        ins = (members, sum_table)
        outs = [
            jax.ShapeDtypeStruct((size, p.rows, tokens_rows, p.lanes), half),
            jax.ShapeDtypeStruct((size, count, tokens_rows), single),
        ]
        return call(
            functools.partial(stats_kernel, p), grid, ins,
            [stored_spec(p, c * size), whole_spec(sum_table)],
            outs, [pack_spec(o) for o in outs], [words, rows_scratch], dft_flops // 4,
        )

    def normalise_chunk(stats, tokens, before):
        tail = (affine, table, plain_scale, wide_table)
        out = sent(1 if before is None else 2)
        return out_call(
            functools.partial(normalise_kernel, p), (*stats, tokens, *tail),
            [pack_spec(s) for s in stats] + [pack_spec(tokens)] + [whole_spec(v) for v in tail],
            out, peer_spec(out, out.shape[1] - 1), [rows_scratch, turn_in], dft_flops, before,
        )

    step_modes = 2 if p.modes % 2 == 0 else 1
    wide_lanes = 2 * p.lanes

    def spectral_chunk(x_in, x_which, g_in, before):
        joined = before is None
        tail = (there_table, back_table, w_first, w_second, b_first, b_second)
        tail += () if joined else (before,)

        def mode_spec(which):
            return pl.BlockSpec(
                (space, 1, 1, step_modes, 2 * p.rows, p.lanes),
                lambda b, m: (0, which, b, m, 0, 0),
            )

        outs = [returned(2)] if joined else [returned(1), returned(1)]
        out_specs = [peer_spec(o, 0, o.shape[1]) for o in outs]
        bias_rows = -(-4 * p.groups // 8) * 8
        totals = jax.ShapeDtypeStruct(
            (4 * p.groups * p.width + bias_rows, LANES), single if joined else half
        )
        kept = pltpu.VMEM((p.modes * p.lat, wide_lanes), half)
        held = pltpu.VMEM((step_modes * p.lat, wide_lanes), single)
        brief = pltpu.VMEM((step_modes * p.lat, wide_lanes), half)
        turn_out = pltpu.VMEM((p.tiles, p.lat * 2 * p.modes, LANES), single)
        return call(
            functools.partial(spectral_kernel, p, step_modes, joined),
            (size, p.modes // step_modes), (x_in, g_in, *tail),
            [mode_spec(x_which), mode_spec(0)] + [whole_spec(v) for v in tail],
            [*outs, totals],
            [*out_specs, whole_spec(totals)],
            [pltpu.VMEM((16, wide_lanes), single), pltpu.VMEM((2, wide_lanes), single)]
            + [kept] * 4 + [held] + [brief] * 3 + [turn_out] * 2
            + [pltpu.VMEM((wide_lanes, wide_lanes), single)] * 2
            + [pltpu.VMEM((wide_lanes, wide_lanes), half)] * 2,
            12 * size * p.modes * p.lat * wide_lanes * wide_lanes,
        )

    def mixed_chunk(c, rows_in, which, before):
        return out_call(
            functools.partial(mixed_kernel, p), (rows_in, mixed_table),
            [peer_spec(rows_in, which), whole_spec(mixed_table)], stored, stored_spec(p, c * size),
            [lines], dft_flops, before,
        )

    def slope_sums_chunk(stats, rows_in, which, tokens):
        tail = (affine, slope_table, wide_table, sum_table)
        outs = [
            jax.ShapeDtypeStruct((size, count, tokens_rows), half),
            jax.ShapeDtypeStruct((2, p.lanes), single),
        ]
        return call(
            functools.partial(slope_sums_kernel, p), grid,
            (*stats, rows_in, tokens, *tail),
            [pack_spec(s) for s in stats] + [peer_spec(rows_in, which), pack_spec(tokens)]
            + [whole_spec(v) for v in tail],
            outs, [pack_spec(outs[0]), whole_spec(outs[1])],
            [
                pltpu.VMEM((16, p.lanes), single), rows_scratch, rows_scratch,
                pltpu.VMEM((count, tokens_rows), single),
            ],
            dft_flops,
        )

    def input_grad_chunk(c, stats, parts, rows_in, which, tokens, before):
        tail = (affine, slope_table, wide_table)
        return out_call(
            functools.partial(input_grad_kernel, p),
            (*stats, *parts, rows_in, tokens, *tail),
            [pack_spec(s) for s in (*stats, *parts)]
            + [peer_spec(rows_in, which), pack_spec(tokens)] + [whole_spec(v) for v in tail],
            stored, stored_spec(p, c * size), [rows_scratch, rows_scratch, lines], dft_flops,
            before,
        )

    def channel_sums(value):
        return around(value, "chan", chan)

    g0 = exchange(cotangent_chunk(0, 1))
    tokens0, sums = stats_chunk(0)
    stats0 = channel_sums(sums)
    x0 = exchange(normalise_chunk(stats0, tokens0, None))
    both1 = cotangent_chunk(1, 2)
    tokens1, sums = stats_chunk(1)
    stats1 = channel_sums(sums)
    both1 = exchange(normalise_chunk(stats1, tokens1, both1))
    out0, totals = spectral_chunk(x0, 0, g0, None)
    rows0 = exchange(out0)
    y1, dx1, totals = spectral_chunk(both1, 1, both1, totals)
    dx1 = exchange(dx1)
    y1 = exchange(y1)
    sums, params0 = slope_sums_chunk(stats0, rows0, 1, tokens0)
    parts = channel_sums(sums)
    grad_input = input_grad_chunk(0, stats0, parts, rows0, 1, tokens0, None)
    mixed = mixed_chunk(0, rows0, 0, None)
    sums, params1 = slope_sums_chunk(stats1, dx1, 0, tokens1)
    parts = channel_sums(sums)
    grad_input = input_grad_chunk(1, stats1, parts, dx1, 0, tokens1, grad_input)
    mixed = mixed_chunk(1, y1, 0, mixed)
    size_w = p.groups * p.width
    flat = reduced(p, totals, half)[:, : p.width]
    grads = flat[: 4 * size_w].reshape((2,) + w_first.shape)
    bias_grads = flat[4 * size_w : 4 * size_w + 4 * p.groups].reshape((2,) + b_first.shape)
    params = reduced(p, params0 + params1, single)
    params = params.reshape(2, p.stack, size_w).sum(1)
    return (
        mixed, grad_input, grads[0], bias_grads[0], grads[1], bias_grads[1], params[0], params[1]
    )


def solution(mesh):
    tokens = P(None, "space", "chan", None)
    weights = P(None, "chan", None, None)
    biases = P(None, "chan", None)
    placed = (tokens, P("chan"), P("chan"), weights, biases, weights, biases, tokens)
    return jax.shard_map(
        functools.partial(on_device, mesh.shape["space"], mesh.shape["chan"]),
        mesh=mesh,
        in_specs=placed,
        out_specs=(tokens, tokens, weights, biases, weights, biases, P("chan"), P("chan")),
        check_vma=False,
    )
```

```python
import functools
import math

import jax
import jax.numpy as jnp
import numpy as np
from jax import lax
from jax.experimental import pallas as pl
from jax.experimental.pallas import tpu as pltpu
from jax.sharding import PartitionSpec as P


MW = 64
LANES = 128
PACK = 4

shrink_level = 0.05
norm_epsilon = 1e-05
gelu_scale = 0.7978845608
gelu_cubic = 0.044715

half = jnp.bfloat16
single = jnp.float32
VMEM_LIMIT = 67043328
SLOTS = 4

TN = (((0,), (0,)), ((), ()))
NT = (((1,), (1,)), ((), ()))


def mul(first_op, second_op, dims=(((1,), (0,)), ((), ()))):
    return lax.dot_general(first_op, second_op, dims, preferred_element_type=single)


def trig(length, columns):
    angles = (np.arange(length)[:, None] * np.arange(columns)[None, :] % length).astype(np.float32)
    angles = (angles * np.float32(2.0 * math.pi / length)).astype(np.float64)
    cast = lambda table: table.astype(np.float32).astype(half).astype(np.float32)
    return cast(np.cos(angles)), cast(np.sin(angles))


class Plan:
    def __init__(self, members, width, space, chan):
        self.batch, self.rows, self.groups, self.long = members.shape
        self.width, self.space, self.chan = width, space, chan
        self.lon = self.long // width
        self.lat = self.rows * space
        self.modes = MW // space
        self.stack = PACK // self.groups
        self.packs = self.batch // self.stack
        self.lanes = PACK * width
        self.tiles = self.lanes // LANES
        self.turn = self.lon // PACK
        self.turn_pad = -(-self.turn // 16) * 16
        self.words = self.long // LANES
        self.step = SLOTS if self.rows % SLOTS == 0 else self.rows
        self.steps = self.rows // self.step
        self.word_pad = self.tiles * self.turn_pad
        self.channels = self.groups * width * chan


def moved_lanes(p, fetch, from_start, to_start, tile):
    pieces = []
    for slot in range(PACK):
        low = max(to_start(slot), tile * LANES)
        high = min(to_start(slot) + p.width, (tile + 1) * LANES)
        at = low
        while at < high:
            source = at - to_start(slot) + from_start(slot)
            stop = min(high, at + LANES - source % LANES)
            shift = (at - source) % LANES
            pieces.append((stop - tile * LANES, fetch(slot, source // LANES, shift)))
            at = stop
    return pieces


def merged(pieces, lane):
    value = pieces[-1][1]
    for stop, piece in reversed(pieces[:-1]):
        value = jnp.where(lane < stop, piece, value)
    return value


def rolled(value, shift):
    return value if shift == 0 else pltpu.roll(value, shift, 1)


def spread(p, stored_ref, words_ref, h):
    for q in range(PACK):
        line = stored_ref[q // p.groups, h, q % p.groups, :]
        words_ref[q, : p.words, :] = line.reshape(p.words, LANES).astype(single)


def gather_row(p, words_ref):
    lane = lax.broadcasted_iota(jnp.int32, (p.turn_pad, LANES), 1)
    source = {}
    for q in range(PACK):
        for i in range(p.tiles):
            source[q, i] = words_ref[q, pl.ds(i, p.turn_pad, stride=p.tiles), :]
    rows = []
    for r in range(PACK):
        cache = {}

        def fetch(q, i, shift):
            key = (q, i, shift)
            if key not in cache:
                cache[key] = rolled(source[q, i], shift)
            return cache[key]

        tiles = []
        for c in range(p.tiles):
            pieces = moved_lanes(p, fetch, lambda q: r * p.width, lambda q: q * p.width, c)
            tiles.append(merged(pieces, lane).astype(half))
        rows.append(jnp.concatenate(tiles, axis=1))
    return jnp.concatenate(rows, axis=0)


def scatter_row(p, tokens, words_ref, stored_ref, h):
    lane = lax.broadcasted_iota(jnp.int32, (p.turn_pad, LANES), 1)
    for q in range(PACK):
        s, n = divmod(q, p.groups)
        cache = {}

        def fetch(r, c, shift):
            if (r, c, shift) not in cache:
                part = tokens[r * p.turn_pad : (r + 1) * p.turn_pad, c * LANES : (c + 1) * LANES]
                cache[r, c, shift] = rolled(part, shift)
            return cache[r, c, shift]

        for i in range(p.tiles):
            pieces = moved_lanes(p, fetch, lambda r: q * p.width, lambda r: r * p.width, i)
            at = pl.ds(i * p.groups + n, p.turn_pad, stride=p.tiles * p.groups)
            words_ref[s, at, :] = merged(pieces, lane)
    for s in range(p.stack):
        lines = words_ref[s, : p.words * p.groups, :].astype(half)
        for t in range(p.words):
            stored_ref[s, h, :, t * LANES : (t + 1) * LANES] = lines[
                t * p.groups : (t + 1) * p.groups, :
            ]


def clear_tail(p, words_ref):
    @pl.when(first_step())
    def _():
        tail = p.word_pad - p.words
        words_ref[:, :, p.words :, :] = jnp.zeros(words_ref.shape[:2] + (tail, LANES), single)


def first_step():
    return (pl.program_id(0) == 0) & (pl.program_id(1) == 0)


def last_step():
    return (pl.program_id(0) == pl.num_programs(0) - 1) & (
        pl.program_id(1) == pl.num_programs(1) - 1
    )


def last_part():
    return pl.program_id(1) == pl.num_programs(1) - 1


def analyse(p, tokens, table, scale, turn_ref, h):
    h = pl.program_id(1) * p.step + h
    spectrum = mul(table, tokens) * scale
    for c in range(p.tiles):
        for ri in range(2):
            turn_ref[c, pl.ds(ri * p.rows + h, MW, stride=2 * p.rows), :] = spectrum[
                ri * MW : (ri + 1) * MW, c * LANES : (c + 1) * LANES
            ]


def send_turn(p, turn_ref, out_ref, outer, inner, which=0):
    count = outer * inner
    for d in range(p.space):
        for c in range(p.tiles):
            part = turn_ref[c, d * count : (d + 1) * count, :].reshape(outer, inner, LANES)
            out_ref[d, which, 0, :, :, c * LANES : (c + 1) * LANES] = part.astype(half)


def split_three(value):
    high = value.astype(half).astype(single)
    rest = value - high
    middle = rest.astype(half).astype(single)
    return high, middle, rest - middle


def expand(p, parts, wide_ref):
    stacked = jnp.concatenate(split_three(parts), axis=0).astype(half)
    pairs = []
    for c in range(p.tiles):
        both = mul(stacked, wide_ref[:, 2 * c * LANES : 2 * (c + 1) * LANES], TN)
        pairs.append((both[:, :LANES], both[:, LANES:]))
    return pairs


def summed(table, value):
    high = value.astype(half)
    low = (value - high.astype(single)).astype(half)
    return mul(table, high, NT) + mul(table, low, NT)


def cotangent_kernel(p, stored_ref, table_ref, scale_ref, out_ref, words_ref, turn_ref):
    clear_tail(p, words_ref)
    for h in range(p.step):
        spread(p, stored_ref, words_ref.at[h], h)
        tokens = gather_row(p, words_ref.at[h])
        analyse(p, tokens, table_ref[...], scale_ref[...], turn_ref, h)

    @pl.when(last_part())
    def _():
        send_turn(p, turn_ref, out_ref, p.modes, 2 * p.rows)


def stats_kernel(p, stored_ref, sum_ref, tokens_ref, stat_ref, words_ref):
    clear_tail(p, words_ref)
    count = 2 * p.stack
    for h in range(p.step):
        spread(p, stored_ref, words_ref.at[h], h)
        tokens = gather_row(p, words_ref.at[h])
        tokens_ref[0, h] = tokens
        wide = tokens.astype(single)
        rows = mul(sum_ref[0], tokens, NT) + summed(sum_ref[1], wide * wide)
        stat_ref[0, h * count : (h + 1) * count, :] = rows[:count]


def moments(p, stat_refs, rows_ref):
    count = 2 * p.stack
    total = stat_refs[0][0]
    for ref in stat_refs[1:]:
        total = total + ref[0]
    for h in range(p.step):
        part = total[h * count : (h + 1) * count] * (1.0 / p.channels)
        mean, square = part[: p.stack], part[p.stack :]
        inverse = lax.rsqrt(square - mean * mean + norm_epsilon)
        rows_ref[h, : p.stack, :] = mean
        rows_ref[h, p.stack : count, :] = inverse
        if count < 8:
            rows_ref[h, count:, :] = jnp.zeros((8 - count, p.turn_pad * PACK), single)


def normalise_kernel(p, *refs):
    stat_refs = refs[: p.chan]
    tokens_ref, affine_ref, table_ref, scale_ref, wide_ref = refs[p.chan : p.chan + 5]
    out_ref, rows_ref, turn_ref = refs[p.chan + 5 :]
    moments(p, stat_refs, rows_ref)

    for h in range(p.step):
        tiles = []
        for c, (mean, inverse) in enumerate(expand(p, rows_ref[h], wide_ref)):
            at = slice(c * LANES, (c + 1) * LANES)
            centred = (tokens_ref[0, h, :, at].astype(single) - mean) * inverse
            tiles.append((centred * affine_ref[0:1, at] + affine_ref[1:2, at]).astype(half))
        normed = jnp.concatenate(tiles, axis=1)
        analyse(p, normed, table_ref[...], scale_ref[...], turn_ref, h)

    @pl.when(last_part())
    def _():
        send_turn(p, turn_ref, out_ref, p.modes, 2 * p.rows)


def gelu_both(values):
    square = values * values
    inner = jnp.tanh(values * (gelu_scale + gelu_scale * gelu_cubic * square))
    upper = 0.5 + 0.5 * inner
    hidden = values * upper
    slope = upper + hidden * (1.0 - upper) * (
        2.0 * gelu_scale + 6.0 * gelu_scale * gelu_cubic * square
    )
    return hidden, slope


BAND = 32
COLUMNS = 256


def widened(p, value):
    blank = jnp.zeros((value.shape[0], LANES - p.width), single)
    return jnp.concatenate([value.astype(single), blank], axis=1)


def placed_slot(p, value, q):
    lane = lax.broadcasted_iota(jnp.int32, value.shape, 1)
    at, shift = divmod(q * p.width, LANES)
    turned = rolled(value, shift)
    tiles = [jnp.zeros_like(value) for _ in range(p.tiles)]
    tiles[at] = jnp.where(lane >= shift, turned, 0.0)
    if shift + p.width > LANES:
        tiles[at + 1] = jnp.where(lane < shift + p.width - LANES, turned, 0.0)
    return jnp.concatenate(tiles, axis=1)


def taken_slot(p, read, q):
    at, shift = divmod(q * p.width, LANES)
    value = rolled(read(at), -shift % LANES)
    if shift + p.width > LANES:
        lane = lax.broadcasted_iota(jnp.int32, value.shape, 1)
        value = jnp.where(lane < LANES - shift, value, rolled(read(at + 1), -shift % LANES))
    return value


PARTS = (((0, 0, 1), (1, 1, 1)), ((0, 1, 1), (1, 0, -1)))


def place_weights(p, w_refs, out_refs):
    for w_ref, out_ref in zip(w_refs, out_refs):
        for q in range(PACK):
            for part in range(2):
                wide = placed_slot(p, widened(p, w_ref[part, q % p.groups]), q)
                for row_ri, col_ri, sign in PARTS[part]:
                    top = row_ri * p.lanes + q * p.width
                    out_ref[top : top + p.width, col_ri * p.lanes : (col_ri + 1) * p.lanes] = (
                        sign * wide
                    ).astype(half)


def place_biases(p, b_refs, out_ref):
    for which, b_ref in enumerate(b_refs):
        for ri in range(2):
            row = jnp.zeros((1, p.lanes), single)
            for q in range(PACK):
                n = q % p.groups
                row = row + placed_slot(p, widened(p, b_ref[ri, n : n + 1, :]), q)
            out_ref[which : which + 1, ri * p.lanes : (ri + 1) * p.lanes] = row


def spectral_kernel(
    p,
    step_modes,
    joined,
    x_ref,
    g_ref,
    there_ref,
    back_ref,
    w_first_ref,
    w_second_ref,
    b_first_ref,
    b_second_ref,
    *refs,
):
    before_ref = None
    if not joined:
        before_ref, refs = refs[0], refs[1:]
    out_refs = refs[: 1 if joined else 2]
    (
    total_ref,
    gb_ref,
    bias_ref,
    lat_ref,
    hid_ref,
    gpost_ref,
    gpre_ref,
    slope_ref,
    gsh_ref,
    shr_ref,
    glat_ref,
    turn_y_ref,
    turn_x_ref,
    acc1_ref,
    acc2_ref,
    w1_ref,
    w2_ref,
    ) = refs[len(out_refs) :]
    pack, group = pl.program_id(0), pl.program_id(1)
    count = step_modes * p.lat
    factor = 1.0 / math.sqrt(p.lat)
    base = pl.multiple_of(group * count, count)

    @pl.when((pack == 0) & (group == 0))
    def _():
        place_weights(p, (w_first_ref, w_second_ref), (w1_ref, w2_ref))
        place_biases(p, (b_first_ref, b_second_ref), bias_ref)
        gb_ref[...] = jnp.zeros_like(gb_ref)
        acc1_ref[...] = jnp.zeros_like(acc1_ref)
        acc2_ref[...] = jnp.zeros_like(acc2_ref)

    def there(ref, into, offset):
        for m in range(step_modes):
            block = ref[:, 0, 0, m].reshape(2 * p.lat, p.lanes)
            out = (mul(there_ref[...], block) * factor).astype(half)
            at = pl.ds(offset + m * p.lat, p.lat)
            into[at, : p.lanes] = out[: p.lat]
            into[at, p.lanes :] = out[p.lat :]

    def back(value_of, turn_ref):
        for m in range(step_modes):
            rows = slice(m * p.lat, (m + 1) * p.lat)
            both = jnp.concatenate([value_of(rows, 0), value_of(rows, 1)], axis=0)
            out = mul(back_ref[...], both) * factor
            mode = group * step_modes + m
            for ri in range(2):
                for c in range(p.tiles):
                    turn_ref[c, pl.ds(ri * p.modes + mode, p.lat, stride=2 * p.modes), :] = out[
                        ri * p.lat : (ri + 1) * p.lat, c * LANES : (c + 1) * LANES
                    ]

    def bands(columns, body):
        for low in range(0, count, BAND):
            at = slice(low, low + BAND)
            body(at, pl.ds(pl.multiple_of(base + low, BAND), BAND), columns)

    def folded(value):
        return value.reshape(BAND // 8, 8, value.shape[1]).sum(0)

    there(x_ref, lat_ref, base)
    there(g_ref, gsh_ref, 0)
    every = [slice(low, low + COLUMNS) for low in range(0, 2 * p.lanes, COLUMNS)]
    lat = lat_ref[pl.ds(base, count), :]
    for columns in every:
        pre = mul(lat, w1_ref[:, columns])

        def first(at, kept, columns):
            hidden, slope = gelu_both(pre[at] + bias_ref[0:1, columns])
            hid_ref[kept, columns] = hidden.astype(half)
            slope_ref[at, columns] = slope

        bands(columns, first)
    hid = hid_ref[pl.ds(base, count), :]
    for columns in every:
        part = mul(hid, w2_ref[:, columns])
        sums = [jnp.zeros((8, COLUMNS), single)]

        def second(at, kept, columns):
            post = part[at] + bias_ref[1:2, columns]
            inner = jnp.tanh(post * (1.0 / shrink_level))
            shr_ref[at, columns] = (post - shrink_level * inner).astype(half)
            gpost = (gsh_ref[at, columns].astype(single) * (inner * inner)).astype(half)
            gpost_ref[kept, columns] = gpost
            sums[0] += folded(gpost.astype(single))

        bands(columns, second)
        gb_ref[8:16, columns] += sums[0]
    back(lambda rows, ri: shr_ref[rows, ri * p.lanes : (ri + 1) * p.lanes], turn_y_ref)
    gpost = gpost_ref[pl.ds(base, count), :]
    for columns in every:
        part = mul(gpost, w2_ref[columns, :], NT)
        sums = [jnp.zeros((8, COLUMNS), single)]

        def third(at, kept, columns):
            gpre = (part[at] * slope_ref[at, columns]).astype(half)
            gpre_ref[kept, columns] = gpre
            sums[0] += folded(gpre.astype(single))

        bands(columns, third)
        gb_ref[0:8, columns] += sums[0]
    gpre = gpre_ref[pl.ds(base, count), :]
    for columns in every:
        glat_ref[:, columns] = mul(gpre, w1_ref[columns, :], NT).astype(half)
    back(lambda rows, ri: glat_ref[rows, ri * p.lanes : (ri + 1) * p.lanes], turn_x_ref)

    @pl.when(group == pl.num_programs(1) - 1)
    def _():
        send_turn(p, turn_y_ref, out_refs[0], p.rows, 2 * p.modes)
        send_turn(p, turn_x_ref, out_refs[-1], p.rows, 2 * p.modes, len(out_refs) % 2)
        acc1_ref[...] += mul(lat_ref[...], gpre_ref[...], TN)
        acc2_ref[...] += mul(hid_ref[...], gpost_ref[...], TN)

    @pl.when((group == pl.num_programs(1) - 1) & (pack == pl.num_programs(0) - 1))
    def _():
        def keep(top, rows, value):
            at = slice(top, top + rows)
            if before_ref is not None:
                value = value + before_ref[at, :]
            total_ref[at, :] = value.astype(total_ref.dtype)

        place = 0
        for acc in (acc1_ref, acc2_ref):
            for part in range(2):
                for n in range(p.groups):
                    total = jnp.zeros((p.width, LANES), single)
                    for s in range(p.stack):
                        q = s * p.groups + n
                        for row_ri, col_ri, sign in PARTS[part]:
                            rows = slice(row_ri * p.lanes + q * p.width, row_ri * p.lanes + (q + 1) * p.width)

                            def read(tile):
                                left = col_ri * p.lanes + tile * LANES
                                return acc[rows, left : left + LANES]

                            total = total + sign * taken_slot(p, read, q)
                    keep(place, p.width, total)
                    place += p.width
        rows = []
        for which in range(2):
            sums = gb_ref[which * 8 : (which + 1) * 8, :].sum(0, keepdims=True)
            for ri in range(2):
                for n in range(p.groups):
                    row = jnp.zeros((1, LANES), single)
                    for s in range(p.stack):

                        def read(tile):
                            left = ri * p.lanes + tile * LANES
                            return sums[:, left : left + LANES]

                        row = row + taken_slot(p, read, s * p.groups + n)
                    rows.append(row)
        rows += [jnp.zeros((1, LANES), single)] * (-len(rows) % 8)
        keep(place, len(rows), jnp.concatenate(rows, axis=0))


def mixed_kernel(p, rows_ref, table_ref, out_ref, words_ref):
    factor = 1.0 / math.sqrt(p.lon)

    for h in range(p.step):
        block = rows_ref[:, 0, 0, h].reshape(2 * MW, p.lanes)
        tokens = mul(table_ref[...], block) * factor
        scatter_row(p, tokens, words_ref.at[h], out_ref, h)


def slope_sums_kernel(p, follows, *refs):
    stat_refs = refs[: p.chan]
    rows_in_ref, tokens_ref, affine_ref, table_ref, wide_ref, sum_ref = refs[p.chan : p.chan + 6]
    refs = refs[p.chan + 6 :]
    before_ref, refs = (refs[0], refs[1:]) if follows else (None, refs)
    sums_ref, total_ref, param_ref, rows_ref, dense_ref = refs
    factor = 1.0 / math.sqrt(p.lon)
    count = 2 * p.stack
    moments(p, stat_refs, rows_ref)

    @pl.when(first_step())
    def _():
        param_ref[...] = jnp.zeros_like(param_ref)

    for h in range(p.step):
        block = rows_in_ref[:, 0, 0, h].reshape(2 * MW, p.lanes)
        folds = (PACK * p.turn_pad // 8, 8, LANES)
        plain, scaled = [], []
        spectrum = mul(table_ref[...], block)
        for c, (mean, inverse) in enumerate(expand(p, rows_ref[h], wide_ref)):
            at = slice(c * LANES, (c + 1) * LANES)
            normed_grad = spectrum[:, at] * factor
            centred = (tokens_ref[0, h, :, at].astype(single) - mean) * inverse
            param_ref[0:8, at] += (normed_grad * centred).reshape(folds).sum(0)
            param_ref[8:16, at] += normed_grad.reshape(folds).sum(0)
            grad = normed_grad * affine_ref[0:1, at]
            plain.append(grad.astype(half))
            scaled.append((grad * centred).astype(half))
        sums = mul(sum_ref[0], jnp.concatenate(plain, axis=1), NT) + mul(
            sum_ref[1], jnp.concatenate(scaled, axis=1), NT
        )
        dense_ref[h * count : (h + 1) * count, :] = sums[:count]
    sums_ref[0] = dense_ref[...].astype(half)

    @pl.when(last_step())
    def _():
        for kind in range(2):
            at = slice(kind, kind + 1)
            total = param_ref[8 * kind : 8 * kind + 8, :].sum(0, keepdims=True)
            if before_ref is not None:
                total = total + before_ref[0, at, :]
            for d in range(p.space):
                total_ref[d, at, :] = total


def input_grad_kernel(p, *refs):
    stat_refs, part_refs = refs[: p.chan], refs[p.chan : 2 * p.chan]
    rows_in_ref, tokens_ref, affine_ref, table_ref, wide_ref = refs[2 * p.chan : 2 * p.chan + 5]
    out_ref, rows_ref, part_ref, words_ref = refs[2 * p.chan + 5 :]
    factor = 1.0 / math.sqrt(p.lon)
    count = 2 * p.stack
    moments(p, stat_refs, rows_ref)
    total = part_refs[0][0].astype(single)
    for ref in part_refs[1:]:
        total = total + ref[0].astype(single)
    for h in range(p.step):
        part_ref[h, :count, :] = total[h * count : (h + 1) * count] * (1.0 / p.channels)
        if count < 8:
            part_ref[h, count:, :] = jnp.zeros((8 - count, p.turn_pad * PACK), single)

    for h in range(p.step):
        block = rows_in_ref[:, 0, 0, h].reshape(2 * MW, p.lanes)
        spectrum = mul(table_ref[...], block)
        moment = expand(p, rows_ref[h], wide_ref)
        means = expand(p, part_ref[h], wide_ref)
        tiles = []
        for c in range(p.tiles):
            at = slice(c * LANES, (c + 1) * LANES)
            (mean, inverse), (first, second) = moment[c], means[c]
            centred = (tokens_ref[0, h, :, at].astype(single) - mean) * inverse
            grad = spectrum[:, at] * factor * affine_ref[0:1, at]
            tiles.append(inverse * (grad - first - centred * second))
        grad = jnp.concatenate(tiles, axis=1)
        scatter_row(p, grad, words_ref.at[h], out_ref, h)


def whole_spec(value):
    dims = value.shape
    return pl.BlockSpec(dims, lambda *_: (0,) * len(dims))


def part_spec(p, value):
    dims = (1, value.shape[1] // p.steps) + value.shape[2:]
    return pl.BlockSpec(dims, lambda b, r: (b, r) + (0,) * (len(dims) - 2))


def peer_spec(value, which=0, wide=1):
    dims = (value.shape[0], wide, 1) + value.shape[3:]
    return pl.BlockSpec(dims, lambda b, *_: (0, which, b) + (0,) * (len(dims) - 3))


def peer_part_spec(p, value, which=0):
    dims = (value.shape[0], 1, 1, value.shape[3] // p.steps) + value.shape[4:]
    return pl.BlockSpec(dims, lambda b, r: (0, which, b, r) + (0,) * (len(dims) - 4))


def stored_spec(p, offset):
    return pl.BlockSpec((p.stack, p.step, p.groups, p.long), lambda b, r: (b + offset, r, 0, 0))


def call(body, grid, ins, in_specs, outs, out_specs, scratch, flops, aliases=None):
    moved = sum(v.size * v.dtype.itemsize for v in ins) + sum(
        math.prod(o.shape) * o.dtype.itemsize for o in outs
    )
    return _call(body, grid, ins, in_specs, outs, out_specs, scratch, flops, moved, aliases)


def _call(body, grid, ins, in_specs, outs, out_specs, scratch, flops, moved, aliases):
    return pl.pallas_call(
        body,
        grid=grid,
        in_specs=in_specs,
        out_specs=out_specs,
        out_shape=outs,
        scratch_shapes=scratch,
        input_output_aliases=aliases or {},
        compiler_params=pltpu.CompilerParams(vmem_limit_bytes=VMEM_LIMIT),
        cost_estimate=pl.CostEstimate(flops=flops, bytes_accessed=moved, transcendentals=0),
    )(*ins)


def lon_tables(p):
    cos_lon, sin_lon = trig(p.lon, MW)
    wave = np.concatenate([cos_lon, -sin_lon], axis=1)
    turned = np.zeros((PACK, p.turn_pad, 2 * MW), np.float32)
    turned[:, : p.turn] = wave.reshape(p.turn, PACK, 2 * MW).transpose(1, 0, 2)
    turned = turned.reshape(PACK * p.turn_pad, 2 * MW)
    doubling = np.where(np.arange(MW) == 0, 1.0, 2.0).astype(np.float32)
    factor = np.float32(1.0 / math.sqrt(p.lon))
    plain_scale = np.full((2 * MW, 1), factor, np.float32)
    double_scale = (factor * np.tile(doubling, 2))[:, None].astype(np.float32)
    owner = turned.reshape(-1, 2, p.space, p.modes).transpose(0, 2, 1, 3).reshape(-1, 2 * MW)
    twice = np.tile(doubling.reshape(p.space, 1, p.modes), (1, 2, 1)).reshape(1, 2 * MW)
    to_half = lambda value: jnp.asarray(value, half)
    return (
        to_half(turned.T),
        jnp.asarray(plain_scale),
        jnp.asarray(double_scale),
        to_half(owner * twice),
        to_half(owner),
    )


def lat_tables(p):
    cos_lat, sin_lat = trig(p.lat, p.lat)
    there = np.block([[cos_lat, sin_lat], [-sin_lat, cos_lat]])
    there = there.reshape(2 * p.lat, 2, p.space, p.rows).transpose(0, 2, 1, 3)
    back = np.block([[cos_lat.T, -sin_lat.T], [sin_lat.T, cos_lat.T]])
    return jnp.asarray(there.reshape(2 * p.lat, 2 * p.lat), half), jnp.asarray(back, half)


def sum_tables(p):
    owner = np.arange(PACK) // p.groups
    lane_owner = np.repeat(owner, p.width)
    sums = np.zeros((2, 8, p.lanes), np.float32)
    wide = np.zeros((3, 8, 2, p.lanes), np.float32)
    for s in range(p.stack):
        sums[0, s] = lane_owner == s
        sums[1, p.stack + s] = lane_owner == s
        wide[:, s, 0] = lane_owner == s
        wide[:, p.stack + s, 1] = lane_owner == s
    wide = wide.reshape(24, 2, p.tiles, LANES).transpose(0, 2, 1, 3)
    return jnp.asarray(sums, half), jnp.asarray(wide.reshape(24, 2 * p.lanes), half)


def exchange(value):
    return lax.all_to_all(value, "space", 0, 0, tiled=True)


def around(value, axis, size):
    gathered = [value]
    for step in range(1, size):
        gathered.append(
            lax.ppermute(value, axis, [(i, (i + step) % size) for i in range(size)])
        )
    return gathered


def reduced(p, value, kind):
    step = 1
    while step < p.space:
        own = value.astype(kind)
        other = lax.ppermute(own, "space", [(i, i ^ step) for i in range(p.space)])
        value = own.astype(single) + other.astype(single)
        step *= 2
    return value


def on_device(space, chan, members, gain, shift, w_first, b_first, w_second, b_second, cotangent):
    p = Plan(members, w_first.shape[-1], space, chan)
    size = p.packs // 2
    grid = (size, p.steps)
    table, plain_scale, double_scale, mixed_table, slope_table = lon_tables(p)
    there_table, back_table = lat_tables(p)
    sum_table, wide_table = sum_tables(p)
    affine = jnp.concatenate([gain] * p.stack + [shift] * p.stack).reshape(2, p.lanes)
    tokens_rows = PACK * p.turn_pad
    dft_flops = 2 * size * p.rows * tokens_rows * 2 * MW * p.lanes
    words = pltpu.VMEM((p.step, PACK, p.word_pad, LANES), single)
    lines = pltpu.VMEM((p.step, p.stack, p.word_pad * p.groups, LANES), single)
    turn_in = pltpu.VMEM((p.tiles, MW * 2 * p.rows, LANES), single)
    rows_scratch = pltpu.VMEM((p.step, 8, tokens_rows), single)

    def sent(wide):
        return jax.ShapeDtypeStruct((space, wide, size, p.modes, 2 * p.rows, p.lanes), half)

    def returned(wide):
        return jax.ShapeDtypeStruct((space, wide, size, p.rows, 2 * p.modes, p.lanes), half)

    count = 2 * p.stack * p.rows
    stored = jax.ShapeDtypeStruct(members.shape, half)

    def out_call(body, ins, specs, out, out_spec, scratch, flops, before):
        ins, specs = list(ins), list(specs)
        aliases = {}
        inner = body
        if before is not None:
            place = len(ins)
            inner = lambda *refs: body(*refs[:place], *refs[place + 1 :])
            ins.append(before)
            specs.append(pl.BlockSpec(memory_space=pl.ANY))
            aliases = {place: 0}
        return call(inner, grid, tuple(ins), specs, [out], [out_spec], scratch, flops, aliases)[0]

    def cotangent_chunk(c, wide):
        return out_call(
            functools.partial(cotangent_kernel, p), (cotangent, table, double_scale),
            [stored_spec(p, c * size), whole_spec(table), whole_spec(double_scale)],
            sent(wide), peer_spec(sent(wide)), [words, turn_in], dft_flops, None,
        )

    def stats_chunk(c):
        ins = (members, sum_table)
        outs = [
            jax.ShapeDtypeStruct((size, p.rows, tokens_rows, p.lanes), half),
            jax.ShapeDtypeStruct((size, count, tokens_rows), single),
        ]
        return call(
            functools.partial(stats_kernel, p), grid, ins,
            [stored_spec(p, c * size), whole_spec(sum_table)],
            outs, [part_spec(p, o) for o in outs], [words], dft_flops // 4,
        )

    def normalise_chunk(stats, tokens, before):
        tail = (affine, table, plain_scale, wide_table)
        out = sent(1 if before is None else 2)
        return out_call(
            functools.partial(normalise_kernel, p), (*stats, tokens, *tail),
            [part_spec(p, s) for s in (*stats, tokens)] + [whole_spec(v) for v in tail],
            out, peer_spec(out, out.shape[1] - 1), [rows_scratch, turn_in], dft_flops, before,
        )

    step_modes = 2 if p.modes % 2 == 0 else 1
    wide_lanes = 2 * p.lanes

    def spectral_chunk(x_in, x_which, g_in, before):
        joined = before is None
        tail = (there_table, back_table, w_first, w_second, b_first, b_second)
        tail += () if joined else (before,)

        def mode_spec(which):
            return pl.BlockSpec(
                (space, 1, 1, step_modes, 2 * p.rows, p.lanes),
                lambda b, m: (0, which, b, m, 0, 0),
            )

        outs = [returned(2)] if joined else [returned(1), returned(1)]
        out_specs = [peer_spec(o, 0, o.shape[1]) for o in outs]
        bias_rows = -(-4 * p.groups // 8) * 8
        totals = jax.ShapeDtypeStruct(
            (4 * p.groups * p.width + bias_rows, LANES), single if joined else half
        )
        kept = pltpu.VMEM((p.modes * p.lat, wide_lanes), half)
        held = pltpu.VMEM((step_modes * p.lat, wide_lanes), single)
        brief = pltpu.VMEM((step_modes * p.lat, wide_lanes), half)
        turn_out = pltpu.VMEM((p.tiles, p.lat * 2 * p.modes, LANES), single)
        return call(
            functools.partial(spectral_kernel, p, step_modes, joined),
            (size, p.modes // step_modes), (x_in, g_in, *tail),
            [mode_spec(x_which), mode_spec(0)] + [whole_spec(v) for v in tail],
            [*outs, totals],
            [*out_specs, whole_spec(totals)],
            [pltpu.VMEM((16, wide_lanes), single), pltpu.VMEM((2, wide_lanes), single)]
            + [kept] * 4 + [held] + [brief] * 3 + [turn_out] * 2
            + [pltpu.VMEM((wide_lanes, wide_lanes), single)] * 2
            + [pltpu.VMEM((wide_lanes, wide_lanes), half)] * 2,
            12 * size * p.modes * p.lat * wide_lanes * wide_lanes,
        )

    def mixed_chunk(c, rows_in, which, before):
        return out_call(
            functools.partial(mixed_kernel, p), (rows_in, mixed_table),
            [peer_part_spec(p, rows_in, which), whole_spec(mixed_table)], stored, stored_spec(p, c * size),
            [lines], dft_flops, before,
        )

    def slope_sums_chunk(stats, rows_in, which, tokens, before):
        tail = (affine, slope_table, wide_table, sum_table)
        tail += () if before is None else (before,)
        outs = [
            jax.ShapeDtypeStruct((size, count, tokens_rows), half),
            jax.ShapeDtypeStruct((space, 2, p.lanes), single),
        ]
        return call(
            functools.partial(slope_sums_kernel, p, before is not None), grid,
            (*stats, rows_in, tokens, *tail),
            [part_spec(p, s) for s in stats]
            + [peer_part_spec(p, rows_in, which), part_spec(p, tokens)]
            + [whole_spec(v) for v in tail],
            outs, [part_spec(p, outs[0]), whole_spec(outs[1])],
            [
                pltpu.VMEM((16, p.lanes), single), rows_scratch,
                pltpu.VMEM((count // p.steps, tokens_rows), single),
            ],
            dft_flops,
        )

    def input_grad_chunk(c, stats, parts, rows_in, which, tokens, before):
        tail = (affine, slope_table, wide_table)
        return out_call(
            functools.partial(input_grad_kernel, p),
            (*stats, *parts, rows_in, tokens, *tail),
            [part_spec(p, s) for s in (*stats, *parts)]
            + [peer_part_spec(p, rows_in, which), part_spec(p, tokens)]
            + [whole_spec(v) for v in tail],
            stored, stored_spec(p, c * size), [rows_scratch, rows_scratch, lines], dft_flops,
            before,
        )

    def channel_sums(value):
        return around(value, "chan", chan)

    g0 = exchange(cotangent_chunk(0, 1))
    tokens0, sums = stats_chunk(0)
    stats0 = channel_sums(sums)
    x0 = exchange(normalise_chunk(stats0, tokens0, None))
    both1 = cotangent_chunk(1, 2)
    tokens1, sums = stats_chunk(1)
    stats1 = channel_sums(sums)
    both1 = exchange(normalise_chunk(stats1, tokens1, both1))
    out0, totals = spectral_chunk(x0, 0, g0, None)
    rows0 = exchange(out0)
    y1, dx1, totals = spectral_chunk(both1, 1, both1, totals)
    dx1 = exchange(dx1)
    y1 = exchange(y1)
    sums, params = slope_sums_chunk(stats0, rows0, 1, tokens0, None)
    parts = channel_sums(sums)
    grad_input = input_grad_chunk(0, stats0, parts, rows0, 1, tokens0, None)
    mixed = mixed_chunk(0, rows0, 0, None)
    sums, params = slope_sums_chunk(stats1, dx1, 0, tokens1, params)
    parts = channel_sums(sums)
    grad_input = input_grad_chunk(1, stats1, parts, dx1, 0, tokens1, grad_input)
    mixed = mixed_chunk(1, y1, 0, mixed)
    size_w = p.groups * p.width
    flat = reduced(p, totals, half)[:, : p.width]
    grads = flat[: 4 * size_w].reshape((2,) + w_first.shape)
    bias_grads = flat[4 * size_w : 4 * size_w + 4 * p.groups].reshape((2,) + b_first.shape)
    params = exchange(params).sum(0)
    params = [
        sum(params[kind, s * size_w : (s + 1) * size_w] for s in range(p.stack)) for kind in range(2)
    ]
    return (
        mixed, grad_input, grads[0], bias_grads[0], grads[1], bias_grads[1], params[0], params[1]
    )


def solution(mesh):
    tokens = P(None, "space", "chan", None)
    weights = P(None, "chan", None, None)
    biases = P(None, "chan", None)
    placed = (tokens, P("chan"), P("chan"), weights, biases, weights, biases, tokens)
    return jax.shard_map(
        functools.partial(on_device, mesh.shape["space"], mesh.shape["chan"]),
        mesh=mesh,
        in_specs=placed,
        out_specs=(tokens, tokens, weights, biases, weights, biases, P("chan"), P("chan")),
        check_vma=False,
    )
```

```python
import functools
import math

import jax
import jax.numpy as jnp
import numpy as np
from jax import lax
from jax.experimental import pallas as pl
from jax.experimental.pallas import tpu as pltpu
from jax.sharding import PartitionSpec as P


MW = 64
LANES = 128
PACK = 4

shrink_level = 0.05
norm_epsilon = 1e-05
gelu_scale = 0.7978845608
gelu_cubic = 0.044715

half = jnp.bfloat16
single = jnp.float32
VMEM_LIMIT = 67043328
SLOTS = 4

TN = (((0,), (0,)), ((), ()))
NT = (((1,), (1,)), ((), ()))


def mul(first_op, second_op, dims=(((1,), (0,)), ((), ()))):
    return lax.dot_general(first_op, second_op, dims, preferred_element_type=single)


def trig(length, columns):
    angles = (np.arange(length)[:, None] * np.arange(columns)[None, :] % length).astype(np.float32)
    angles = (angles * np.float32(2.0 * math.pi / length)).astype(np.float64)
    cast = lambda table: table.astype(np.float32).astype(half).astype(np.float32)
    return cast(np.cos(angles)), cast(np.sin(angles))


class Plan:
    def __init__(self, members, width, space, chan):
        self.batch, self.rows, self.groups, self.long = members.shape
        self.width, self.space, self.chan = width, space, chan
        self.lon = self.long // width
        self.lat = self.rows * space
        self.modes = MW // space
        self.stack = PACK // self.groups
        self.packs = self.batch // self.stack
        self.lanes = PACK * width
        self.tiles = self.lanes // LANES
        self.turn = self.lon // PACK
        self.turn_pad = -(-self.turn // 16) * 16
        self.words = self.long // LANES
        self.step = SLOTS if self.rows % SLOTS == 0 else self.rows
        self.steps = self.rows // self.step
        self.word_pad = self.tiles * self.turn_pad
        self.channels = self.groups * width * chan


def moved_lanes(p, fetch, from_start, to_start, tile):
    pieces = []
    for slot in range(PACK):
        low = max(to_start(slot), tile * LANES)
        high = min(to_start(slot) + p.width, (tile + 1) * LANES)
        at = low
        while at < high:
            source = at - to_start(slot) + from_start(slot)
            stop = min(high, at + LANES - source % LANES)
            shift = (at - source) % LANES
            pieces.append((stop - tile * LANES, fetch(slot, source // LANES, shift)))
            at = stop
    return pieces


def merged(pieces, lane):
    value = pieces[-1][1]
    for stop, piece in reversed(pieces[:-1]):
        value = jnp.where(lane < stop, piece, value)
    return value


def rolled(value, shift):
    return value if shift == 0 else pltpu.roll(value, shift, 1)


def spread(p, stored_ref, words_ref, h):
    for q in range(PACK):
        line = stored_ref[q // p.groups, h, q % p.groups, :]
        words_ref[q, : p.words, :] = line.reshape(p.words, LANES).astype(single)


def gather_row(p, words_ref):
    lane = lax.broadcasted_iota(jnp.int32, (p.turn_pad, LANES), 1)
    source = {}
    for q in range(PACK):
        for i in range(p.tiles):
            source[q, i] = words_ref[q, pl.ds(i, p.turn_pad, stride=p.tiles), :]
    rows = []
    for r in range(PACK):
        cache = {}

        def fetch(q, i, shift):
            key = (q, i, shift)
            if key not in cache:
                cache[key] = rolled(source[q, i], shift)
            return cache[key]

        tiles = []
        for c in range(p.tiles):
            pieces = moved_lanes(p, fetch, lambda q: r * p.width, lambda q: q * p.width, c)
            tiles.append(merged(pieces, lane).astype(half))
        rows.append(jnp.concatenate(tiles, axis=1))
    return jnp.concatenate(rows, axis=0)


def scatter_row(p, tokens, words_ref, stored_ref, h):
    lane = lax.broadcasted_iota(jnp.int32, (p.turn_pad, LANES), 1)
    for q in range(PACK):
        s, n = divmod(q, p.groups)
        cache = {}

        def fetch(r, c, shift):
            if (r, c, shift) not in cache:
                part = tokens[r * p.turn_pad : (r + 1) * p.turn_pad, c * LANES : (c + 1) * LANES]
                cache[r, c, shift] = rolled(part, shift)
            return cache[r, c, shift]

        for i in range(p.tiles):
            pieces = moved_lanes(p, fetch, lambda r: q * p.width, lambda r: r * p.width, i)
            at = pl.ds(i * p.groups + n, p.turn_pad, stride=p.tiles * p.groups)
            words_ref[s, at, :] = merged(pieces, lane)
    for s in range(p.stack):
        lines = words_ref[s, : p.words * p.groups, :].astype(half)
        for t in range(p.words):
            stored_ref[s, h, :, t * LANES : (t + 1) * LANES] = lines[
                t * p.groups : (t + 1) * p.groups, :
            ]


def clear_tail(p, words_ref):
    @pl.when(first_step())
    def _():
        tail = p.word_pad - p.words
        words_ref[:, :, p.words :, :] = jnp.zeros(words_ref.shape[:2] + (tail, LANES), single)


def first_step():
    return (pl.program_id(0) == 0) & (pl.program_id(1) == 0)


def last_step():
    return (pl.program_id(0) == pl.num_programs(0) - 1) & (
        pl.program_id(1) == pl.num_programs(1) - 1
    )


def last_part():
    return pl.program_id(1) == pl.num_programs(1) - 1


def analyse(p, tokens, table, scale, turn_ref, h):
    h = pl.program_id(1) * p.step + h
    spectrum = mul(table, tokens) * scale
    for c in range(p.tiles):
        for ri in range(2):
            turn_ref[c, pl.ds(ri * p.rows + h, MW, stride=2 * p.rows), :] = spectrum[
                ri * MW : (ri + 1) * MW, c * LANES : (c + 1) * LANES
            ]


def send_turn(p, turn_ref, out_refs, outer, inner, which=0, me=None):
    count = outer * inner
    for x in range(p.space):
        for c in range(p.tiles):
            lanes = slice(c * LANES, (c + 1) * LANES)
            if me is None:
                part = turn_ref[c, x * count : (x + 1) * count, :]
                out_refs[0][x, which, 0, :, :, lanes] = part.reshape(outer, inner, LANES).astype(half)
            else:
                at = pl.ds(pl.multiple_of((me ^ x) * count, 8), count)
                part = turn_ref[c, at, :]
                out_refs[x][which, 0, :, :, lanes] = part.reshape(outer, inner, LANES).astype(half)


def peer_rows(p, refs, i):
    if len(refs) == 1:
        return refs[0][:, 0, 0, i].reshape(-1, p.lanes)
    return jnp.concatenate([ref[0, 0, i] for ref in refs], axis=0)


def split_three(value):
    high = value.astype(half).astype(single)
    rest = value - high
    middle = rest.astype(half).astype(single)
    return high, middle, rest - middle


def expand(p, parts, wide_ref):
    stacked = jnp.concatenate(split_three(parts), axis=0).astype(half)
    pairs = []
    for c in range(p.tiles):
        both = mul(stacked, wide_ref[:, 2 * c * LANES : 2 * (c + 1) * LANES], TN)
        pairs.append((both[:, :LANES], both[:, LANES:]))
    return pairs


def summed(table, value):
    high = value.astype(half)
    low = (value - high.astype(single)).astype(half)
    return mul(table, high, NT) + mul(table, low, NT)


def cotangent_kernel(p, split, stored_ref, table_ref, scale_ref, *refs):
    me, refs = (refs[0][0], refs[1:]) if split else (None, refs)
    out_refs, (words_ref, turn_ref) = refs[:-2], refs[-2:]
    clear_tail(p, words_ref)
    for h in range(p.step):
        spread(p, stored_ref, words_ref.at[h], h)
        tokens = gather_row(p, words_ref.at[h])
        analyse(p, tokens, table_ref[...], scale_ref[...], turn_ref, h)

    @pl.when(last_part())
    def _():
        send_turn(p, turn_ref, out_refs, p.modes, 2 * p.rows, 0, me)


def stats_kernel(p, stored_ref, sum_ref, tokens_ref, stat_ref, words_ref):
    clear_tail(p, words_ref)
    count = 2 * p.stack
    for h in range(p.step):
        spread(p, stored_ref, words_ref.at[h], h)
        tokens = gather_row(p, words_ref.at[h])
        tokens_ref[0, h] = tokens
        wide = tokens.astype(single)
        rows = mul(sum_ref[0], tokens, NT) + summed(sum_ref[1], wide * wide)
        stat_ref[0, h * count : (h + 1) * count, :] = rows[:count]


def moments(p, stat_refs, rows_ref):
    count = 2 * p.stack
    total = stat_refs[0][0]
    for ref in stat_refs[1:]:
        total = total + ref[0]
    for h in range(p.step):
        part = total[h * count : (h + 1) * count] * (1.0 / p.channels)
        mean, square = part[: p.stack], part[p.stack :]
        inverse = lax.rsqrt(square - mean * mean + norm_epsilon)
        rows_ref[h, : p.stack, :] = mean
        rows_ref[h, p.stack : count, :] = inverse
        if count < 8:
            rows_ref[h, count:, :] = jnp.zeros((8 - count, p.turn_pad * PACK), single)


def normalise_kernel(p, split, *refs):
    stat_refs = refs[: p.chan]
    tokens_ref, affine_ref, table_ref, scale_ref, wide_ref = refs[p.chan : p.chan + 5]
    refs = refs[p.chan + 5 :]
    me, refs = (refs[0][0], refs[1:]) if split else (None, refs)
    out_refs, (rows_ref, turn_ref) = refs[:-2], refs[-2:]
    moments(p, stat_refs, rows_ref)

    for h in range(p.step):
        tiles = []
        for c, (mean, inverse) in enumerate(expand(p, rows_ref[h], wide_ref)):
            at = slice(c * LANES, (c + 1) * LANES)
            centred = (tokens_ref[0, h, :, at].astype(single) - mean) * inverse
            tiles.append((centred * affine_ref[0:1, at] + affine_ref[1:2, at]).astype(half))
        normed = jnp.concatenate(tiles, axis=1)
        analyse(p, normed, table_ref[...], scale_ref[...], turn_ref, h)

    @pl.when(last_part())
    def _():
        send_turn(p, turn_ref, out_refs, p.modes, 2 * p.rows, 0, me)


def gelu_both(values):
    square = values * values
    inner = jnp.tanh(values * (gelu_scale + gelu_scale * gelu_cubic * square))
    upper = 0.5 + 0.5 * inner
    hidden = values * upper
    slope = upper + hidden * (1.0 - upper) * (
        2.0 * gelu_scale + 6.0 * gelu_scale * gelu_cubic * square
    )
    return hidden, slope


BAND = 32
COLUMNS = 256


def widened(p, value):
    blank = jnp.zeros((value.shape[0], LANES - p.width), single)
    return jnp.concatenate([value.astype(single), blank], axis=1)


def placed_slot(p, value, q):
    lane = lax.broadcasted_iota(jnp.int32, value.shape, 1)
    at, shift = divmod(q * p.width, LANES)
    turned = rolled(value, shift)
    tiles = [jnp.zeros_like(value) for _ in range(p.tiles)]
    tiles[at] = jnp.where(lane >= shift, turned, 0.0)
    if shift + p.width > LANES:
        tiles[at + 1] = jnp.where(lane < shift + p.width - LANES, turned, 0.0)
    return jnp.concatenate(tiles, axis=1)


def taken_slot(p, read, q):
    at, shift = divmod(q * p.width, LANES)
    value = rolled(read(at), -shift % LANES)
    if shift + p.width > LANES:
        lane = lax.broadcasted_iota(jnp.int32, value.shape, 1)
        value = jnp.where(lane < LANES - shift, value, rolled(read(at + 1), -shift % LANES))
    return value


PARTS = (((0, 0, 1), (1, 1, 1)), ((0, 1, 1), (1, 0, -1)))


def place_weights(p, w_refs, out_refs):
    for w_ref, out_ref in zip(w_refs, out_refs):
        for q in range(PACK):
            for part in range(2):
                wide = placed_slot(p, widened(p, w_ref[part, q % p.groups]), q)
                for row_ri, col_ri, sign in PARTS[part]:
                    top = row_ri * p.lanes + q * p.width
                    out_ref[top : top + p.width, col_ri * p.lanes : (col_ri + 1) * p.lanes] = (
                        sign * wide
                    ).astype(half)


def place_biases(p, b_refs, out_ref):
    for which, b_ref in enumerate(b_refs):
        for ri in range(2):
            row = jnp.zeros((1, p.lanes), single)
            for q in range(PACK):
                n = q % p.groups
                row = row + placed_slot(p, widened(p, b_ref[ri, n : n + 1, :]), q)
            out_ref[which : which + 1, ri * p.lanes : (ri + 1) * p.lanes] = row


def spectral_kernel(p, step_modes, peers, split, joined, *refs):
    x_refs, g_refs, refs = refs[:peers], refs[peers : 2 * peers], refs[2 * peers :]
    there_ref, back_ref, w_first_ref, w_second_ref, b_first_ref, b_second_ref = refs[:6]
    refs = refs[6:]
    me, before_ref = None, None
    if not joined:
        before_ref, refs = refs[0], refs[1:]
    if split:
        me, refs = refs[0][0], refs[1:]
    y_refs, refs = refs[:1], refs[1:]
    x_out_refs = y_refs
    if not joined:
        x_outs = p.space if split else 1
        x_out_refs, refs = refs[:x_outs], refs[x_outs:]
    (
        total_ref,
        gb_ref,
        bias_ref,
        lat_ref,
        hid_ref,
        gpost_ref,
        gpre_ref,
        slope_ref,
        gsh_ref,
        shr_ref,
        glat_ref,
        turn_y_ref,
        turn_x_ref,
        acc1_ref,
        acc2_ref,
        w1_ref,
        w2_ref,
    ) = refs
    pack, group = pl.program_id(0), pl.program_id(1)
    count = step_modes * p.lat
    factor = 1.0 / math.sqrt(p.lat)
    base = pl.multiple_of(group * count, count)

    @pl.when((pack == 0) & (group == 0))
    def _():
        place_weights(p, (w_first_ref, w_second_ref), (w1_ref, w2_ref))
        place_biases(p, (b_first_ref, b_second_ref), bias_ref)
        gb_ref[...] = jnp.zeros_like(gb_ref)
        acc1_ref[...] = jnp.zeros_like(acc1_ref)
        acc2_ref[...] = jnp.zeros_like(acc2_ref)

    def there(refs, into, offset):
        for m in range(step_modes):
            block = peer_rows(p, refs, m)
            out = (mul(there_ref[...], block) * factor).astype(half)
            at = pl.ds(offset + m * p.lat, p.lat)
            into[at, : p.lanes] = out[: p.lat]
            into[at, p.lanes :] = out[p.lat :]

    def back(value_of, turn_ref):
        for m in range(step_modes):
            rows = slice(m * p.lat, (m + 1) * p.lat)
            both = jnp.concatenate([value_of(rows, 0), value_of(rows, 1)], axis=0)
            out = mul(back_ref[...], both) * factor
            mode = group * step_modes + m
            for ri in range(2):
                for c in range(p.tiles):
                    turn_ref[c, pl.ds(ri * p.modes + mode, p.lat, stride=2 * p.modes), :] = out[
                        ri * p.lat : (ri + 1) * p.lat, c * LANES : (c + 1) * LANES
                    ]

    def bands(columns, body):
        for low in range(0, count, BAND):
            at = slice(low, low + BAND)
            body(at, pl.ds(pl.multiple_of(base + low, BAND), BAND), columns)

    def folded(value):
        return value.reshape(BAND // 8, 8, value.shape[1]).sum(0)

    there(x_refs, lat_ref, base)
    there(g_refs, gsh_ref, 0)
    every = [slice(low, low + COLUMNS) for low in range(0, 2 * p.lanes, COLUMNS)]
    lat = lat_ref[pl.ds(base, count), :]
    for columns in every:
        pre = mul(lat, w1_ref[:, columns])

        def first(at, kept, columns):
            hidden, slope = gelu_both(pre[at] + bias_ref[0:1, columns])
            hid_ref[kept, columns] = hidden.astype(half)
            slope_ref[at, columns] = slope

        bands(columns, first)
    hid = hid_ref[pl.ds(base, count), :]
    for columns in every:
        part = mul(hid, w2_ref[:, columns])
        sums = [jnp.zeros((8, COLUMNS), single)]

        def second(at, kept, columns):
            post = part[at] + bias_ref[1:2, columns]
            inner = jnp.tanh(post * (1.0 / shrink_level))
            shr_ref[at, columns] = (post - shrink_level * inner).astype(half)
            gpost = (gsh_ref[at, columns].astype(single) * (inner * inner)).astype(half)
            gpost_ref[kept, columns] = gpost
            sums[0] += folded(gpost.astype(single))

        bands(columns, second)
        gb_ref[8:16, columns] += sums[0]
    back(lambda rows, ri: shr_ref[rows, ri * p.lanes : (ri + 1) * p.lanes], turn_y_ref)
    gpost = gpost_ref[pl.ds(base, count), :]
    for columns in every:
        part = mul(gpost, w2_ref[columns, :], NT)
        sums = [jnp.zeros((8, COLUMNS), single)]

        def third(at, kept, columns):
            gpre = (part[at] * slope_ref[at, columns]).astype(half)
            gpre_ref[kept, columns] = gpre
            sums[0] += folded(gpre.astype(single))

        bands(columns, third)
        gb_ref[0:8, columns] += sums[0]
    gpre = gpre_ref[pl.ds(base, count), :]
    for columns in every:
        glat_ref[:, columns] = mul(gpre, w1_ref[columns, :], NT).astype(half)
    back(lambda rows, ri: glat_ref[rows, ri * p.lanes : (ri + 1) * p.lanes], turn_x_ref)

    @pl.when(group == pl.num_programs(1) - 1)
    def _():
        send_turn(p, turn_y_ref, y_refs, p.rows, 2 * p.modes)
        send_turn(p, turn_x_ref, x_out_refs, p.rows, 2 * p.modes, 1 if joined else 0, me)
        acc1_ref[...] += mul(lat_ref[...], gpre_ref[...], TN)
        acc2_ref[...] += mul(hid_ref[...], gpost_ref[...], TN)

    @pl.when((group == pl.num_programs(1) - 1) & (pack == pl.num_programs(0) - 1))
    def _():
        def keep(top, rows, value):
            at = slice(top, top + rows)
            if before_ref is not None:
                value = value + before_ref[at, :]
            total_ref[at, :] = value.astype(total_ref.dtype)

        place = 0
        for acc in (acc1_ref, acc2_ref):
            for part in range(2):
                for n in range(p.groups):
                    total = jnp.zeros((p.width, LANES), single)
                    for s in range(p.stack):
                        q = s * p.groups + n
                        for row_ri, col_ri, sign in PARTS[part]:
                            rows = slice(row_ri * p.lanes + q * p.width, row_ri * p.lanes + (q + 1) * p.width)

                            def read(tile):
                                left = col_ri * p.lanes + tile * LANES
                                return acc[rows, left : left + LANES]

                            total = total + sign * taken_slot(p, read, q)
                    keep(place, p.width, total)
                    place += p.width
        rows = []
        for which in range(2):
            sums = gb_ref[which * 8 : (which + 1) * 8, :].sum(0, keepdims=True)
            for ri in range(2):
                for n in range(p.groups):
                    row = jnp.zeros((1, LANES), single)
                    for s in range(p.stack):

                        def read(tile):
                            left = ri * p.lanes + tile * LANES
                            return sums[:, left : left + LANES]

                        row = row + taken_slot(p, read, s * p.groups + n)
                    rows.append(row)
        rows += [jnp.zeros((1, LANES), single)] * (-len(rows) % 8)
        keep(place, len(rows), jnp.concatenate(rows, axis=0))


def mixed_kernel(p, rows_ref, table_ref, out_ref, words_ref):
    factor = 1.0 / math.sqrt(p.lon)

    for h in range(p.step):
        block = peer_rows(p, (rows_ref,), h)
        tokens = mul(table_ref[...], block) * factor
        scatter_row(p, tokens, words_ref.at[h], out_ref, h)


def slope_sums_kernel(p, peers, follows, *refs):
    stat_refs, refs = refs[: p.chan], refs[p.chan :]
    rows_in_refs, refs = refs[:peers], refs[peers:]
    tokens_ref, affine_ref, table_ref, wide_ref, sum_ref = refs[:5]
    refs = refs[5:]
    before_ref, refs = (refs[0], refs[1:]) if follows else (None, refs)
    sums_ref, total_ref, param_ref, rows_ref, dense_ref = refs
    factor = 1.0 / math.sqrt(p.lon)
    count = 2 * p.stack
    moments(p, stat_refs, rows_ref)

    @pl.when(first_step())
    def _():
        param_ref[...] = jnp.zeros_like(param_ref)

    for h in range(p.step):
        block = peer_rows(p, rows_in_refs, h)
        folds = (PACK * p.turn_pad // 8, 8, LANES)
        plain, scaled = [], []
        spectrum = mul(table_ref[...], block)
        for c, (mean, inverse) in enumerate(expand(p, rows_ref[h], wide_ref)):
            at = slice(c * LANES, (c + 1) * LANES)
            normed_grad = spectrum[:, at] * factor
            centred = (tokens_ref[0, h, :, at].astype(single) - mean) * inverse
            param_ref[0:8, at] += (normed_grad * centred).reshape(folds).sum(0)
            param_ref[8:16, at] += normed_grad.reshape(folds).sum(0)
            grad = normed_grad * affine_ref[0:1, at]
            plain.append(grad.astype(half))
            scaled.append((grad * centred).astype(half))
        sums = mul(sum_ref[0], jnp.concatenate(plain, axis=1), NT) + mul(
            sum_ref[1], jnp.concatenate(scaled, axis=1), NT
        )
        dense_ref[h * count : (h + 1) * count, :] = sums[:count]
    sums_ref[0] = dense_ref[...].astype(half)

    @pl.when(last_step())
    def _():
        for kind in range(2):
            at = slice(kind, kind + 1)
            total = param_ref[8 * kind : 8 * kind + 8, :].sum(0, keepdims=True)
            if before_ref is not None:
                total = total + before_ref[0, at, :]
            for d in range(p.space):
                total_ref[d, at, :] = total


def input_grad_kernel(p, peers, *refs):
    stat_refs, part_refs, refs = refs[: p.chan], refs[p.chan : 2 * p.chan], refs[2 * p.chan :]
    rows_in_refs, refs = refs[:peers], refs[peers:]
    tokens_ref, affine_ref, table_ref, wide_ref, out_ref, rows_ref, part_ref, words_ref = refs
    factor = 1.0 / math.sqrt(p.lon)
    count = 2 * p.stack
    moments(p, stat_refs, rows_ref)
    total = part_refs[0][0].astype(single)
    for ref in part_refs[1:]:
        total = total + ref[0].astype(single)
    for h in range(p.step):
        part_ref[h, :count, :] = total[h * count : (h + 1) * count] * (1.0 / p.channels)
        if count < 8:
            part_ref[h, count:, :] = jnp.zeros((8 - count, p.turn_pad * PACK), single)

    for h in range(p.step):
        block = peer_rows(p, rows_in_refs, h)
        spectrum = mul(table_ref[...], block)
        moment = expand(p, rows_ref[h], wide_ref)
        means = expand(p, part_ref[h], wide_ref)
        tiles = []
        for c in range(p.tiles):
            at = slice(c * LANES, (c + 1) * LANES)
            (mean, inverse), (first, second) = moment[c], means[c]
            centred = (tokens_ref[0, h, :, at].astype(single) - mean) * inverse
            grad = spectrum[:, at] * factor * affine_ref[0:1, at]
            tiles.append(inverse * (grad - first - centred * second))
        grad = jnp.concatenate(tiles, axis=1)
        scatter_row(p, grad, words_ref.at[h], out_ref, h)


def whole_spec(value):
    dims = value.shape
    return pl.BlockSpec(dims, lambda *_: (0,) * len(dims))


def part_spec(p, value):
    dims = (1, value.shape[1] // p.steps) + value.shape[2:]
    return pl.BlockSpec(dims, lambda b, r: (b, r) + (0,) * (len(dims) - 2))


def peer_spec(value, which=0, wide=1):
    dims = (value.shape[0], wide, 1) + value.shape[3:]
    return pl.BlockSpec(dims, lambda b, *_: (0, which, b) + (0,) * (len(dims) - 3))


def peer_part_spec(p, value, which=0):
    dims = (value.shape[0], 1, 1, value.shape[3] // p.steps) + value.shape[4:]
    return pl.BlockSpec(dims, lambda b, r: (0, which, b, r) + (0,) * (len(dims) - 4))


def one_peer_spec(value, which=0):
    dims = (1, 1) + value.shape[2:]
    return pl.BlockSpec(dims, lambda b, *_: (which, b) + (0,) * (len(dims) - 2))


def one_peer_part_spec(p, value):
    dims = (1, 1, value.shape[2] // p.steps) + value.shape[3:]
    return pl.BlockSpec(dims, lambda b, r: (0, b, r) + (0,) * (len(dims) - 3))


def stored_spec(p, offset):
    return pl.BlockSpec((p.stack, p.step, p.groups, p.long), lambda b, r: (b + offset, r, 0, 0))


def call(body, grid, ins, in_specs, outs, out_specs, scratch, flops, aliases=None):
    moved = sum(v.size * v.dtype.itemsize for v in ins) + sum(
        math.prod(o.shape) * o.dtype.itemsize for o in outs
    )
    return _call(body, grid, ins, in_specs, outs, out_specs, scratch, flops, moved, aliases)


def _call(body, grid, ins, in_specs, outs, out_specs, scratch, flops, moved, aliases):
    return pl.pallas_call(
        body,
        grid=grid,
        in_specs=in_specs,
        out_specs=out_specs,
        out_shape=outs,
        scratch_shapes=scratch,
        input_output_aliases=aliases or {},
        compiler_params=pltpu.CompilerParams(vmem_limit_bytes=VMEM_LIMIT),
        cost_estimate=pl.CostEstimate(flops=flops, bytes_accessed=moved, transcendentals=0),
    )(*ins)


def lon_tables(p):
    cos_lon, sin_lon = trig(p.lon, MW)
    wave = np.concatenate([cos_lon, -sin_lon], axis=1)
    turned = np.zeros((PACK, p.turn_pad, 2 * MW), np.float32)
    turned[:, : p.turn] = wave.reshape(p.turn, PACK, 2 * MW).transpose(1, 0, 2)
    turned = turned.reshape(PACK * p.turn_pad, 2 * MW)
    doubling = np.where(np.arange(MW) == 0, 1.0, 2.0).astype(np.float32)
    factor = np.float32(1.0 / math.sqrt(p.lon))
    plain_scale = np.full((2 * MW, 1), factor, np.float32)
    double_scale = (factor * np.tile(doubling, 2))[:, None].astype(np.float32)
    owner = turned.reshape(-1, 2, p.space, p.modes).transpose(0, 2, 1, 3).reshape(-1, 2 * MW)
    twice = np.tile(doubling.reshape(p.space, 1, p.modes), (1, 2, 1)).reshape(1, 2 * MW)
    to_half = lambda value: jnp.asarray(value, half)
    return (
        to_half(turned.T),
        jnp.asarray(plain_scale),
        jnp.asarray(double_scale),
        to_half(owner * twice),
        owner,
    )


def by_distance(p, table, inner):
    at = np.arange(p.space * inner, dtype=np.int32)
    source = ((at // inner) ^ lax.axis_index("space").astype(jnp.int32)) * inner + at % inner
    chosen = (at[:, None] == source[None, :]).astype(half)
    return mul(jnp.asarray(table, half), chosen).astype(half)


def lat_tables(p):
    cos_lat, sin_lat = trig(p.lat, p.lat)
    there = np.block([[cos_lat, sin_lat], [-sin_lat, cos_lat]])
    there = there.reshape(2 * p.lat, 2, p.space, p.rows).transpose(0, 2, 1, 3)
    back = np.block([[cos_lat.T, -sin_lat.T], [sin_lat.T, cos_lat.T]])
    return there.reshape(2 * p.lat, 2 * p.lat), jnp.asarray(back, half)


def sum_tables(p):
    owner = np.arange(PACK) // p.groups
    lane_owner = np.repeat(owner, p.width)
    sums = np.zeros((2, 8, p.lanes), np.float32)
    wide = np.zeros((3, 8, 2, p.lanes), np.float32)
    for s in range(p.stack):
        sums[0, s] = lane_owner == s
        sums[1, p.stack + s] = lane_owner == s
        wide[:, s, 0] = lane_owner == s
        wide[:, p.stack + s, 1] = lane_owner == s
    wide = wide.reshape(24, 2, p.tiles, LANES).transpose(0, 2, 1, 3)
    return jnp.asarray(sums, half), jnp.asarray(wide.reshape(24, 2 * p.lanes), half)


def splits(space):
    return (MW // space) % 4 == 0 and space & (space - 1) == 0


def exchange_near(values):
    count = len(values)
    return tuple(
        value if x == 0 else lax.ppermute(value, "space", [(i, i ^ x) for i in range(count)])
        for x, value in enumerate(values)
    )


def exchange(value):
    return lax.all_to_all(value, "space", 0, 0, tiled=True)


def around(value, axis, size):
    gathered = [value]
    for step in range(1, size):
        gathered.append(
            lax.ppermute(value, axis, [(i, (i + step) % size) for i in range(size)])
        )
    return gathered


def reduced(p, value, kind):
    step = 1
    while step < p.space:
        own = value.astype(kind)
        other = lax.ppermute(own, "space", [(i, i ^ step) for i in range(p.space)])
        value = own.astype(single) + other.astype(single)
        step *= 2
    return value


def on_device(space, chan, members, gain, shift, w_first, b_first, w_second, b_second, cotangent):
    p = Plan(members, w_first.shape[-1], space, chan)
    size = p.packs // 2
    grid = (size, p.steps)
    table, plain_scale, double_scale, mixed_table, slope_plain = lon_tables(p)
    there_plain, back_table = lat_tables(p)
    slope_table, there_table = jnp.asarray(slope_plain, half), jnp.asarray(there_plain, half)
    split = splits(space)
    if split:
        slope_near = by_distance(p, slope_plain, 2 * p.modes)
        there_near = by_distance(p, there_plain, 2 * p.rows)
        me = lax.axis_index("space").astype(jnp.int32).reshape(1)
    own_spec = pl.BlockSpec(memory_space=pltpu.SMEM)
    sum_table, wide_table = sum_tables(p)
    affine = jnp.concatenate([gain] * p.stack + [shift] * p.stack).reshape(2, p.lanes)
    tokens_rows = PACK * p.turn_pad
    dft_flops = 2 * size * p.rows * tokens_rows * 2 * MW * p.lanes
    words = pltpu.VMEM((p.step, PACK, p.word_pad, LANES), single)
    lines = pltpu.VMEM((p.step, p.stack, p.word_pad * p.groups, LANES), single)
    turn_in = pltpu.VMEM((p.tiles, MW * 2 * p.rows, LANES), single)
    rows_scratch = pltpu.VMEM((p.step, 8, tokens_rows), single)

    def sent(wide):
        return jax.ShapeDtypeStruct((space, wide, size, p.modes, 2 * p.rows, p.lanes), half)

    def returned(wide):
        return jax.ShapeDtypeStruct((space, wide, size, p.rows, 2 * p.modes, p.lanes), half)

    count = 2 * p.stack * p.rows
    stored = jax.ShapeDtypeStruct(members.shape, half)

    def out_call(body, ins, specs, outs, out_specs, scratch, flops, before):
        ins, specs = list(ins), list(specs)
        aliases = {}
        inner = body
        if before is not None:
            place, extra = len(ins), len(before)
            inner = lambda *refs: body(*refs[:place], *refs[place + extra :])
            ins += before
            specs += [pl.BlockSpec(memory_space=pl.ANY)] * extra
            aliases = {place + k: k for k in range(extra)}
        return call(inner, grid, tuple(ins), specs, outs, out_specs, scratch, flops, aliases)

    def spectra_out(wide, which, near):
        if near:
            one = jax.ShapeDtypeStruct(sent(wide).shape[1:], half)
            return [one] * space, [one_peer_spec(one, which)] * space
        return [sent(wide)], [peer_spec(sent(wide), which)]

    def cotangent_chunk(c, wide, near):
        outs, out_specs = spectra_out(wide, 0, near)
        ins, specs = (cotangent, table, double_scale), [whole_spec(table), whole_spec(double_scale)]
        if near:
            ins, specs = (*ins, me), [*specs, own_spec]
        return out_call(
            functools.partial(cotangent_kernel, p, near), ins,
            [stored_spec(p, c * size), *specs], outs, out_specs, [words, turn_in], dft_flops, None,
        )

    def stats_chunk(c):
        ins = (members, sum_table)
        outs = [
            jax.ShapeDtypeStruct((size, p.rows, tokens_rows, p.lanes), half),
            jax.ShapeDtypeStruct((size, count, tokens_rows), single),
        ]
        return call(
            functools.partial(stats_kernel, p), grid, ins,
            [stored_spec(p, c * size), whole_spec(sum_table)],
            outs, [part_spec(p, o) for o in outs], [words], dft_flops // 4,
        )

    def normalise_chunk(stats, tokens, before, near):
        tail = (affine, table, plain_scale, wide_table)
        ins = (*stats, tokens, *tail)
        specs = [part_spec(p, s) for s in (*stats, tokens)] + [whole_spec(v) for v in tail]
        if near:
            ins, specs = (*ins, me), [*specs, own_spec]
        which = 0 if before is None else 1
        outs, out_specs = spectra_out(which + 1, which, near)
        return out_call(
            functools.partial(normalise_kernel, p, near), ins, specs,
            outs, out_specs, [rows_scratch, turn_in], dft_flops, before,
        )

    step_modes = 2 if p.modes % 2 == 0 else 1
    wide_lanes = 2 * p.lanes

    def spectral_chunk(x_in, x_which, g_in, before, near):
        joined = before is None
        tail = (there_near if near else there_table, back_table)
        tail += (w_first, w_second, b_first, b_second)
        tail += () if joined else (before,)
        specs = [whole_spec(v) for v in tail]
        if near:
            tail, specs = (*tail, me), [*specs, own_spec]

        def mode_spec(which):
            lead = (1, 1) if near else (space, 1, 1)
            at = (which,) if near else (0, which)
            return pl.BlockSpec(
                lead + (step_modes, 2 * p.rows, p.lanes), lambda b, m: at + (b, m, 0, 0)
            )

        peers = len(x_in)
        outs = [returned(2 if joined else 1)]
        out_specs = [peer_spec(o, 0, o.shape[1]) for o in outs]
        if near:
            one = jax.ShapeDtypeStruct(returned(1).shape[1:], half)
            outs, out_specs = outs + [one] * space, out_specs + [one_peer_spec(one)] * space
        elif not joined:
            outs, out_specs = outs * 2, out_specs * 2
        bias_rows = -(-4 * p.groups // 8) * 8
        totals = jax.ShapeDtypeStruct(
            (4 * p.groups * p.width + bias_rows, LANES), single if joined else half
        )
        kept = pltpu.VMEM((p.modes * p.lat, wide_lanes), half)
        held = pltpu.VMEM((step_modes * p.lat, wide_lanes), single)
        brief = pltpu.VMEM((step_modes * p.lat, wide_lanes), half)
        turn_out = pltpu.VMEM((p.tiles, p.lat * 2 * p.modes, LANES), single)
        return call(
            functools.partial(spectral_kernel, p, step_modes, peers, near, joined),
            (size, p.modes // step_modes), (*x_in, *g_in, *tail),
            [mode_spec(x_which)] * peers + [mode_spec(0)] * peers + specs,
            [*outs, totals],
            [*out_specs, whole_spec(totals)],
            [pltpu.VMEM((16, wide_lanes), single), pltpu.VMEM((2, wide_lanes), single)]
            + [kept] * 4 + [held] + [brief] * 3 + [turn_out] * 2
            + [pltpu.VMEM((wide_lanes, wide_lanes), single)] * 2
            + [pltpu.VMEM((wide_lanes, wide_lanes), half)] * 2,
            12 * size * p.modes * p.lat * wide_lanes * wide_lanes,
        )

    def mixed_chunk(c, rows_in, which, before):
        return out_call(
            functools.partial(mixed_kernel, p), (rows_in, mixed_table),
            [peer_part_spec(p, rows_in, which), whole_spec(mixed_table)],
            [stored], [stored_spec(p, c * size)], [lines], dft_flops, before,
        )

    def rows_specs(rows_in, which):
        if len(rows_in) == 1:
            return [peer_part_spec(p, rows_in[0], which)]
        return [one_peer_part_spec(p, value) for value in rows_in]

    def slope_sums_chunk(stats, rows_in, which, tokens, before):
        near = len(rows_in) > 1
        tail = (affine, slope_near if near else slope_table, wide_table, sum_table)
        tail += () if before is None else (before,)
        outs = [
            jax.ShapeDtypeStruct((size, count, tokens_rows), half),
            jax.ShapeDtypeStruct((space, 2, p.lanes), single),
        ]
        return call(
            functools.partial(slope_sums_kernel, p, len(rows_in), before is not None),
            grid, (*stats, *rows_in, tokens, *tail),
            [part_spec(p, s) for s in stats] + rows_specs(rows_in, which)
            + [part_spec(p, tokens)] + [whole_spec(v) for v in tail],
            outs, [part_spec(p, outs[0]), whole_spec(outs[1])],
            [
                pltpu.VMEM((16, p.lanes), single), rows_scratch,
                pltpu.VMEM((count // p.steps, tokens_rows), single),
            ],
            dft_flops,
        )

    def input_grad_chunk(c, stats, parts, rows_in, which, tokens, before):
        near = len(rows_in) > 1
        tail = (affine, slope_near if near else slope_table, wide_table)
        return out_call(
            functools.partial(input_grad_kernel, p, len(rows_in)),
            (*stats, *parts, *rows_in, tokens, *tail),
            [part_spec(p, s) for s in (*stats, *parts)] + rows_specs(rows_in, which)
            + [part_spec(p, tokens)] + [whole_spec(v) for v in tail],
            [stored], [stored_spec(p, c * size)], [rows_scratch, rows_scratch, lines], dft_flops,
            before,
        )

    def channel_sums(value):
        return around(value, "chan", chan)

    def moved(values, near):
        return exchange_near(values) if near else (exchange(values[0]),)

    g0 = moved(cotangent_chunk(0, 1, False), False)
    tokens0, sums = stats_chunk(0)
    stats0 = channel_sums(sums)
    x0 = moved(normalise_chunk(stats0, tokens0, None, False), False)
    both1 = cotangent_chunk(1, 2, split)
    tokens1, sums = stats_chunk(1)
    stats1 = channel_sums(sums)
    both1 = moved(normalise_chunk(stats1, tokens1, both1, split), split)
    out0, totals = spectral_chunk(x0, 0, g0, None, False)
    rows0 = exchange(out0)
    y1, *dx1, totals = spectral_chunk(both1, 1, both1, totals, split)
    dx1 = moved(dx1, split)
    y1 = exchange(y1)
    sums, params = slope_sums_chunk(stats0, (rows0,), 1, tokens0, None)
    parts = channel_sums(sums)
    grad_input = input_grad_chunk(0, stats0, parts, (rows0,), 1, tokens0, None)
    mixed = mixed_chunk(0, rows0, 0, None)
    sums, params = slope_sums_chunk(stats1, dx1, 0, tokens1, params)
    parts = channel_sums(sums)
    grad_input = input_grad_chunk(1, stats1, parts, dx1, 0, tokens1, grad_input)[0]
    mixed = mixed_chunk(1, y1, 0, mixed)[0]

    size_w = p.groups * p.width
    flat = reduced(p, totals, half)[:, : p.width]
    grads = flat[: 4 * size_w].reshape((2,) + w_first.shape)
    bias_grads = flat[4 * size_w : 4 * size_w + 4 * p.groups].reshape((2,) + b_first.shape)
    params = exchange(params).sum(0)
    params = [
        sum(params[kind, s * size_w : (s + 1) * size_w] for s in range(p.stack)) for kind in range(2)
    ]
    return (
        mixed, grad_input, grads[0], bias_grads[0], grads[1], bias_grads[1], params[0], params[1]
    )


def solution(mesh):
    tokens = P(None, "space", "chan", None)
    weights = P(None, "chan", None, None)
    biases = P(None, "chan", None)
    placed = (tokens, P("chan"), P("chan"), weights, biases, weights, biases, tokens)
    return jax.shard_map(
        functools.partial(on_device, mesh.shape["space"], mesh.shape["chan"]),
        mesh=mesh,
        in_specs=placed,
        out_specs=(tokens, tokens, weights, biases, weights, biases, P("chan"), P("chan")),
        check_vma=False,
    )
```

```python
import functools
import math

import jax
import jax.numpy as jnp
import numpy as np
from jax import lax
from jax.experimental import pallas as pl
from jax.experimental.pallas import tpu as pltpu
from jax.sharding import PartitionSpec as P


MW = 64
LANES = 128
PACK = 4

shrink_level = 0.05
norm_epsilon = 1e-05
gelu_scale = 0.7978845608
gelu_cubic = 0.044715

half = jnp.bfloat16
single = jnp.float32
VMEM_LIMIT = 67043328
SLOTS = 4

TN = (((0,), (0,)), ((), ()))
NT = (((1,), (1,)), ((), ()))


def mul(first_op, second_op, dims=(((1,), (0,)), ((), ()))):
    return lax.dot_general(first_op, second_op, dims, preferred_element_type=single)


def trig(length, columns):
    angles = (np.arange(length)[:, None] * np.arange(columns)[None, :] % length).astype(np.float32)
    angles = (angles * np.float32(2.0 * math.pi / length)).astype(np.float64)
    cast = lambda table: table.astype(np.float32).astype(half).astype(np.float32)
    return cast(np.cos(angles)), cast(np.sin(angles))


class Plan:
    def __init__(self, members, width, space, chan):
        self.batch, self.rows, self.groups, self.long = members.shape
        self.width, self.space, self.chan = width, space, chan
        self.lon = self.long // width
        self.lat = self.rows * space
        self.modes = MW // space
        self.stack = PACK // self.groups
        self.packs = self.batch // self.stack
        self.lanes = PACK * width
        self.tiles = self.lanes // LANES
        self.turn = self.lon // PACK
        self.turn_pad = -(-self.turn // 16) * 16
        self.words = self.long // LANES
        self.step = SLOTS if self.rows % SLOTS == 0 else self.rows
        self.steps = self.rows // self.step
        self.word_pad = self.tiles * self.turn_pad
        self.channels = self.groups * width * chan


def moved_lanes(p, fetch, from_start, to_start, tile):
    pieces = []
    for slot in range(PACK):
        low = max(to_start(slot), tile * LANES)
        high = min(to_start(slot) + p.width, (tile + 1) * LANES)
        at = low
        while at < high:
            source = at - to_start(slot) + from_start(slot)
            stop = min(high, at + LANES - source % LANES)
            shift = (at - source) % LANES
            pieces.append((stop - tile * LANES, fetch(slot, source // LANES, shift)))
            at = stop
    return pieces


def merged(pieces, lane):
    value = pieces[-1][1]
    for stop, piece in reversed(pieces[:-1]):
        value = jnp.where(lane < stop, piece, value)
    return value


def rolled(value, shift):
    return value if shift == 0 else pltpu.roll(value, shift, 1)


def spread(p, stored_ref, words_ref, h):
    for q in range(PACK):
        line = stored_ref[q // p.groups, h, q % p.groups, :]
        words_ref[q, : p.words, :] = line.reshape(p.words, LANES).astype(single)


def gather_row(p, words_ref):
    lane = lax.broadcasted_iota(jnp.int32, (p.turn_pad, LANES), 1)
    source = {}
    for q in range(PACK):
        for i in range(p.tiles):
            source[q, i] = words_ref[q, pl.ds(i, p.turn_pad, stride=p.tiles), :]
    rows = []
    for r in range(PACK):
        cache = {}

        def fetch(q, i, shift):
            key = (q, i, shift)
            if key not in cache:
                cache[key] = rolled(source[q, i], shift)
            return cache[key]

        tiles = []
        for c in range(p.tiles):
            pieces = moved_lanes(p, fetch, lambda q: r * p.width, lambda q: q * p.width, c)
            tiles.append(merged(pieces, lane).astype(half))
        rows.append(jnp.concatenate(tiles, axis=1))
    return jnp.concatenate(rows, axis=0)


def scatter_row(p, tokens, words_ref, stored_ref, h):
    lane = lax.broadcasted_iota(jnp.int32, (p.turn_pad, LANES), 1)
    for q in range(PACK):
        s, n = divmod(q, p.groups)
        cache = {}

        def fetch(r, c, shift):
            if (r, c, shift) not in cache:
                part = tokens[r * p.turn_pad : (r + 1) * p.turn_pad, c * LANES : (c + 1) * LANES]
                cache[r, c, shift] = rolled(part, shift)
            return cache[r, c, shift]

        for i in range(p.tiles):
            pieces = moved_lanes(p, fetch, lambda r: q * p.width, lambda r: r * p.width, i)
            at = pl.ds(i * p.groups + n, p.turn_pad, stride=p.tiles * p.groups)
            words_ref[s, at, :] = merged(pieces, lane)
    for s in range(p.stack):
        lines = words_ref[s, : p.words * p.groups, :].astype(half)
        for t in range(p.words):
            stored_ref[s, h, :, t * LANES : (t + 1) * LANES] = lines[
                t * p.groups : (t + 1) * p.groups, :
            ]


def clear_tail(p, words_ref):
    @pl.when(first_step())
    def _():
        tail = p.word_pad - p.words
        words_ref[:, :, p.words :, :] = jnp.zeros(words_ref.shape[:2] + (tail, LANES), single)


def first_step():
    return (pl.program_id(0) == 0) & (pl.program_id(1) == 0)


def last_step():
    return (pl.program_id(0) == pl.num_programs(0) - 1) & (
        pl.program_id(1) == pl.num_programs(1) - 1
    )


def last_part():
    return pl.program_id(1) == pl.num_programs(1) - 1


def analyse(p, tokens, table, scale, turn_ref, h):
    h = pl.program_id(1) * p.step + h
    spectrum = mul(table, tokens) * scale
    for c in range(p.tiles):
        for ri in range(2):
            turn_ref[c, pl.ds(ri * p.rows + h, MW, stride=2 * p.rows), :] = spectrum[
                ri * MW : (ri + 1) * MW, c * LANES : (c + 1) * LANES
            ]


def send_turn(p, turn_ref, out_refs, outer, inner, which=0, me=None):
    count = outer * inner
    for x in range(p.space):
        for c in range(p.tiles):
            lanes = slice(c * LANES, (c + 1) * LANES)
            if me is None:
                part = turn_ref[c, x * count : (x + 1) * count, :]
                out_refs[0][x, which, 0, :, :, lanes] = part.reshape(outer, inner, LANES).astype(half)
            else:
                at = pl.ds(pl.multiple_of((me ^ x) * count, 8), count)
                part = turn_ref[c, at, :]
                out_refs[x][which, 0, :, :, lanes] = part.reshape(outer, inner, LANES).astype(half)


def peer_rows(p, refs, i):
    if len(refs) == 1:
        return refs[0][:, 0, 0, i].reshape(-1, p.lanes)
    return jnp.concatenate([ref[0, 0, i] for ref in refs], axis=0)


def split_three(value):
    high = value.astype(half).astype(single)
    rest = value - high
    middle = rest.astype(half).astype(single)
    return high, middle, rest - middle


def expand(p, parts, wide_ref):
    stacked = jnp.concatenate(split_three(parts), axis=0).astype(half)
    pairs = []
    for c in range(p.tiles):
        both = mul(stacked, wide_ref[:, 2 * c * LANES : 2 * (c + 1) * LANES], TN)
        pairs.append((both[:, :LANES], both[:, LANES:]))
    return pairs


def summed(table, value):
    high = value.astype(half)
    low = (value - high.astype(single)).astype(half)
    return mul(table, high, NT) + mul(table, low, NT)


def cotangent_kernel(p, split, stored_ref, table_ref, scale_ref, *refs):
    me, refs = (refs[0][0], refs[1:]) if split else (None, refs)
    out_refs, (words_ref, turn_ref) = refs[:-2], refs[-2:]
    clear_tail(p, words_ref)
    for h in range(p.step):
        spread(p, stored_ref, words_ref.at[h], h)
        tokens = gather_row(p, words_ref.at[h])
        analyse(p, tokens, table_ref[...], scale_ref[...], turn_ref, h)

    @pl.when(last_part())
    def _():
        send_turn(p, turn_ref, out_refs, p.modes, 2 * p.rows, 0, me)


def stats_kernel(p, stored_ref, sum_ref, tokens_ref, stat_ref, words_ref):
    clear_tail(p, words_ref)
    count = 2 * p.stack
    for h in range(p.step):
        spread(p, stored_ref, words_ref.at[h], h)
        tokens = gather_row(p, words_ref.at[h])
        tokens_ref[0, h] = tokens
        wide = tokens.astype(single)
        rows = mul(sum_ref[0], tokens, NT) + summed(sum_ref[1], wide * wide)
        stat_ref[0, h * count : (h + 1) * count, :] = rows[:count]


def moments(p, stat_refs, rows_ref):
    count = 2 * p.stack
    total = stat_refs[0][0]
    for ref in stat_refs[1:]:
        total = total + ref[0]
    for h in range(p.step):
        part = total[h * count : (h + 1) * count] * (1.0 / p.channels)
        mean, square = part[: p.stack], part[p.stack :]
        inverse = lax.rsqrt(square - mean * mean + norm_epsilon)
        rows_ref[h, : p.stack, :] = mean
        rows_ref[h, p.stack : count, :] = inverse
        if count < 8:
            rows_ref[h, count:, :] = jnp.zeros((8 - count, p.turn_pad * PACK), single)


def normalise_kernel(p, split, *refs):
    stat_refs = refs[: p.chan]
    tokens_ref, affine_ref, table_ref, scale_ref, wide_ref = refs[p.chan : p.chan + 5]
    refs = refs[p.chan + 5 :]
    me, refs = (refs[0][0], refs[1:]) if split else (None, refs)
    out_refs, (rows_ref, turn_ref) = refs[:-2], refs[-2:]
    moments(p, stat_refs, rows_ref)

    for h in range(p.step):
        tiles = []
        for c, (mean, inverse) in enumerate(expand(p, rows_ref[h], wide_ref)):
            at = slice(c * LANES, (c + 1) * LANES)
            centred = (tokens_ref[0, h, :, at].astype(single) - mean) * inverse
            tiles.append((centred * affine_ref[0:1, at] + affine_ref[1:2, at]).astype(half))
        normed = jnp.concatenate(tiles, axis=1)
        analyse(p, normed, table_ref[...], scale_ref[...], turn_ref, h)

    @pl.when(last_part())
    def _():
        send_turn(p, turn_ref, out_refs, p.modes, 2 * p.rows, 0, me)


def gelu_both(values):
    square = values * values
    inner = jnp.tanh(values * (gelu_scale + gelu_scale * gelu_cubic * square))
    upper = 0.5 + 0.5 * inner
    hidden = values * upper
    slope = upper + hidden * (1.0 - upper) * (
        2.0 * gelu_scale + 6.0 * gelu_scale * gelu_cubic * square
    )
    return hidden, slope


BAND = 32
COLUMNS = 256


def widened(p, value):
    blank = jnp.zeros((value.shape[0], LANES - p.width), single)
    return jnp.concatenate([value.astype(single), blank], axis=1)


def placed_slot(p, value, q):
    lane = lax.broadcasted_iota(jnp.int32, value.shape, 1)
    at, shift = divmod(q * p.width, LANES)
    turned = rolled(value, shift)
    tiles = [jnp.zeros_like(value) for _ in range(p.tiles)]
    tiles[at] = jnp.where(lane >= shift, turned, 0.0)
    if shift + p.width > LANES:
        tiles[at + 1] = jnp.where(lane < shift + p.width - LANES, turned, 0.0)
    return jnp.concatenate(tiles, axis=1)


def taken_slot(p, read, q):
    at, shift = divmod(q * p.width, LANES)
    value = rolled(read(at), -shift % LANES)
    if shift + p.width > LANES:
        lane = lax.broadcasted_iota(jnp.int32, value.shape, 1)
        value = jnp.where(lane < LANES - shift, value, rolled(read(at + 1), -shift % LANES))
    return value


PARTS = (((0, 0, 1), (1, 1, 1)), ((0, 1, 1), (1, 0, -1)))


def place_weights(p, w_refs, out_refs):
    for w_ref, out_ref in zip(w_refs, out_refs):
        for q in range(PACK):
            for part in range(2):
                wide = placed_slot(p, widened(p, w_ref[part, q % p.groups]), q)
                for row_ri, col_ri, sign in PARTS[part]:
                    top = row_ri * p.lanes + q * p.width
                    out_ref[top : top + p.width, col_ri * p.lanes : (col_ri + 1) * p.lanes] = (
                        sign * wide
                    ).astype(half)


def place_biases(p, b_refs, out_ref):
    for which, b_ref in enumerate(b_refs):
        for ri in range(2):
            row = jnp.zeros((1, p.lanes), single)
            for q in range(PACK):
                n = q % p.groups
                row = row + placed_slot(p, widened(p, b_ref[ri, n : n + 1, :]), q)
            out_ref[which : which + 1, ri * p.lanes : (ri + 1) * p.lanes] = row


def spectral_kernel(p, step_modes, peers, y_near, x_near, follows, *refs):
    x_refs, g_refs, refs = refs[:peers], refs[peers : 2 * peers], refs[2 * peers :]
    there_ref, back_ref, w_first_ref, w_second_ref, b_first_ref, b_second_ref = refs[:6]
    refs = refs[6:]
    before_ref, refs = (refs[0], refs[1:]) if follows else (None, refs)
    me, refs = (refs[0][0], refs[1:]) if y_near or x_near else (None, refs)
    y_count, x_count = (p.space if near else 1 for near in (y_near, x_near))
    y_refs, x_out_refs, refs = refs[:y_count], refs[y_count : y_count + x_count], refs[y_count + x_count :]
    (
        total_ref,
        gb_ref,
        bias_ref,
        lat_ref,
        hid_ref,
        gpost_ref,
        gpre_ref,
        slope_ref,
        gsh_ref,
        shr_ref,
        glat_ref,
        turn_y_ref,
        turn_x_ref,
        acc1_ref,
        acc2_ref,
        w1_ref,
        w2_ref,
    ) = refs
    pack, group = pl.program_id(0), pl.program_id(1)
    count = step_modes * p.lat
    factor = 1.0 / math.sqrt(p.lat)
    base = pl.multiple_of(group * count, count)

    @pl.when((pack == 0) & (group == 0))
    def _():
        place_weights(p, (w_first_ref, w_second_ref), (w1_ref, w2_ref))
        place_biases(p, (b_first_ref, b_second_ref), bias_ref)
        gb_ref[...] = jnp.zeros_like(gb_ref)
        acc1_ref[...] = jnp.zeros_like(acc1_ref)
        acc2_ref[...] = jnp.zeros_like(acc2_ref)

    def there(refs, into, offset):
        for m in range(step_modes):
            block = peer_rows(p, refs, m)
            out = (mul(there_ref[...], block) * factor).astype(half)
            at = pl.ds(offset + m * p.lat, p.lat)
            into[at, : p.lanes] = out[: p.lat]
            into[at, p.lanes :] = out[p.lat :]

    def back(value_of, turn_ref):
        for m in range(step_modes):
            rows = slice(m * p.lat, (m + 1) * p.lat)
            both = jnp.concatenate([value_of(rows, 0), value_of(rows, 1)], axis=0)
            out = mul(back_ref[...], both) * factor
            mode = group * step_modes + m
            for ri in range(2):
                for c in range(p.tiles):
                    turn_ref[c, pl.ds(ri * p.modes + mode, p.lat, stride=2 * p.modes), :] = out[
                        ri * p.lat : (ri + 1) * p.lat, c * LANES : (c + 1) * LANES
                    ]

    def bands(columns, body):
        for low in range(0, count, BAND):
            at = slice(low, low + BAND)
            body(at, pl.ds(pl.multiple_of(base + low, BAND), BAND), columns)

    def folded(value):
        return value.reshape(BAND // 8, 8, value.shape[1]).sum(0)

    there(x_refs, lat_ref, base)
    there(g_refs, gsh_ref, 0)
    every = [slice(low, low + COLUMNS) for low in range(0, 2 * p.lanes, COLUMNS)]
    lat = lat_ref[pl.ds(base, count), :]
    for columns in every:
        pre = mul(lat, w1_ref[:, columns])

        def first(at, kept, columns):
            hidden, slope = gelu_both(pre[at] + bias_ref[0:1, columns])
            hid_ref[kept, columns] = hidden.astype(half)
            slope_ref[at, columns] = slope

        bands(columns, first)
    hid = hid_ref[pl.ds(base, count), :]
    for columns in every:
        part = mul(hid, w2_ref[:, columns])
        sums = [jnp.zeros((8, COLUMNS), single)]

        def second(at, kept, columns):
            post = part[at] + bias_ref[1:2, columns]
            inner = jnp.tanh(post * (1.0 / shrink_level))
            shr_ref[at, columns] = (post - shrink_level * inner).astype(half)
            gpost = (gsh_ref[at, columns].astype(single) * (inner * inner)).astype(half)
            gpost_ref[kept, columns] = gpost
            sums[0] += folded(gpost.astype(single))

        bands(columns, second)
        gb_ref[8:16, columns] += sums[0]
    back(lambda rows, ri: shr_ref[rows, ri * p.lanes : (ri + 1) * p.lanes], turn_y_ref)
    gpost = gpost_ref[pl.ds(base, count), :]
    for columns in every:
        part = mul(gpost, w2_ref[columns, :], NT)
        sums = [jnp.zeros((8, COLUMNS), single)]

        def third(at, kept, columns):
            gpre = (part[at] * slope_ref[at, columns]).astype(half)
            gpre_ref[kept, columns] = gpre
            sums[0] += folded(gpre.astype(single))

        bands(columns, third)
        gb_ref[0:8, columns] += sums[0]
    gpre = gpre_ref[pl.ds(base, count), :]
    for columns in every:
        glat_ref[:, columns] = mul(gpre, w1_ref[columns, :], NT).astype(half)
    back(lambda rows, ri: glat_ref[rows, ri * p.lanes : (ri + 1) * p.lanes], turn_x_ref)

    @pl.when(group == pl.num_programs(1) - 1)
    def _():
        send_turn(p, turn_y_ref, y_refs, p.rows, 2 * p.modes, 0, me if y_near else None)
        send_turn(p, turn_x_ref, x_out_refs, p.rows, 2 * p.modes, 0, me if x_near else None)
        acc1_ref[...] += mul(lat_ref[...], gpre_ref[...], TN)
        acc2_ref[...] += mul(hid_ref[...], gpost_ref[...], TN)

    @pl.when((group == pl.num_programs(1) - 1) & (pack == pl.num_programs(0) - 1))
    def _():
        def keep(top, rows, value):
            at = slice(top, top + rows)
            if before_ref is not None:
                value = value + before_ref[at, :]
            total_ref[at, :] = value.astype(total_ref.dtype)

        place = 0
        for acc in (acc1_ref, acc2_ref):
            for part in range(2):
                for n in range(p.groups):
                    total = jnp.zeros((p.width, LANES), single)
                    for s in range(p.stack):
                        q = s * p.groups + n
                        for row_ri, col_ri, sign in PARTS[part]:
                            rows = slice(row_ri * p.lanes + q * p.width, row_ri * p.lanes + (q + 1) * p.width)

                            def read(tile):
                                left = col_ri * p.lanes + tile * LANES
                                return acc[rows, left : left + LANES]

                            total = total + sign * taken_slot(p, read, q)
                    keep(place, p.width, total)
                    place += p.width
        rows = []
        for which in range(2):
            sums = gb_ref[which * 8 : (which + 1) * 8, :].sum(0, keepdims=True)
            for ri in range(2):
                for n in range(p.groups):
                    row = jnp.zeros((1, LANES), single)
                    for s in range(p.stack):

                        def read(tile):
                            left = ri * p.lanes + tile * LANES
                            return sums[:, left : left + LANES]

                        row = row + taken_slot(p, read, s * p.groups + n)
                    rows.append(row)
        rows += [jnp.zeros((1, LANES), single)] * (-len(rows) % 8)
        keep(place, len(rows), jnp.concatenate(rows, axis=0))


def mixed_kernel(p, peers, *refs):
    rows_refs, (table_ref, out_ref, words_ref) = refs[:peers], refs[peers:]
    factor = 1.0 / math.sqrt(p.lon)

    for h in range(p.step):
        block = peer_rows(p, rows_refs, h)
        tokens = mul(table_ref[...], block) * factor
        scatter_row(p, tokens, words_ref.at[h], out_ref, h)


def slope_sums_kernel(p, peers, follows, *refs):
    stat_refs, refs = refs[: p.chan], refs[p.chan :]
    rows_in_refs, refs = refs[:peers], refs[peers:]
    tokens_ref, affine_ref, table_ref, wide_ref, sum_ref = refs[:5]
    refs = refs[5:]
    before_ref, refs = (refs[0], refs[1:]) if follows else (None, refs)
    sums_ref, total_ref, param_ref, rows_ref, dense_ref = refs
    factor = 1.0 / math.sqrt(p.lon)
    count = 2 * p.stack
    moments(p, stat_refs, rows_ref)

    @pl.when(first_step())
    def _():
        param_ref[...] = jnp.zeros_like(param_ref)

    for h in range(p.step):
        block = peer_rows(p, rows_in_refs, h)
        folds = (PACK * p.turn_pad // 8, 8, LANES)
        plain, scaled = [], []
        spectrum = mul(table_ref[...], block)
        for c, (mean, inverse) in enumerate(expand(p, rows_ref[h], wide_ref)):
            at = slice(c * LANES, (c + 1) * LANES)
            normed_grad = spectrum[:, at] * factor
            centred = (tokens_ref[0, h, :, at].astype(single) - mean) * inverse
            param_ref[0:8, at] += (normed_grad * centred).reshape(folds).sum(0)
            param_ref[8:16, at] += normed_grad.reshape(folds).sum(0)
            grad = normed_grad * affine_ref[0:1, at]
            plain.append(grad.astype(half))
            scaled.append((grad * centred).astype(half))
        sums = mul(sum_ref[0], jnp.concatenate(plain, axis=1), NT) + mul(
            sum_ref[1], jnp.concatenate(scaled, axis=1), NT
        )
        dense_ref[h * count : (h + 1) * count, :] = sums[:count]
    sums_ref[0] = dense_ref[...].astype(half)

    @pl.when(last_step())
    def _():
        for kind in range(2):
            at = slice(kind, kind + 1)
            total = param_ref[8 * kind : 8 * kind + 8, :].sum(0, keepdims=True)
            if before_ref is not None:
                total = total + before_ref[0, at, :]
            for d in range(p.space):
                total_ref[d, at, :] = total


def input_grad_kernel(p, peers, *refs):
    stat_refs, part_refs, refs = refs[: p.chan], refs[p.chan : 2 * p.chan], refs[2 * p.chan :]
    rows_in_refs, refs = refs[:peers], refs[peers:]
    tokens_ref, affine_ref, table_ref, wide_ref, out_ref, rows_ref, part_ref, words_ref = refs
    factor = 1.0 / math.sqrt(p.lon)
    count = 2 * p.stack
    moments(p, stat_refs, rows_ref)
    total = part_refs[0][0].astype(single)
    for ref in part_refs[1:]:
        total = total + ref[0].astype(single)
    for h in range(p.step):
        part_ref[h, :count, :] = total[h * count : (h + 1) * count] * (1.0 / p.channels)
        if count < 8:
            part_ref[h, count:, :] = jnp.zeros((8 - count, p.turn_pad * PACK), single)

    for h in range(p.step):
        block = peer_rows(p, rows_in_refs, h)
        spectrum = mul(table_ref[...], block)
        moment = expand(p, rows_ref[h], wide_ref)
        means = expand(p, part_ref[h], wide_ref)
        tiles = []
        for c in range(p.tiles):
            at = slice(c * LANES, (c + 1) * LANES)
            (mean, inverse), (first, second) = moment[c], means[c]
            centred = (tokens_ref[0, h, :, at].astype(single) - mean) * inverse
            grad = spectrum[:, at] * factor * affine_ref[0:1, at]
            tiles.append(inverse * (grad - first - centred * second))
        grad = jnp.concatenate(tiles, axis=1)
        scatter_row(p, grad, words_ref.at[h], out_ref, h)


def whole_spec(value):
    dims = value.shape
    return pl.BlockSpec(dims, lambda *_: (0,) * len(dims))


def part_spec(p, value):
    dims = (1, value.shape[1] // p.steps) + value.shape[2:]
    return pl.BlockSpec(dims, lambda b, r: (b, r) + (0,) * (len(dims) - 2))


def peer_spec(value, which=0, wide=1):
    dims = (value.shape[0], wide, 1) + value.shape[3:]
    return pl.BlockSpec(dims, lambda b, *_: (0, which, b) + (0,) * (len(dims) - 3))


def peer_part_spec(p, value, which=0):
    dims = (value.shape[0], 1, 1, value.shape[3] // p.steps) + value.shape[4:]
    return pl.BlockSpec(dims, lambda b, r: (0, which, b, r) + (0,) * (len(dims) - 4))


def one_peer_spec(value, which=0):
    dims = (1, 1) + value.shape[2:]
    return pl.BlockSpec(dims, lambda b, *_: (which, b) + (0,) * (len(dims) - 2))


def one_peer_part_spec(p, value):
    dims = (1, 1, value.shape[2] // p.steps) + value.shape[3:]
    return pl.BlockSpec(dims, lambda b, r: (0, b, r) + (0,) * (len(dims) - 3))


def stored_spec(p, offset):
    return pl.BlockSpec((p.stack, p.step, p.groups, p.long), lambda b, r: (b + offset, r, 0, 0))


def call(body, grid, ins, in_specs, outs, out_specs, scratch, flops, aliases=None):
    moved = sum(v.size * v.dtype.itemsize for v in ins) + sum(
        math.prod(o.shape) * o.dtype.itemsize for o in outs
    )
    return _call(body, grid, ins, in_specs, outs, out_specs, scratch, flops, moved, aliases)


def _call(body, grid, ins, in_specs, outs, out_specs, scratch, flops, moved, aliases):
    return pl.pallas_call(
        body,
        grid=grid,
        in_specs=in_specs,
        out_specs=out_specs,
        out_shape=outs,
        scratch_shapes=scratch,
        input_output_aliases=aliases or {},
        compiler_params=pltpu.CompilerParams(vmem_limit_bytes=VMEM_LIMIT),
        cost_estimate=pl.CostEstimate(flops=flops, bytes_accessed=moved, transcendentals=0),
    )(*ins)


def lon_tables(p):
    cos_lon, sin_lon = trig(p.lon, MW)
    wave = np.concatenate([cos_lon, -sin_lon], axis=1)
    turned = np.zeros((PACK, p.turn_pad, 2 * MW), np.float32)
    turned[:, : p.turn] = wave.reshape(p.turn, PACK, 2 * MW).transpose(1, 0, 2)
    turned = turned.reshape(PACK * p.turn_pad, 2 * MW)
    doubling = np.where(np.arange(MW) == 0, 1.0, 2.0).astype(np.float32)
    factor = np.float32(1.0 / math.sqrt(p.lon))
    plain_scale = np.full((2 * MW, 1), factor, np.float32)
    double_scale = (factor * np.tile(doubling, 2))[:, None].astype(np.float32)
    owner = turned.reshape(-1, 2, p.space, p.modes).transpose(0, 2, 1, 3).reshape(-1, 2 * MW)
    twice = np.tile(doubling.reshape(p.space, 1, p.modes), (1, 2, 1)).reshape(1, 2 * MW)
    to_half = lambda value: jnp.asarray(value, half)
    return (
        to_half(turned.T),
        jnp.asarray(plain_scale),
        jnp.asarray(double_scale),
        owner * twice,
        owner,
    )


def by_distance(p, table, inner):
    at = np.arange(p.space * inner, dtype=np.int32)
    source = ((at // inner) ^ lax.axis_index("space").astype(jnp.int32)) * inner + at % inner
    chosen = (at[:, None] == source[None, :]).astype(half)
    return mul(jnp.asarray(table, half), chosen).astype(half)


def lat_tables(p):
    cos_lat, sin_lat = trig(p.lat, p.lat)
    there = np.block([[cos_lat, sin_lat], [-sin_lat, cos_lat]])
    there = there.reshape(2 * p.lat, 2, p.space, p.rows).transpose(0, 2, 1, 3)
    back = np.block([[cos_lat.T, -sin_lat.T], [sin_lat.T, cos_lat.T]])
    return there.reshape(2 * p.lat, 2 * p.lat), jnp.asarray(back, half)


def sum_tables(p):
    owner = np.arange(PACK) // p.groups
    lane_owner = np.repeat(owner, p.width)
    sums = np.zeros((2, 8, p.lanes), np.float32)
    wide = np.zeros((3, 8, 2, p.lanes), np.float32)
    for s in range(p.stack):
        sums[0, s] = lane_owner == s
        sums[1, p.stack + s] = lane_owner == s
        wide[:, s, 0] = lane_owner == s
        wide[:, p.stack + s, 1] = lane_owner == s
    wide = wide.reshape(24, 2, p.tiles, LANES).transpose(0, 2, 1, 3)
    return jnp.asarray(sums, half), jnp.asarray(wide.reshape(24, 2 * p.lanes), half)


def splits(space):
    return (MW // space) % 4 == 0 and space & (space - 1) == 0


def exchange_near(values):
    count = len(values)
    return tuple(
        value if x == 0 else lax.ppermute(value, "space", [(i, i ^ x) for i in range(count)])
        for x, value in enumerate(values)
    )


def exchange(value):
    return lax.all_to_all(value, "space", 0, 0, tiled=True)


def around(value, axis, size):
    gathered = [value]
    for step in range(1, size):
        gathered.append(
            lax.ppermute(value, axis, [(i, (i + step) % size) for i in range(size)])
        )
    return gathered


def reduced(p, value, kind):
    step = 1
    while step < p.space:
        wide = step > 1 and 4 * step <= p.space
        own = value.astype(kind)
        near, far, both = (
            lax.ppermute(own, "space", [(i, i ^ (step * k)) for i in range(p.space)])
            if k == 1 or wide
            else None
            for k in (1, 2, 3)
        )
        value = own.astype(single) + near.astype(single)
        if wide:
            value = value + (far.astype(single) + both.astype(single))
        step *= 4 if wide else 2
    return value


def on_device(space, chan, members, gain, shift, w_first, b_first, w_second, b_second, cotangent):
    p = Plan(members, w_first.shape[-1], space, chan)
    size = p.packs // 2
    grid = (size, p.steps)
    table, plain_scale, double_scale, mixed_plain, slope_plain = lon_tables(p)
    there_plain, back_table = lat_tables(p)
    slope_table, there_table = jnp.asarray(slope_plain, half), jnp.asarray(there_plain, half)
    mixed_table = jnp.asarray(mixed_plain, half)
    split = splits(space)
    if split:
        slope_near = by_distance(p, slope_plain, 2 * p.modes)
        mixed_near = by_distance(p, mixed_plain, 2 * p.modes)
        there_near = by_distance(p, there_plain, 2 * p.rows)
        me = lax.axis_index("space").astype(jnp.int32).reshape(1)
    own_spec = pl.BlockSpec(memory_space=pltpu.SMEM)
    sum_table, wide_table = sum_tables(p)
    affine = jnp.concatenate([gain] * p.stack + [shift] * p.stack).reshape(2, p.lanes)
    tokens_rows = PACK * p.turn_pad
    dft_flops = 2 * size * p.rows * tokens_rows * 2 * MW * p.lanes
    words = pltpu.VMEM((p.step, PACK, p.word_pad, LANES), single)
    lines = pltpu.VMEM((p.step, p.stack, p.word_pad * p.groups, LANES), single)
    turn_in = pltpu.VMEM((p.tiles, MW * 2 * p.rows, LANES), single)
    rows_scratch = pltpu.VMEM((p.step, 8, tokens_rows), single)

    def sent(wide):
        return jax.ShapeDtypeStruct((space, wide, size, p.modes, 2 * p.rows, p.lanes), half)

    returned = jax.ShapeDtypeStruct((space, 1, size, p.rows, 2 * p.modes, p.lanes), half)

    count = 2 * p.stack * p.rows
    stored = jax.ShapeDtypeStruct(members.shape, half)

    def out_call(body, ins, specs, outs, out_specs, scratch, flops, before):
        ins, specs = list(ins), list(specs)
        aliases = {}
        inner = body
        if before is not None:
            place, extra = len(ins), len(before)
            inner = lambda *refs: body(*refs[:place], *refs[place + extra :])
            ins += before
            specs += [pl.BlockSpec(memory_space=pl.ANY)] * extra
            aliases = {place + k: k for k in range(extra)}
        return call(inner, grid, tuple(ins), specs, outs, out_specs, scratch, flops, aliases)

    def spectra_out(wide, which, near):
        if near:
            one = jax.ShapeDtypeStruct(sent(wide).shape[1:], half)
            return [one] * space, [one_peer_spec(one, which)] * space
        return [sent(wide)], [peer_spec(sent(wide), which)]

    def cotangent_chunk(c, wide, near):
        outs, out_specs = spectra_out(wide, 0, near)
        ins, specs = (cotangent, table, double_scale), [whole_spec(table), whole_spec(double_scale)]
        if near:
            ins, specs = (*ins, me), [*specs, own_spec]
        return out_call(
            functools.partial(cotangent_kernel, p, near), ins,
            [stored_spec(p, c * size), *specs], outs, out_specs, [words, turn_in], dft_flops, None,
        )

    def stats_chunk(c):
        ins = (members, sum_table)
        outs = [
            jax.ShapeDtypeStruct((size, p.rows, tokens_rows, p.lanes), half),
            jax.ShapeDtypeStruct((size, count, tokens_rows), single),
        ]
        return call(
            functools.partial(stats_kernel, p), grid, ins,
            [stored_spec(p, c * size), whole_spec(sum_table)],
            outs, [part_spec(p, o) for o in outs], [words], dft_flops // 4,
        )

    def normalise_chunk(stats, tokens, before, near):
        tail = (affine, table, plain_scale, wide_table)
        ins = (*stats, tokens, *tail)
        specs = [part_spec(p, s) for s in (*stats, tokens)] + [whole_spec(v) for v in tail]
        if near:
            ins, specs = (*ins, me), [*specs, own_spec]
        which = 0 if before is None else 1
        outs, out_specs = spectra_out(which + 1, which, near)
        return out_call(
            functools.partial(normalise_kernel, p, near), ins, specs,
            outs, out_specs, [rows_scratch, turn_in], dft_flops, before,
        )

    step_modes = 2 if p.modes % 2 == 0 else 1
    wide_lanes = 2 * p.lanes

    def spectral_chunk(x_in, x_which, g_in, before, y_near, x_near):
        peers = len(x_in)
        tail = (there_near if peers > 1 else there_table, back_table)
        tail += (w_first, w_second, b_first, b_second)
        tail += () if before is None else (before,)
        specs = [whole_spec(v) for v in tail]
        if y_near or x_near:
            tail, specs = (*tail, me), [*specs, own_spec]

        def mode_spec(which):
            lead = (1, 1) if peers > 1 else (space, 1, 1)
            at = (which,) if peers > 1 else (0, which)
            return pl.BlockSpec(
                lead + (step_modes, 2 * p.rows, p.lanes), lambda b, m: at + (b, m, 0, 0)
            )

        outs, out_specs = [], []
        one = jax.ShapeDtypeStruct(returned.shape[1:], half)
        for near in (y_near, x_near):
            outs += [one] * space if near else [returned]
            out_specs += [one_peer_spec(one)] * space if near else [peer_spec(returned)]
        bias_rows = -(-4 * p.groups // 8) * 8
        totals = jax.ShapeDtypeStruct(
            (4 * p.groups * p.width + bias_rows, LANES), single if before is None else half
        )
        kept = pltpu.VMEM((p.modes * p.lat, wide_lanes), half)
        held = pltpu.VMEM((step_modes * p.lat, wide_lanes), single)
        brief = pltpu.VMEM((step_modes * p.lat, wide_lanes), half)
        turn_out = pltpu.VMEM((p.tiles, p.lat * 2 * p.modes, LANES), single)
        return call(
            functools.partial(
                spectral_kernel, p, step_modes, peers, y_near, x_near, before is not None
            ),
            (size, p.modes // step_modes), (*x_in, *g_in, *tail),
            [mode_spec(x_which)] * peers + [mode_spec(0)] * peers + specs,
            [*outs, totals],
            [*out_specs, whole_spec(totals)],
            [pltpu.VMEM((16, wide_lanes), single), pltpu.VMEM((2, wide_lanes), single)]
            + [kept] * 4 + [held] + [brief] * 3 + [turn_out] * 2
            + [pltpu.VMEM((wide_lanes, wide_lanes), single)] * 2
            + [pltpu.VMEM((wide_lanes, wide_lanes), half)] * 2,
            12 * size * p.modes * p.lat * wide_lanes * wide_lanes,
        )

    def mixed_chunk(c, rows_in, before):
        table_in = mixed_near if len(rows_in) > 1 else mixed_table
        return out_call(
            functools.partial(mixed_kernel, p, len(rows_in)), (*rows_in, table_in),
            rows_specs(rows_in) + [whole_spec(table_in)],
            [stored], [stored_spec(p, c * size)], [lines], dft_flops, before,
        )

    def rows_specs(rows_in):
        if len(rows_in) == 1:
            return [peer_part_spec(p, rows_in[0])]
        return [one_peer_part_spec(p, value) for value in rows_in]

    def slope_sums_chunk(stats, rows_in, tokens, before):
        near = len(rows_in) > 1
        tail = (affine, slope_near if near else slope_table, wide_table, sum_table)
        tail += () if before is None else (before,)
        outs = [
            jax.ShapeDtypeStruct((size, count, tokens_rows), half),
            jax.ShapeDtypeStruct((space, 2, p.lanes), single),
        ]
        return call(
            functools.partial(slope_sums_kernel, p, len(rows_in), before is not None),
            grid, (*stats, *rows_in, tokens, *tail),
            [part_spec(p, s) for s in stats] + rows_specs(rows_in)
            + [part_spec(p, tokens)] + [whole_spec(v) for v in tail],
            outs, [part_spec(p, outs[0]), whole_spec(outs[1])],
            [
                pltpu.VMEM((16, p.lanes), single), rows_scratch,
                pltpu.VMEM((count // p.steps, tokens_rows), single),
            ],
            dft_flops,
        )

    def input_grad_chunk(c, stats, parts, rows_in, tokens, before):
        near = len(rows_in) > 1
        tail = (affine, slope_near if near else slope_table, wide_table)
        return out_call(
            functools.partial(input_grad_kernel, p, len(rows_in)),
            (*stats, *parts, *rows_in, tokens, *tail),
            [part_spec(p, s) for s in (*stats, *parts)] + rows_specs(rows_in)
            + [part_spec(p, tokens)] + [whole_spec(v) for v in tail],
            [stored], [stored_spec(p, c * size)], [rows_scratch, rows_scratch, lines], dft_flops,
            before,
        )

    def channel_sums(value):
        return around(value, "chan", chan)

    def moved(values, near):
        return exchange_near(values) if near else (exchange(values[0]),)

    g0 = moved(cotangent_chunk(0, 1, False), False)
    tokens0, sums = stats_chunk(0)
    stats0 = channel_sums(sums)
    x0 = moved(normalise_chunk(stats0, tokens0, None, False), False)
    both1 = cotangent_chunk(1, 2, split)
    tokens1, sums = stats_chunk(1)
    stats1 = channel_sums(sums)
    both1 = moved(normalise_chunk(stats1, tokens1, both1, split), split)
    cut = space if split else 1
    *outs, totals = spectral_chunk(x0, 0, g0, None, split, False)
    dx0 = moved(outs[cut:], False)
    y0 = moved(outs[:cut], split)
    *outs, totals = spectral_chunk(both1, 1, both1, totals, False, split)
    dx1 = moved(outs[1:], split)
    y1 = moved(outs[:1], False)
    sums, params = slope_sums_chunk(stats0, dx0, tokens0, None)
    parts = channel_sums(sums)
    grad_input = input_grad_chunk(0, stats0, parts, dx0, tokens0, None)
    mixed = mixed_chunk(0, y0, None)
    sums, params = slope_sums_chunk(stats1, dx1, tokens1, params)
    parts = channel_sums(sums)
    grad_input = input_grad_chunk(1, stats1, parts, dx1, tokens1, grad_input)[0]
    mixed = mixed_chunk(1, y1, mixed)[0]

    size_w = p.groups * p.width
    flat = reduced(p, totals, half)[:, : p.width]
    grads = flat[: 4 * size_w].reshape((2,) + w_first.shape)
    bias_grads = flat[4 * size_w : 4 * size_w + 4 * p.groups].reshape((2,) + b_first.shape)
    params = exchange(params).sum(0)
    params = [
        sum(params[kind, s * size_w : (s + 1) * size_w] for s in range(p.stack)) for kind in range(2)
    ]
    return (
        mixed, grad_input, grads[0], bias_grads[0], grads[1], bias_grads[1], params[0], params[1]
    )


def solution(mesh):
    tokens = P(None, "space", "chan", None)
    weights = P(None, "chan", None, None)
    biases = P(None, "chan", None)
    placed = (tokens, P("chan"), P("chan"), weights, biases, weights, biases, tokens)
    return jax.shard_map(
        functools.partial(on_device, mesh.shape["space"], mesh.shape["chan"]),
        mesh=mesh,
        in_specs=placed,
        out_specs=(tokens, tokens, weights, biases, weights, biases, P("chan"), P("chan")),
        check_vma=False,
    )
```

```python
import functools
import math

import jax
import jax.numpy as jnp
import numpy as np
from jax import lax
from jax.experimental import pallas as pl
from jax.experimental.pallas import tpu as pltpu
from jax.sharding import PartitionSpec as P


MW = 64
LANES = 128
PACK = 4

shrink_level = 0.05
norm_epsilon = 1e-05
gelu_scale = 0.7978845608
gelu_cubic = 0.044715

half = jnp.bfloat16
single = jnp.float32
VMEM_LIMIT = 67043328
SLOTS = 4

TN = (((0,), (0,)), ((), ()))
NT = (((1,), (1,)), ((), ()))


def mul(first_op, second_op, dims=(((1,), (0,)), ((), ()))):
    return lax.dot_general(first_op, second_op, dims, preferred_element_type=single)


def trig(length, columns):
    angles = (np.arange(length)[:, None] * np.arange(columns)[None, :] % length).astype(np.float32)
    angles = (angles * np.float32(2.0 * math.pi / length)).astype(np.float64)
    cast = lambda table: table.astype(np.float32).astype(half).astype(np.float32)
    return cast(np.cos(angles)), cast(np.sin(angles))


class Plan:
    def __init__(self, members, width, space, chan):
        self.batch, self.rows, self.groups, self.long = members.shape
        self.width, self.space, self.chan = width, space, chan
        self.lon = self.long // width
        self.lat = self.rows * space
        self.modes = MW // space
        self.stack = PACK // self.groups
        self.packs = self.batch // self.stack
        self.lanes = PACK * width
        self.tiles = self.lanes // LANES
        self.turn = self.lon // PACK
        self.turn_pad = -(-self.turn // 16) * 16
        self.words = self.long // LANES
        self.step = SLOTS if self.rows % SLOTS == 0 else self.rows
        self.steps = self.rows // self.step
        self.word_pad = self.tiles * self.turn_pad
        self.channels = self.groups * width * chan


def moved_lanes(p, fetch, from_start, to_start, tile):
    pieces = []
    for slot in range(PACK):
        low = max(to_start(slot), tile * LANES)
        high = min(to_start(slot) + p.width, (tile + 1) * LANES)
        at = low
        while at < high:
            source = at - to_start(slot) + from_start(slot)
            stop = min(high, at + LANES - source % LANES)
            shift = (at - source) % LANES
            pieces.append((stop - tile * LANES, fetch(slot, source // LANES, shift)))
            at = stop
    return pieces


def merged(pieces, lane):
    value = pieces[-1][1]
    for stop, piece in reversed(pieces[:-1]):
        value = jnp.where(lane < stop, piece, value)
    return value


def rolled(value, shift):
    return value if shift == 0 else pltpu.roll(value, shift, 1)


def spread(p, stored_ref, words_ref, h):
    for q in range(PACK):
        line = stored_ref[q // p.groups, h, q % p.groups, :]
        words_ref[q, : p.words, :] = line.reshape(p.words, LANES).astype(single)


def gather_row(p, words_ref):
    lane = lax.broadcasted_iota(jnp.int32, (p.turn_pad, LANES), 1)
    source = {}
    for q in range(PACK):
        for i in range(p.tiles):
            source[q, i] = words_ref[q, pl.ds(i, p.turn_pad, stride=p.tiles), :]
    rows = []
    for r in range(PACK):
        cache = {}

        def fetch(q, i, shift):
            key = (q, i, shift)
            if key not in cache:
                cache[key] = rolled(source[q, i], shift)
            return cache[key]

        tiles = []
        for c in range(p.tiles):
            pieces = moved_lanes(p, fetch, lambda q: r * p.width, lambda q: q * p.width, c)
            tiles.append(merged(pieces, lane).astype(half))
        rows.append(jnp.concatenate(tiles, axis=1))
    return jnp.concatenate(rows, axis=0)


def scatter_row(p, tokens, words_ref, stored_ref, h):
    lane = lax.broadcasted_iota(jnp.int32, (p.turn_pad, LANES), 1)
    for q in range(PACK):
        s, n = divmod(q, p.groups)
        cache = {}

        def fetch(r, c, shift):
            if (r, c, shift) not in cache:
                part = tokens[r * p.turn_pad : (r + 1) * p.turn_pad, c * LANES : (c + 1) * LANES]
                cache[r, c, shift] = rolled(part, shift)
            return cache[r, c, shift]

        for i in range(p.tiles):
            pieces = moved_lanes(p, fetch, lambda r: q * p.width, lambda r: r * p.width, i)
            at = pl.ds(i * p.groups + n, p.turn_pad, stride=p.tiles * p.groups)
            words_ref[s, at, :] = merged(pieces, lane)
    for s in range(p.stack):
        lines = words_ref[s, : p.words * p.groups, :].astype(half)
        for t in range(p.words):
            stored_ref[s, h, :, t * LANES : (t + 1) * LANES] = lines[
                t * p.groups : (t + 1) * p.groups, :
            ]


def clear_tail(p, words_ref):
    @pl.when(first_step())
    def _():
        tail = p.word_pad - p.words
        words_ref[:, :, p.words :, :] = jnp.zeros(words_ref.shape[:2] + (tail, LANES), single)


def pipelined(p, fetch, use):
    ahead = fetch(0)
    for h in range(p.step):
        now, ahead = ahead, fetch(h + 1) if h + 1 < p.step else None
        use(h, now)


def first_step():
    return (pl.program_id(0) == 0) & (pl.program_id(1) == 0)


def last_step():
    return (pl.program_id(0) == pl.num_programs(0) - 1) & (
        pl.program_id(1) == pl.num_programs(1) - 1
    )


def last_part():
    return pl.program_id(1) == pl.num_programs(1) - 1


def analyse(p, tokens, table, scale, turn_ref, h):
    h = pl.program_id(1) * p.step + h
    spectrum = mul(table, tokens) * scale
    for c in range(p.tiles):
        for ri in range(2):
            turn_ref[c, pl.ds(ri * p.rows + h, MW, stride=2 * p.rows), :] = spectrum[
                ri * MW : (ri + 1) * MW, c * LANES : (c + 1) * LANES
            ]


def send_turn(p, turn_ref, out_refs, outer, inner, which=0, me=None):
    count = outer * inner
    for x in range(p.space):
        for c in range(p.tiles):
            lanes = slice(c * LANES, (c + 1) * LANES)
            if me is None:
                part = turn_ref[c, x * count : (x + 1) * count, :]
                out_refs[0][x, which, 0, :, :, lanes] = part.reshape(outer, inner, LANES).astype(half)
            else:
                at = pl.ds(pl.multiple_of((me ^ x) * count, 8), count)
                part = turn_ref[c, at, :]
                out_refs[x][which, 0, :, :, lanes] = part.reshape(outer, inner, LANES).astype(half)


def peer_rows(p, refs, i):
    if len(refs) == 1:
        return refs[0][:, 0, 0, i].reshape(-1, p.lanes)
    return jnp.concatenate([ref[0, 0, i] for ref in refs], axis=0)


def split_three(value):
    high = value.astype(half).astype(single)
    rest = value - high
    middle = rest.astype(half).astype(single)
    return high, middle, rest - middle


def expand(p, parts, wide_ref):
    stacked = jnp.concatenate(split_three(parts), axis=0).astype(half)
    pairs = []
    for c in range(p.tiles):
        both = mul(stacked, wide_ref[:, 2 * c * LANES : 2 * (c + 1) * LANES], TN)
        pairs.append((both[:, :LANES], both[:, LANES:]))
    return pairs


def summed(table, value):
    high = value.astype(half)
    low = (value - high.astype(single)).astype(half)
    return mul(table, high, NT) + mul(table, low, NT)


def cotangent_kernel(p, split, stored_ref, table_ref, scale_ref, *refs):
    me, refs = (refs[0][0], refs[1:]) if split else (None, refs)
    out_refs, (words_ref, turn_ref) = refs[:-2], refs[-2:]
    clear_tail(p, words_ref)

    def fetch(h):
        spread(p, stored_ref, words_ref.at[h], h)
        return gather_row(p, words_ref.at[h])

    def use(h, tokens):
        analyse(p, tokens, table_ref[...], scale_ref[...], turn_ref, h)

    pipelined(p, fetch, use)

    @pl.when(last_part())
    def _():
        send_turn(p, turn_ref, out_refs, p.modes, 2 * p.rows, 0, me)


def stats_kernel(p, stored_ref, sum_ref, tokens_ref, stat_ref, words_ref):
    clear_tail(p, words_ref)
    count = 2 * p.stack

    def fetch(h):
        spread(p, stored_ref, words_ref.at[h], h)
        return gather_row(p, words_ref.at[h])

    def use(h, tokens):
        tokens_ref[0, h] = tokens
        wide = tokens.astype(single)
        rows = mul(sum_ref[0], tokens, NT) + summed(sum_ref[1], wide * wide)
        stat_ref[0, h * count : (h + 1) * count, :] = rows[:count]

    pipelined(p, fetch, use)


def moments(p, stat_refs, rows_ref):
    count = 2 * p.stack
    total = stat_refs[0][0]
    for ref in stat_refs[1:]:
        total = total + ref[0]
    for h in range(p.step):
        part = total[h * count : (h + 1) * count] * (1.0 / p.channels)
        mean, square = part[: p.stack], part[p.stack :]
        inverse = lax.rsqrt(square - mean * mean + norm_epsilon)
        rows_ref[h, : p.stack, :] = mean
        rows_ref[h, p.stack : count, :] = inverse
        if count < 8:
            rows_ref[h, count:, :] = jnp.zeros((8 - count, p.turn_pad * PACK), single)


def normalise_kernel(p, split, *refs):
    stat_refs = refs[: p.chan]
    tokens_ref, affine_ref, table_ref, scale_ref, wide_ref = refs[p.chan : p.chan + 5]
    refs = refs[p.chan + 5 :]
    me, refs = (refs[0][0], refs[1:]) if split else (None, refs)
    out_refs, (rows_ref, turn_ref) = refs[:-2], refs[-2:]
    moments(p, stat_refs, rows_ref)

    def use(h, pairs):
        tiles = []
        for c, (mean, inverse) in enumerate(pairs):
            at = slice(c * LANES, (c + 1) * LANES)
            centred = (tokens_ref[0, h, :, at].astype(single) - mean) * inverse
            tiles.append((centred * affine_ref[0:1, at] + affine_ref[1:2, at]).astype(half))
        normed = jnp.concatenate(tiles, axis=1)
        analyse(p, normed, table_ref[...], scale_ref[...], turn_ref, h)

    pipelined(p, lambda h: expand(p, rows_ref[h], wide_ref), use)

    @pl.when(last_part())
    def _():
        send_turn(p, turn_ref, out_refs, p.modes, 2 * p.rows, 0, me)


def gelu_both(values):
    square = values * values
    inner = jnp.tanh(values * (gelu_scale + gelu_scale * gelu_cubic * square))
    upper = 0.5 + 0.5 * inner
    hidden = values * upper
    slope = upper + hidden * (1.0 - upper) * (
        2.0 * gelu_scale + 6.0 * gelu_scale * gelu_cubic * square
    )
    return hidden, slope


BAND = 32
COLUMNS = 256


def widened(p, value):
    blank = jnp.zeros((value.shape[0], LANES - p.width), single)
    return jnp.concatenate([value.astype(single), blank], axis=1)


def placed_slot(p, value, q):
    lane = lax.broadcasted_iota(jnp.int32, value.shape, 1)
    at, shift = divmod(q * p.width, LANES)
    turned = rolled(value, shift)
    tiles = [jnp.zeros_like(value) for _ in range(p.tiles)]
    tiles[at] = jnp.where(lane >= shift, turned, 0.0)
    if shift + p.width > LANES:
        tiles[at + 1] = jnp.where(lane < shift + p.width - LANES, turned, 0.0)
    return jnp.concatenate(tiles, axis=1)


def taken_slot(p, read, q):
    at, shift = divmod(q * p.width, LANES)
    value = rolled(read(at), -shift % LANES)
    if shift + p.width > LANES:
        lane = lax.broadcasted_iota(jnp.int32, value.shape, 1)
        value = jnp.where(lane < LANES - shift, value, rolled(read(at + 1), -shift % LANES))
    return value


PARTS = (((0, 0, 1), (1, 1, 1)), ((0, 1, 1), (1, 0, -1)))


def place_weights(p, w_refs, out_refs):
    for w_ref, out_ref in zip(w_refs, out_refs):
        for q in range(PACK):
            for part in range(2):
                wide = placed_slot(p, widened(p, w_ref[part, q % p.groups]), q)
                for row_ri, col_ri, sign in PARTS[part]:
                    top = row_ri * p.lanes + q * p.width
                    out_ref[top : top + p.width, col_ri * p.lanes : (col_ri + 1) * p.lanes] = (
                        sign * wide
                    ).astype(half)


def place_biases(p, b_refs, out_ref):
    for which, b_ref in enumerate(b_refs):
        for ri in range(2):
            row = jnp.zeros((1, p.lanes), single)
            for q in range(PACK):
                n = q % p.groups
                row = row + placed_slot(p, widened(p, b_ref[ri, n : n + 1, :]), q)
            out_ref[which : which + 1, ri * p.lanes : (ri + 1) * p.lanes] = row


def spectral_kernel(p, step_modes, peers, y_near, x_near, follows, *refs):
    x_refs, g_refs, refs = refs[:peers], refs[peers : 2 * peers], refs[2 * peers :]
    there_ref, back_ref, w_first_ref, w_second_ref, b_first_ref, b_second_ref = refs[:6]
    refs = refs[6:]
    before_ref, refs = (refs[0], refs[1:]) if follows else (None, refs)
    me, refs = (refs[0][0], refs[1:]) if y_near or x_near else (None, refs)
    y_count, x_count = (p.space if near else 1 for near in (y_near, x_near))
    y_refs, x_out_refs, refs = refs[:y_count], refs[y_count : y_count + x_count], refs[y_count + x_count :]
    (
        total_ref,
        gb_ref,
        bias_ref,
        lat_ref,
        hid_ref,
        gpost_ref,
        gpre_ref,
        slope_ref,
        gsh_ref,
        shr_ref,
        glat_ref,
        turn_y_ref,
        turn_x_ref,
        acc1_ref,
        acc2_ref,
        w1_ref,
        w2_ref,
    ) = refs
    pack, group = pl.program_id(0), pl.program_id(1)
    count = step_modes * p.lat
    factor = 1.0 / math.sqrt(p.lat)
    base = pl.multiple_of(group * count, count)

    @pl.when((pack == 0) & (group == 0))
    def _():
        place_weights(p, (w_first_ref, w_second_ref), (w1_ref, w2_ref))
        place_biases(p, (b_first_ref, b_second_ref), bias_ref)
        gb_ref[...] = jnp.zeros_like(gb_ref)
        acc1_ref[...] = jnp.zeros_like(acc1_ref)
        acc2_ref[...] = jnp.zeros_like(acc2_ref)

    def there(refs, into, offset):
        for m in range(step_modes):
            block = peer_rows(p, refs, m)
            out = (mul(there_ref[...], block) * factor).astype(half)
            at = pl.ds(offset + m * p.lat, p.lat)
            into[at, : p.lanes] = out[: p.lat]
            into[at, p.lanes :] = out[p.lat :]

    def back(value_of, turn_ref):
        for m in range(step_modes):
            rows = slice(m * p.lat, (m + 1) * p.lat)
            both = jnp.concatenate([value_of(rows, 0), value_of(rows, 1)], axis=0)
            out = mul(back_ref[...], both) * factor
            mode = group * step_modes + m
            for ri in range(2):
                for c in range(p.tiles):
                    turn_ref[c, pl.ds(ri * p.modes + mode, p.lat, stride=2 * p.modes), :] = out[
                        ri * p.lat : (ri + 1) * p.lat, c * LANES : (c + 1) * LANES
                    ]

    def bands(columns, body):
        for low in range(0, count, BAND):
            at = slice(low, low + BAND)
            body(at, pl.ds(pl.multiple_of(base + low, BAND), BAND), columns)

    def folded(value):
        return value.reshape(BAND // 8, 8, value.shape[1]).sum(0)

    there(x_refs, lat_ref, base)
    there(g_refs, gsh_ref, 0)
    every = [slice(low, low + COLUMNS) for low in range(0, 2 * p.lanes, COLUMNS)]
    lat = lat_ref[pl.ds(base, count), :]
    for columns in every:
        pre = mul(lat, w1_ref[:, columns])

        def first(at, kept, columns):
            hidden, slope = gelu_both(pre[at] + bias_ref[0:1, columns])
            hid_ref[kept, columns] = hidden.astype(half)
            slope_ref[at, columns] = slope

        bands(columns, first)
    hid = hid_ref[pl.ds(base, count), :]
    for columns in every:
        part = mul(hid, w2_ref[:, columns])
        sums = [jnp.zeros((8, COLUMNS), single)]

        def second(at, kept, columns):
            post = part[at] + bias_ref[1:2, columns]
            inner = jnp.tanh(post * (1.0 / shrink_level))
            shr_ref[at, columns] = (post - shrink_level * inner).astype(half)
            gpost = (gsh_ref[at, columns].astype(single) * (inner * inner)).astype(half)
            gpost_ref[kept, columns] = gpost
            sums[0] += folded(gpost.astype(single))

        bands(columns, second)
        gb_ref[8:16, columns] += sums[0]
    back(lambda rows, ri: shr_ref[rows, ri * p.lanes : (ri + 1) * p.lanes], turn_y_ref)
    gpost = gpost_ref[pl.ds(base, count), :]
    for columns in every:
        part = mul(gpost, w2_ref[columns, :], NT)
        sums = [jnp.zeros((8, COLUMNS), single)]

        def third(at, kept, columns):
            gpre = (part[at] * slope_ref[at, columns]).astype(half)
            gpre_ref[kept, columns] = gpre
            sums[0] += folded(gpre.astype(single))

        bands(columns, third)
        gb_ref[0:8, columns] += sums[0]
    gpre = gpre_ref[pl.ds(base, count), :]
    for columns in every:
        glat_ref[:, columns] = mul(gpre, w1_ref[columns, :], NT).astype(half)
    back(lambda rows, ri: glat_ref[rows, ri * p.lanes : (ri + 1) * p.lanes], turn_x_ref)

    @pl.when(group == pl.num_programs(1) - 1)
    def _():
        send_turn(p, turn_y_ref, y_refs, p.rows, 2 * p.modes, 0, me if y_near else None)
        send_turn(p, turn_x_ref, x_out_refs, p.rows, 2 * p.modes, 0, me if x_near else None)
        acc1_ref[...] += mul(lat_ref[...], gpre_ref[...], TN)
        acc2_ref[...] += mul(hid_ref[...], gpost_ref[...], TN)

    @pl.when((group == pl.num_programs(1) - 1) & (pack == pl.num_programs(0) - 1))
    def _():
        def keep(top, rows, value):
            at = slice(top, top + rows)
            if before_ref is not None:
                value = value + before_ref[at, :]
            total_ref[at, :] = value.astype(total_ref.dtype)

        place = 0
        for acc in (acc1_ref, acc2_ref):
            for part in range(2):
                for n in range(p.groups):
                    total = jnp.zeros((p.width, LANES), single)
                    for s in range(p.stack):
                        q = s * p.groups + n
                        for row_ri, col_ri, sign in PARTS[part]:
                            rows = slice(row_ri * p.lanes + q * p.width, row_ri * p.lanes + (q + 1) * p.width)

                            def read(tile):
                                left = col_ri * p.lanes + tile * LANES
                                return acc[rows, left : left + LANES]

                            total = total + sign * taken_slot(p, read, q)
                    keep(place, p.width, total)
                    place += p.width
        rows = []
        for which in range(2):
            sums = gb_ref[which * 8 : (which + 1) * 8, :].sum(0, keepdims=True)
            for ri in range(2):
                for n in range(p.groups):
                    row = jnp.zeros((1, LANES), single)
                    for s in range(p.stack):

                        def read(tile):
                            left = ri * p.lanes + tile * LANES
                            return sums[:, left : left + LANES]

                        row = row + taken_slot(p, read, s * p.groups + n)
                    rows.append(row)
        rows += [jnp.zeros((1, LANES), single)] * (-len(rows) % 8)
        keep(place, len(rows), jnp.concatenate(rows, axis=0))


def mixed_kernel(p, peers, *refs):
    rows_refs, (table_ref, out_ref, words_ref) = refs[:peers], refs[peers:]
    factor = 1.0 / math.sqrt(p.lon)

    def fetch(h):
        return mul(table_ref[...], peer_rows(p, rows_refs, h)) * factor

    pipelined(p, fetch, lambda h, tokens: scatter_row(p, tokens, words_ref.at[h], out_ref, h))


def slope_sums_kernel(p, peers, follows, *refs):
    stat_refs, refs = refs[: p.chan], refs[p.chan :]
    rows_in_refs, refs = refs[:peers], refs[peers:]
    tokens_ref, affine_ref, table_ref, wide_ref, sum_ref = refs[:5]
    refs = refs[5:]
    before_ref, refs = (refs[0], refs[1:]) if follows else (None, refs)
    sums_ref, total_ref, param_ref, rows_ref, dense_ref = refs
    factor = 1.0 / math.sqrt(p.lon)
    count = 2 * p.stack
    moments(p, stat_refs, rows_ref)

    @pl.when(first_step())
    def _():
        param_ref[...] = jnp.zeros_like(param_ref)

    def fetch(h):
        spectrum = mul(table_ref[...], peer_rows(p, rows_in_refs, h))
        return spectrum, expand(p, rows_ref[h], wide_ref)

    def use(h, fetched):
        folds = (PACK * p.turn_pad // 8, 8, LANES)
        plain, scaled = [], []
        spectrum, pairs = fetched
        for c, (mean, inverse) in enumerate(pairs):
            at = slice(c * LANES, (c + 1) * LANES)
            normed_grad = spectrum[:, at] * factor
            centred = (tokens_ref[0, h, :, at].astype(single) - mean) * inverse
            param_ref[0:8, at] += (normed_grad * centred).reshape(folds).sum(0)
            param_ref[8:16, at] += normed_grad.reshape(folds).sum(0)
            grad = normed_grad * affine_ref[0:1, at]
            plain.append(grad.astype(half))
            scaled.append((grad * centred).astype(half))
        sums = mul(sum_ref[0], jnp.concatenate(plain, axis=1), NT) + mul(
            sum_ref[1], jnp.concatenate(scaled, axis=1), NT
        )
        dense_ref[h * count : (h + 1) * count, :] = sums[:count]

    pipelined(p, fetch, use)
    sums_ref[0] = dense_ref[...].astype(half)

    @pl.when(last_step())
    def _():
        for kind in range(2):
            at = slice(kind, kind + 1)
            total = param_ref[8 * kind : 8 * kind + 8, :].sum(0, keepdims=True)
            if before_ref is not None:
                total = total + before_ref[0, at, :]
            for d in range(p.space):
                total_ref[d, at, :] = total


def input_grad_kernel(p, peers, *refs):
    stat_refs, part_refs, refs = refs[: p.chan], refs[p.chan : 2 * p.chan], refs[2 * p.chan :]
    rows_in_refs, refs = refs[:peers], refs[peers:]
    tokens_ref, affine_ref, table_ref, wide_ref, out_ref, rows_ref, part_ref, words_ref = refs
    factor = 1.0 / math.sqrt(p.lon)
    count = 2 * p.stack
    moments(p, stat_refs, rows_ref)
    total = part_refs[0][0].astype(single)
    for ref in part_refs[1:]:
        total = total + ref[0].astype(single)
    for h in range(p.step):
        part_ref[h, :count, :] = total[h * count : (h + 1) * count] * (1.0 / p.channels)
        if count < 8:
            part_ref[h, count:, :] = jnp.zeros((8 - count, p.turn_pad * PACK), single)

    def fetch(h):
        spectrum = mul(table_ref[...], peer_rows(p, rows_in_refs, h))
        return spectrum, expand(p, rows_ref[h], wide_ref), expand(p, part_ref[h], wide_ref)

    def use(h, fetched):
        spectrum, moment, means = fetched
        tiles = []
        for c in range(p.tiles):
            at = slice(c * LANES, (c + 1) * LANES)
            (mean, inverse), (first, second) = moment[c], means[c]
            centred = (tokens_ref[0, h, :, at].astype(single) - mean) * inverse
            grad = spectrum[:, at] * factor * affine_ref[0:1, at]
            tiles.append(inverse * (grad - first - centred * second))
        grad = jnp.concatenate(tiles, axis=1)
        scatter_row(p, grad, words_ref.at[h], out_ref, h)

    pipelined(p, fetch, use)


def whole_spec(value):
    dims = value.shape
    return pl.BlockSpec(dims, lambda *_: (0,) * len(dims))


def part_spec(p, value):
    dims = (1, value.shape[1] // p.steps) + value.shape[2:]
    return pl.BlockSpec(dims, lambda b, r: (b, r) + (0,) * (len(dims) - 2))


def peer_spec(value, which=0, wide=1):
    dims = (value.shape[0], wide, 1) + value.shape[3:]
    return pl.BlockSpec(dims, lambda b, *_: (0, which, b) + (0,) * (len(dims) - 3))


def peer_part_spec(p, value, which=0):
    dims = (value.shape[0], 1, 1, value.shape[3] // p.steps) + value.shape[4:]
    return pl.BlockSpec(dims, lambda b, r: (0, which, b, r) + (0,) * (len(dims) - 4))


def one_peer_spec(value, which=0):
    dims = (1, 1) + value.shape[2:]
    return pl.BlockSpec(dims, lambda b, *_: (which, b) + (0,) * (len(dims) - 2))


def one_peer_part_spec(p, value):
    dims = (1, 1, value.shape[2] // p.steps) + value.shape[3:]
    return pl.BlockSpec(dims, lambda b, r: (0, b, r) + (0,) * (len(dims) - 3))


def stored_spec(p, offset):
    return pl.BlockSpec((p.stack, p.step, p.groups, p.long), lambda b, r: (b + offset, r, 0, 0))


def call(body, grid, ins, in_specs, outs, out_specs, scratch, flops, aliases=None):
    moved = sum(v.size * v.dtype.itemsize for v in ins) + sum(
        math.prod(o.shape) * o.dtype.itemsize for o in outs
    )
    return _call(body, grid, ins, in_specs, outs, out_specs, scratch, flops, moved, aliases)


def _call(body, grid, ins, in_specs, outs, out_specs, scratch, flops, moved, aliases):
    return pl.pallas_call(
        body,
        grid=grid,
        in_specs=in_specs,
        out_specs=out_specs,
        out_shape=outs,
        scratch_shapes=scratch,
        input_output_aliases=aliases or {},
        compiler_params=pltpu.CompilerParams(vmem_limit_bytes=VMEM_LIMIT),
        cost_estimate=pl.CostEstimate(flops=flops, bytes_accessed=moved, transcendentals=0),
    )(*ins)


def lon_tables(p):
    cos_lon, sin_lon = trig(p.lon, MW)
    wave = np.concatenate([cos_lon, -sin_lon], axis=1)
    turned = np.zeros((PACK, p.turn_pad, 2 * MW), np.float32)
    turned[:, : p.turn] = wave.reshape(p.turn, PACK, 2 * MW).transpose(1, 0, 2)
    turned = turned.reshape(PACK * p.turn_pad, 2 * MW)
    doubling = np.where(np.arange(MW) == 0, 1.0, 2.0).astype(np.float32)
    factor = np.float32(1.0 / math.sqrt(p.lon))
    plain_scale = np.full((2 * MW, 1), factor, np.float32)
    double_scale = (factor * np.tile(doubling, 2))[:, None].astype(np.float32)
    owner = turned.reshape(-1, 2, p.space, p.modes).transpose(0, 2, 1, 3).reshape(-1, 2 * MW)
    twice = np.tile(doubling.reshape(p.space, 1, p.modes), (1, 2, 1)).reshape(1, 2 * MW)
    to_half = lambda value: jnp.asarray(value, half)
    return (
        to_half(turned.T),
        jnp.asarray(plain_scale),
        jnp.asarray(double_scale),
        owner * twice,
        owner,
    )


def by_distance(p, table, inner):
    at = np.arange(p.space * inner, dtype=np.int32)
    source = ((at // inner) ^ lax.axis_index("space").astype(jnp.int32)) * inner + at % inner
    chosen = (at[:, None] == source[None, :]).astype(half)
    return mul(jnp.asarray(table, half), chosen).astype(half)


def lat_tables(p):
    cos_lat, sin_lat = trig(p.lat, p.lat)
    there = np.block([[cos_lat, sin_lat], [-sin_lat, cos_lat]])
    there = there.reshape(2 * p.lat, 2, p.space, p.rows).transpose(0, 2, 1, 3)
    back = np.block([[cos_lat.T, -sin_lat.T], [sin_lat.T, cos_lat.T]])
    return there.reshape(2 * p.lat, 2 * p.lat), jnp.asarray(back, half)


def sum_tables(p):
    owner = np.arange(PACK) // p.groups
    lane_owner = np.repeat(owner, p.width)
    sums = np.zeros((2, 8, p.lanes), np.float32)
    wide = np.zeros((3, 8, 2, p.lanes), np.float32)
    for s in range(p.stack):
        sums[0, s] = lane_owner == s
        sums[1, p.stack + s] = lane_owner == s
        wide[:, s, 0] = lane_owner == s
        wide[:, p.stack + s, 1] = lane_owner == s
    wide = wide.reshape(24, 2, p.tiles, LANES).transpose(0, 2, 1, 3)
    return jnp.asarray(sums, half), jnp.asarray(wide.reshape(24, 2 * p.lanes), half)


def splits(space):
    return (MW // space) % 4 == 0 and space & (space - 1) == 0


def exchange_near(values):
    count = len(values)
    return tuple(
        value if x == 0 else lax.ppermute(value, "space", [(i, i ^ x) for i in range(count)])
        for x, value in enumerate(values)
    )


def exchange(value):
    return lax.all_to_all(value, "space", 0, 0, tiled=True)


def around(value, axis, size):
    gathered = [value]
    for step in range(1, size):
        gathered.append(
            lax.ppermute(value, axis, [(i, (i + step) % size) for i in range(size)])
        )
    return gathered


def reduced(p, value, kind):
    step = 1
    while step < p.space:
        wide = step > 1 and 4 * step <= p.space
        own = value.astype(kind)
        near, far, both = (
            lax.ppermute(own, "space", [(i, i ^ (step * k)) for i in range(p.space)])
            if k == 1 or wide
            else None
            for k in (1, 2, 3)
        )
        value = own.astype(single) + near.astype(single)
        if wide:
            value = value + (far.astype(single) + both.astype(single))
        step *= 4 if wide else 2
    return value


def on_device(space, chan, members, gain, shift, w_first, b_first, w_second, b_second, cotangent):
    p = Plan(members, w_first.shape[-1], space, chan)
    size = p.packs // 2
    grid = (size, p.steps)
    table, plain_scale, double_scale, mixed_plain, slope_plain = lon_tables(p)
    there_plain, back_table = lat_tables(p)
    slope_table, there_table = jnp.asarray(slope_plain, half), jnp.asarray(there_plain, half)
    mixed_table = jnp.asarray(mixed_plain, half)
    split = splits(space)
    if split:
        slope_near = by_distance(p, slope_plain, 2 * p.modes)
        mixed_near = by_distance(p, mixed_plain, 2 * p.modes)
        there_near = by_distance(p, there_plain, 2 * p.rows)
        me = lax.axis_index("space").astype(jnp.int32).reshape(1)
    own_spec = pl.BlockSpec(memory_space=pltpu.SMEM)
    sum_table, wide_table = sum_tables(p)
    affine = jnp.concatenate([gain] * p.stack + [shift] * p.stack).reshape(2, p.lanes)
    tokens_rows = PACK * p.turn_pad
    dft_flops = 2 * size * p.rows * tokens_rows * 2 * MW * p.lanes
    words = pltpu.VMEM((p.step, PACK, p.word_pad, LANES), single)
    lines = pltpu.VMEM((p.step, p.stack, p.word_pad * p.groups, LANES), single)
    turn_in = pltpu.VMEM((p.tiles, MW * 2 * p.rows, LANES), single)
    rows_scratch = pltpu.VMEM((p.step, 8, tokens_rows), single)

    def sent(wide):
        return jax.ShapeDtypeStruct((space, wide, size, p.modes, 2 * p.rows, p.lanes), half)

    returned = jax.ShapeDtypeStruct((space, 1, size, p.rows, 2 * p.modes, p.lanes), half)

    count = 2 * p.stack * p.rows
    stored = jax.ShapeDtypeStruct(members.shape, half)

    def out_call(body, ins, specs, outs, out_specs, scratch, flops, before):
        ins, specs = list(ins), list(specs)
        aliases = {}
        inner = body
        if before is not None:
            place, extra = len(ins), len(before)
            inner = lambda *refs: body(*refs[:place], *refs[place + extra :])
            ins += before
            specs += [pl.BlockSpec(memory_space=pl.ANY)] * extra
            aliases = {place + k: k for k in range(extra)}
        return call(inner, grid, tuple(ins), specs, outs, out_specs, scratch, flops, aliases)

    def spectra_out(wide, which, near):
        if near:
            one = jax.ShapeDtypeStruct(sent(wide).shape[1:], half)
            return [one] * space, [one_peer_spec(one, which)] * space
        return [sent(wide)], [peer_spec(sent(wide), which)]

    def cotangent_chunk(c, wide, near):
        outs, out_specs = spectra_out(wide, 0, near)
        ins, specs = (cotangent, table, double_scale), [whole_spec(table), whole_spec(double_scale)]
        if near:
            ins, specs = (*ins, me), [*specs, own_spec]
        return out_call(
            functools.partial(cotangent_kernel, p, near), ins,
            [stored_spec(p, c * size), *specs], outs, out_specs, [words, turn_in], dft_flops, None,
        )

    def stats_chunk(c):
        ins = (members, sum_table)
        outs = [
            jax.ShapeDtypeStruct((size, p.rows, tokens_rows, p.lanes), half),
            jax.ShapeDtypeStruct((size, count, tokens_rows), single),
        ]
        return call(
            functools.partial(stats_kernel, p), grid, ins,
            [stored_spec(p, c * size), whole_spec(sum_table)],
            outs, [part_spec(p, o) for o in outs], [words], dft_flops // 4,
        )

    def normalise_chunk(stats, tokens, before, near):
        tail = (affine, table, plain_scale, wide_table)
        ins = (*stats, tokens, *tail)
        specs = [part_spec(p, s) for s in (*stats, tokens)] + [whole_spec(v) for v in tail]
        if near:
            ins, specs = (*ins, me), [*specs, own_spec]
        which = 0 if before is None else 1
        outs, out_specs = spectra_out(which + 1, which, near)
        return out_call(
            functools.partial(normalise_kernel, p, near), ins, specs,
            outs, out_specs, [rows_scratch, turn_in], dft_flops, before,
        )

    step_modes = 2 if p.modes % 2 == 0 else 1
    wide_lanes = 2 * p.lanes

    def spectral_chunk(x_in, x_which, g_in, before, y_near, x_near):
        peers = len(x_in)
        tail = (there_near if peers > 1 else there_table, back_table)
        tail += (w_first, w_second, b_first, b_second)
        tail += () if before is None else (before,)
        specs = [whole_spec(v) for v in tail]
        if y_near or x_near:
            tail, specs = (*tail, me), [*specs, own_spec]

        def mode_spec(which):
            lead = (1, 1) if peers > 1 else (space, 1, 1)
            at = (which,) if peers > 1 else (0, which)
            return pl.BlockSpec(
                lead + (step_modes, 2 * p.rows, p.lanes), lambda b, m: at + (b, m, 0, 0)
            )

        outs, out_specs = [], []
        one = jax.ShapeDtypeStruct(returned.shape[1:], half)
        for near in (y_near, x_near):
            outs += [one] * space if near else [returned]
            out_specs += [one_peer_spec(one)] * space if near else [peer_spec(returned)]
        bias_rows = -(-4 * p.groups // 8) * 8
        totals = jax.ShapeDtypeStruct(
            (4 * p.groups * p.width + bias_rows, LANES), single if before is None else half
        )
        kept = pltpu.VMEM((p.modes * p.lat, wide_lanes), half)
        held = pltpu.VMEM((step_modes * p.lat, wide_lanes), single)
        brief = pltpu.VMEM((step_modes * p.lat, wide_lanes), half)
        turn_out = pltpu.VMEM((p.tiles, p.lat * 2 * p.modes, LANES), single)
        return call(
            functools.partial(
                spectral_kernel, p, step_modes, peers, y_near, x_near, before is not None
            ),
            (size, p.modes // step_modes), (*x_in, *g_in, *tail),
            [mode_spec(x_which)] * peers + [mode_spec(0)] * peers + specs,
            [*outs, totals],
            [*out_specs, whole_spec(totals)],
            [pltpu.VMEM((16, wide_lanes), single), pltpu.VMEM((2, wide_lanes), single)]
            + [kept] * 4 + [held] + [brief] * 3 + [turn_out] * 2
            + [pltpu.VMEM((wide_lanes, wide_lanes), single)] * 2
            + [pltpu.VMEM((wide_lanes, wide_lanes), half)] * 2,
            12 * size * p.modes * p.lat * wide_lanes * wide_lanes,
        )

    def mixed_chunk(c, rows_in, before):
        table_in = mixed_near if len(rows_in) > 1 else mixed_table
        return out_call(
            functools.partial(mixed_kernel, p, len(rows_in)), (*rows_in, table_in),
            rows_specs(rows_in) + [whole_spec(table_in)],
            [stored], [stored_spec(p, c * size)], [lines], dft_flops, before,
        )

    def rows_specs(rows_in):
        if len(rows_in) == 1:
            return [peer_part_spec(p, rows_in[0])]
        return [one_peer_part_spec(p, value) for value in rows_in]

    def slope_sums_chunk(stats, rows_in, tokens, before):
        near = len(rows_in) > 1
        tail = (affine, slope_near if near else slope_table, wide_table, sum_table)
        tail += () if before is None else (before,)
        outs = [
            jax.ShapeDtypeStruct((size, count, tokens_rows), half),
            jax.ShapeDtypeStruct((space, 2, p.lanes), single),
        ]
        return call(
            functools.partial(slope_sums_kernel, p, len(rows_in), before is not None),
            grid, (*stats, *rows_in, tokens, *tail),
            [part_spec(p, s) for s in stats] + rows_specs(rows_in)
            + [part_spec(p, tokens)] + [whole_spec(v) for v in tail],
            outs, [part_spec(p, outs[0]), whole_spec(outs[1])],
            [
                pltpu.VMEM((16, p.lanes), single), rows_scratch,
                pltpu.VMEM((count // p.steps, tokens_rows), single),
            ],
            dft_flops,
        )

    def input_grad_chunk(c, stats, parts, rows_in, tokens, before):
        near = len(rows_in) > 1
        tail = (affine, slope_near if near else slope_table, wide_table)
        return out_call(
            functools.partial(input_grad_kernel, p, len(rows_in)),
            (*stats, *parts, *rows_in, tokens, *tail),
            [part_spec(p, s) for s in (*stats, *parts)] + rows_specs(rows_in)
            + [part_spec(p, tokens)] + [whole_spec(v) for v in tail],
            [stored], [stored_spec(p, c * size)], [rows_scratch, rows_scratch, lines], dft_flops,
            before,
        )

    def channel_sums(value):
        return around(value, "chan", chan)

    def moved(values, near):
        return exchange_near(values) if near else (exchange(values[0]),)

    g0 = moved(cotangent_chunk(0, 1, False), False)
    tokens0, sums = stats_chunk(0)
    stats0 = channel_sums(sums)
    x0 = moved(normalise_chunk(stats0, tokens0, None, False), False)
    both1 = cotangent_chunk(1, 2, split)
    tokens1, sums = stats_chunk(1)
    stats1 = channel_sums(sums)
    both1 = moved(normalise_chunk(stats1, tokens1, both1, split), split)
    cut = space if split else 1
    *outs, totals = spectral_chunk(x0, 0, g0, None, split, False)
    dx0 = moved(outs[cut:], False)
    y0 = moved(outs[:cut], split)
    *outs, totals = spectral_chunk(both1, 1, both1, totals, False, split)
    dx1 = moved(outs[1:], split)
    y1 = moved(outs[:1], False)
    sums, params = slope_sums_chunk(stats0, dx0, tokens0, None)
    parts = channel_sums(sums)
    grad_input = input_grad_chunk(0, stats0, parts, dx0, tokens0, None)
    mixed = mixed_chunk(0, y0, None)
    sums, params = slope_sums_chunk(stats1, dx1, tokens1, params)
    parts = channel_sums(sums)
    grad_input = input_grad_chunk(1, stats1, parts, dx1, tokens1, grad_input)[0]
    mixed = mixed_chunk(1, y1, mixed)[0]

    size_w = p.groups * p.width
    flat = reduced(p, totals, half)[:, : p.width]
    grads = flat[: 4 * size_w].reshape((2,) + w_first.shape)
    bias_grads = flat[4 * size_w : 4 * size_w + 4 * p.groups].reshape((2,) + b_first.shape)
    params = exchange(params).sum(0)
    params = [
        sum(params[kind, s * size_w : (s + 1) * size_w] for s in range(p.stack)) for kind in range(2)
    ]
    return (
        mixed, grad_input, grads[0], bias_grads[0], grads[1], bias_grads[1], params[0], params[1]
    )


def solution(mesh):
    tokens = P(None, "space", "chan", None)
    weights = P(None, "chan", None, None)
    biases = P(None, "chan", None)
    placed = (tokens, P("chan"), P("chan"), weights, biases, weights, biases, tokens)
    return jax.shard_map(
        functools.partial(on_device, mesh.shape["space"], mesh.shape["chan"]),
        mesh=mesh,
        in_specs=placed,
        out_specs=(tokens, tokens, weights, biases, weights, biases, P("chan"), P("chan")),
        check_vma=False,
    )
```

```python
import functools
import math

import jax
import jax.numpy as jnp
import numpy as np
from jax import lax
from jax.experimental import pallas as pl
from jax.experimental.pallas import tpu as pltpu
from jax.sharding import PartitionSpec as P


MW = 64
LANES = 128
PACK = 4

shrink_level = 0.05
norm_epsilon = 1e-05
gelu_scale = 0.7978845608
gelu_cubic = 0.044715

half = jnp.bfloat16
single = jnp.float32
VMEM_LIMIT = 67043328
SLOTS = 4

TN = (((0,), (0,)), ((), ()))
NT = (((1,), (1,)), ((), ()))


def mul(first_op, second_op, dims=(((1,), (0,)), ((), ()))):
    return lax.dot_general(first_op, second_op, dims, preferred_element_type=single)


def trig(length, columns):
    angles = (np.arange(length)[:, None] * np.arange(columns)[None, :] % length).astype(np.float32)
    angles = (angles * np.float32(2.0 * math.pi / length)).astype(np.float64)
    cast = lambda table: table.astype(np.float32).astype(half).astype(np.float32)
    return cast(np.cos(angles)), cast(np.sin(angles))


class Plan:
    def __init__(self, members, width, space, chan):
        self.batch, self.rows, self.groups, self.long = members.shape
        self.width, self.space, self.chan = width, space, chan
        self.lon = self.long // width
        self.lat = self.rows * space
        self.modes = MW // space
        self.stack = PACK // self.groups
        self.packs = self.batch // self.stack
        self.lanes = PACK * width
        self.tiles = self.lanes // LANES
        self.turn = self.lon // PACK
        self.turn_pad = -(-self.turn // 16) * 16
        self.words = self.long // LANES
        self.step = SLOTS if self.rows % SLOTS == 0 else self.rows
        self.steps = self.rows // self.step
        self.word_pad = self.tiles * self.turn_pad
        self.channels = self.groups * width * chan


def moved_lanes(p, fetch, from_start, to_start, tile):
    pieces = []
    for slot in range(PACK):
        low = max(to_start(slot), tile * LANES)
        high = min(to_start(slot) + p.width, (tile + 1) * LANES)
        at = low
        while at < high:
            source = at - to_start(slot) + from_start(slot)
            stop = min(high, at + LANES - source % LANES)
            shift = (at - source) % LANES
            pieces.append((stop - tile * LANES, fetch(slot, source // LANES, shift)))
            at = stop
    return pieces


def merged(pieces, lane):
    value = pieces[-1][1]
    for stop, piece in reversed(pieces[:-1]):
        value = jnp.where(lane < stop, piece, value)
    return value


def rolled(value, shift):
    return value if shift == 0 else pltpu.roll(value, shift, 1)


def spread(p, stored_ref, words_ref, h):
    for q in range(PACK):
        line = stored_ref[q // p.groups, h, q % p.groups, :]
        words_ref[q, : p.words, :] = line.reshape(p.words, LANES).astype(single)


def gather_row(p, words_ref):
    lane = lax.broadcasted_iota(jnp.int32, (p.turn_pad, LANES), 1)
    source = {}
    for q in range(PACK):
        for i in range(p.tiles):
            source[q, i] = words_ref[q, pl.ds(i, p.turn_pad, stride=p.tiles), :]
    rows = []
    for r in range(PACK):
        cache = {}

        def fetch(q, i, shift):
            key = (q, i, shift)
            if key not in cache:
                cache[key] = rolled(source[q, i], shift)
            return cache[key]

        tiles = []
        for c in range(p.tiles):
            pieces = moved_lanes(p, fetch, lambda q: r * p.width, lambda q: q * p.width, c)
            tiles.append(merged(pieces, lane).astype(half))
        rows.append(jnp.concatenate(tiles, axis=1))
    return jnp.concatenate(rows, axis=0)


def scatter_row(p, tokens, words_ref, stored_ref, h):
    lane = lax.broadcasted_iota(jnp.int32, (p.turn_pad, LANES), 1)
    for q in range(PACK):
        s, n = divmod(q, p.groups)
        cache = {}

        def fetch(r, c, shift):
            if (r, c, shift) not in cache:
                part = tokens[r * p.turn_pad : (r + 1) * p.turn_pad, c * LANES : (c + 1) * LANES]
                cache[r, c, shift] = rolled(part, shift)
            return cache[r, c, shift]

        for i in range(p.tiles):
            pieces = moved_lanes(p, fetch, lambda r: q * p.width, lambda r: r * p.width, i)
            at = pl.ds(i * p.groups + n, p.turn_pad, stride=p.tiles * p.groups)
            words_ref[s, at, :] = merged(pieces, lane)
    for s in range(p.stack):
        lines = words_ref[s, : p.words * p.groups, :].astype(half)
        for t in range(p.words):
            stored_ref[s, h, :, t * LANES : (t + 1) * LANES] = lines[
                t * p.groups : (t + 1) * p.groups, :
            ]


def clear_tail(p, words_ref):
    @pl.when(first_step())
    def _():
        tail = p.word_pad - p.words
        words_ref[:, :, p.words :, :] = jnp.zeros(words_ref.shape[:2] + (tail, LANES), single)


def pipelined(p, fetch, use):
    ahead = fetch(0)
    for h in range(p.step):
        now, ahead = ahead, fetch(h + 1) if h + 1 < p.step else None
        use(h, now)


def first_step():
    return (pl.program_id(0) == 0) & (pl.program_id(1) == 0)


def last_step():
    return (pl.program_id(0) == pl.num_programs(0) - 1) & (
        pl.program_id(1) == pl.num_programs(1) - 1
    )


def last_part():
    return pl.program_id(1) == pl.num_programs(1) - 1


def analyse(p, tokens, table, scale, turn_ref, h):
    h = pl.program_id(1) * p.step + h
    spectrum = mul(table, tokens) * scale
    for c in range(p.tiles):
        for ri in range(2):
            turn_ref[c, pl.ds(ri * p.rows + h, MW, stride=2 * p.rows), :] = spectrum[
                ri * MW : (ri + 1) * MW, c * LANES : (c + 1) * LANES
            ]


def send_turn(p, turn_ref, out_refs, outer, inner, which=0, me=None):
    count = outer * inner
    for x in range(p.space):
        for c in range(p.tiles):
            lanes = slice(c * LANES, (c + 1) * LANES)
            if me is None:
                part = turn_ref[c, x * count : (x + 1) * count, :]
                out_refs[0][x, which, 0, :, :, lanes] = part.reshape(outer, inner, LANES).astype(half)
            else:
                at = pl.ds(pl.multiple_of((me ^ x) * count, 8), count)
                part = turn_ref[c, at, :]
                out_refs[x][which, 0, :, :, lanes] = part.reshape(outer, inner, LANES).astype(half)


def peer_rows(p, refs, i):
    if len(refs) == 1:
        return refs[0][:, 0, 0, i].reshape(-1, p.lanes)
    return jnp.concatenate([ref[0, 0, i] for ref in refs], axis=0)


def split_three(value):
    high = value.astype(half).astype(single)
    rest = value - high
    middle = rest.astype(half).astype(single)
    return high, middle, rest - middle


def expand(p, parts, wide_ref):
    stacked = jnp.concatenate(split_three(parts), axis=0).astype(half)
    pairs = []
    for c in range(p.tiles):
        both = mul(stacked, wide_ref[:, 2 * c * LANES : 2 * (c + 1) * LANES], TN)
        pairs.append((both[:, :LANES], both[:, LANES:]))
    return pairs


def summed(table, value):
    high = value.astype(half)
    low = (value - high.astype(single)).astype(half)
    return mul(table, high, NT) + mul(table, low, NT)


def cotangent_kernel(p, split, stored_ref, table_ref, scale_ref, *refs):
    me, refs = (refs[0][0], refs[1:]) if split else (None, refs)
    out_refs, (words_ref, turn_ref) = refs[:-2], refs[-2:]
    clear_tail(p, words_ref)

    def fetch(h):
        spread(p, stored_ref, words_ref.at[h], h)
        return gather_row(p, words_ref.at[h])

    def use(h, tokens):
        analyse(p, tokens, table_ref[...], scale_ref[...], turn_ref, h)

    pipelined(p, fetch, use)

    @pl.when(last_part())
    def _():
        send_turn(p, turn_ref, out_refs, p.modes, 2 * p.rows, 0, me)


def stats_kernel(p, stored_ref, sum_ref, tokens_ref, stat_ref, words_ref):
    clear_tail(p, words_ref)
    count = 2 * p.stack

    def fetch(h):
        spread(p, stored_ref, words_ref.at[h], h)
        return gather_row(p, words_ref.at[h])

    def use(h, tokens):
        tokens_ref[0, h] = tokens
        wide = tokens.astype(single)
        rows = mul(sum_ref[0], tokens, NT) + summed(sum_ref[1], wide * wide)
        stat_ref[0, h * count : (h + 1) * count, :] = rows[:count]

    pipelined(p, fetch, use)


def moments(p, stat_refs, rows_ref):
    count = 2 * p.stack
    total = stat_refs[0][0]
    for ref in stat_refs[1:]:
        total = total + ref[0]
    for h in range(p.step):
        part = total[h * count : (h + 1) * count] * (1.0 / p.channels)
        mean, square = part[: p.stack], part[p.stack :]
        inverse = lax.rsqrt(square - mean * mean + norm_epsilon)
        rows_ref[h, : p.stack, :] = mean
        rows_ref[h, p.stack : count, :] = inverse
        if count < 8:
            rows_ref[h, count:, :] = jnp.zeros((8 - count, p.turn_pad * PACK), single)


def normalise_kernel(p, split, *refs):
    stat_refs = refs[: p.chan]
    tokens_ref, affine_ref, table_ref, wide_ref = refs[p.chan : p.chan + 4]
    refs = refs[p.chan + 4 :]
    me, refs = (refs[0][0], refs[1:]) if split else (None, refs)
    out_refs, (rows_ref, turn_ref) = refs[:-2], refs[-2:]
    moments(p, stat_refs, rows_ref)

    def use(h, pairs):
        tiles = []
        for c, (mean, inverse) in enumerate(pairs):
            at = slice(c * LANES, (c + 1) * LANES)
            centred = (tokens_ref[0, h, :, at].astype(single) - mean) * inverse
            tiles.append((centred * affine_ref[0:1, at] + affine_ref[1:2, at]).astype(half))
        normed = jnp.concatenate(tiles, axis=1)
        analyse(p, normed, table_ref[...], 1.0 / math.sqrt(p.lon), turn_ref, h)

    pipelined(p, lambda h: expand(p, rows_ref[h], wide_ref), use)

    @pl.when(last_part())
    def _():
        send_turn(p, turn_ref, out_refs, p.modes, 2 * p.rows, 0, me)


def gelu_both(values):
    square = values * values
    inner = jnp.tanh(values * (gelu_scale + gelu_scale * gelu_cubic * square))
    upper = 0.5 + 0.5 * inner
    hidden = values * upper
    slope = upper + hidden * (1.0 - upper) * (
        2.0 * gelu_scale + 6.0 * gelu_scale * gelu_cubic * square
    )
    return hidden, slope


BAND = 32
COLUMNS = 256


def widened(p, value):
    blank = jnp.zeros((value.shape[0], LANES - p.width), single)
    return jnp.concatenate([value.astype(single), blank], axis=1)


def placed_slot(p, value, q):
    lane = lax.broadcasted_iota(jnp.int32, value.shape, 1)
    at, shift = divmod(q * p.width, LANES)
    turned = rolled(value, shift)
    tiles = [jnp.zeros_like(value) for _ in range(p.tiles)]
    tiles[at] = jnp.where(lane >= shift, turned, 0.0)
    if shift + p.width > LANES:
        tiles[at + 1] = jnp.where(lane < shift + p.width - LANES, turned, 0.0)
    return jnp.concatenate(tiles, axis=1)


def taken_slot(p, read, q):
    at, shift = divmod(q * p.width, LANES)
    value = rolled(read(at), -shift % LANES)
    if shift + p.width > LANES:
        lane = lax.broadcasted_iota(jnp.int32, value.shape, 1)
        value = jnp.where(lane < LANES - shift, value, rolled(read(at + 1), -shift % LANES))
    return value


PARTS = (((0, 0, 1), (1, 1, 1)), ((0, 1, 1), (1, 0, -1)))


def place_weights(p, w_refs, out_refs):
    for w_ref, out_ref in zip(w_refs, out_refs):
        for q in range(PACK):
            for part in range(2):
                wide = placed_slot(p, widened(p, w_ref[part, q % p.groups]), q)
                for row_ri, col_ri, sign in PARTS[part]:
                    top = row_ri * p.lanes + q * p.width
                    out_ref[top : top + p.width, col_ri * p.lanes : (col_ri + 1) * p.lanes] = (
                        sign * wide
                    ).astype(half)


def place_biases(p, b_refs, out_ref):
    for which, b_ref in enumerate(b_refs):
        for ri in range(2):
            row = jnp.zeros((1, p.lanes), single)
            for q in range(PACK):
                n = q % p.groups
                row = row + placed_slot(p, widened(p, b_ref[ri, n : n + 1, :]), q)
            out_ref[which : which + 1, ri * p.lanes : (ri + 1) * p.lanes] = row


def spectral_kernel(p, step_modes, peers, y_near, x_near, follows, *refs):
    x_refs, g_refs, refs = refs[:peers], refs[peers : 2 * peers], refs[2 * peers :]
    there_ref, back_ref, w_first_ref, w_second_ref, b_first_ref, b_second_ref = refs[:6]
    refs = refs[6:]
    before_ref, refs = (refs[0], refs[1:]) if follows else (None, refs)
    me, refs = (refs[0][0], refs[1:]) if y_near or x_near else (None, refs)
    y_count, x_count = (p.space if near else 1 for near in (y_near, x_near))
    y_refs, x_out_refs, refs = refs[:y_count], refs[y_count : y_count + x_count], refs[y_count + x_count :]
    (
        total_ref,
        gb_ref,
        bias_ref,
        lat_ref,
        hid_ref,
        gpost_ref,
        gpre_ref,
        slope_ref,
        gsh_ref,
        shr_ref,
        glat_ref,
        turn_y_ref,
        turn_x_ref,
        acc1_ref,
        acc2_ref,
        w1_ref,
        w2_ref,
    ) = refs
    pack, group = pl.program_id(0), pl.program_id(1)
    count = step_modes * p.lat
    factor = 1.0 / math.sqrt(p.lat)
    base = pl.multiple_of(group * count, count)

    @pl.when((pack == 0) & (group == 0))
    def _():
        place_weights(p, (w_first_ref, w_second_ref), (w1_ref, w2_ref))
        place_biases(p, (b_first_ref, b_second_ref), bias_ref)
        gb_ref[...] = jnp.zeros_like(gb_ref)
        acc1_ref[...] = jnp.zeros_like(acc1_ref)
        acc2_ref[...] = jnp.zeros_like(acc2_ref)

    def there(refs, into, offset):
        for m in range(step_modes):
            block = peer_rows(p, refs, m)
            out = (mul(there_ref[...], block) * factor).astype(half)
            at = pl.ds(offset + m * p.lat, p.lat)
            into[at, : p.lanes] = out[: p.lat]
            into[at, p.lanes :] = out[p.lat :]

    def back(value_of, turn_ref):
        for m in range(step_modes):
            rows = slice(m * p.lat, (m + 1) * p.lat)
            both = jnp.concatenate([value_of(rows, 0), value_of(rows, 1)], axis=0)
            out = mul(back_ref[...], both) * factor
            mode = group * step_modes + m
            for ri in range(2):
                for c in range(p.tiles):
                    turn_ref[c, pl.ds(ri * p.modes + mode, p.lat, stride=2 * p.modes), :] = out[
                        ri * p.lat : (ri + 1) * p.lat, c * LANES : (c + 1) * LANES
                    ]

    def bands(columns, body):
        for low in range(0, count, BAND):
            at = slice(low, low + BAND)
            body(at, pl.ds(pl.multiple_of(base + low, BAND), BAND), columns)

    def folded(value):
        return value.reshape(BAND // 8, 8, value.shape[1]).sum(0)

    there(x_refs, lat_ref, base)
    there(g_refs, gsh_ref, 0)
    every = [slice(low, low + COLUMNS) for low in range(0, 2 * p.lanes, COLUMNS)]
    lat = lat_ref[pl.ds(base, count), :]
    for columns in every:
        pre = mul(lat, w1_ref[:, columns])

        def first(at, kept, columns):
            hidden, slope = gelu_both(pre[at] + bias_ref[0:1, columns])
            hid_ref[kept, columns] = hidden.astype(half)
            slope_ref[at, columns] = slope

        bands(columns, first)
    hid = hid_ref[pl.ds(base, count), :]
    for columns in every:
        part = mul(hid, w2_ref[:, columns])
        sums = [jnp.zeros((8, COLUMNS), single)]

        def second(at, kept, columns):
            post = part[at] + bias_ref[1:2, columns]
            inner = jnp.tanh(post * (1.0 / shrink_level))
            shr_ref[at, columns] = (post - shrink_level * inner).astype(half)
            gpost = (gsh_ref[at, columns].astype(single) * (inner * inner)).astype(half)
            gpost_ref[kept, columns] = gpost
            sums[0] += folded(gpost.astype(single))

        bands(columns, second)
        gb_ref[8:16, columns] += sums[0]
    back(lambda rows, ri: shr_ref[rows, ri * p.lanes : (ri + 1) * p.lanes], turn_y_ref)
    gpost = gpost_ref[pl.ds(base, count), :]
    for columns in every:
        part = mul(gpost, w2_ref[columns, :], NT)
        sums = [jnp.zeros((8, COLUMNS), single)]

        def third(at, kept, columns):
            gpre = (part[at] * slope_ref[at, columns]).astype(half)
            gpre_ref[kept, columns] = gpre
            sums[0] += folded(gpre.astype(single))

        bands(columns, third)
        gb_ref[0:8, columns] += sums[0]
    gpre = gpre_ref[pl.ds(base, count), :]
    for columns in every:
        glat_ref[:, columns] = mul(gpre, w1_ref[columns, :], NT).astype(half)
    back(lambda rows, ri: glat_ref[rows, ri * p.lanes : (ri + 1) * p.lanes], turn_x_ref)

    @pl.when(group == pl.num_programs(1) - 1)
    def _():
        send_turn(p, turn_y_ref, y_refs, p.rows, 2 * p.modes, 0, me if y_near else None)
        send_turn(p, turn_x_ref, x_out_refs, p.rows, 2 * p.modes, 0, me if x_near else None)
        acc1_ref[...] += mul(lat_ref[...], gpre_ref[...], TN)
        acc2_ref[...] += mul(hid_ref[...], gpost_ref[...], TN)

    @pl.when((group == pl.num_programs(1) - 1) & (pack == pl.num_programs(0) - 1))
    def _():
        def keep(top, rows, value):
            at = slice(top, top + rows)
            if before_ref is not None:
                value = value + before_ref[at, :]
            total_ref[at, :] = value.astype(total_ref.dtype)

        place = 0
        for acc in (acc1_ref, acc2_ref):
            for part in range(2):
                for n in range(p.groups):
                    total = jnp.zeros((p.width, LANES), single)
                    for s in range(p.stack):
                        q = s * p.groups + n
                        for row_ri, col_ri, sign in PARTS[part]:
                            rows = slice(row_ri * p.lanes + q * p.width, row_ri * p.lanes + (q + 1) * p.width)

                            def read(tile):
                                left = col_ri * p.lanes + tile * LANES
                                return acc[rows, left : left + LANES]

                            total = total + sign * taken_slot(p, read, q)
                    keep(place, p.width, total)
                    place += p.width
        rows = []
        for which in range(2):
            sums = gb_ref[which * 8 : (which + 1) * 8, :].sum(0, keepdims=True)
            for ri in range(2):
                for n in range(p.groups):
                    row = jnp.zeros((1, LANES), single)
                    for s in range(p.stack):

                        def read(tile):
                            left = ri * p.lanes + tile * LANES
                            return sums[:, left : left + LANES]

                        row = row + taken_slot(p, read, s * p.groups + n)
                    rows.append(row)
        rows += [jnp.zeros((1, LANES), single)] * (-len(rows) % 8)
        keep(place, len(rows), jnp.concatenate(rows, axis=0))


def mixed_kernel(p, peers, *refs):
    rows_refs, (table_ref, out_ref, words_ref) = refs[:peers], refs[peers:]
    factor = 1.0 / math.sqrt(p.lon)

    def fetch(h):
        return mul(table_ref[...], peer_rows(p, rows_refs, h)) * factor

    pipelined(p, fetch, lambda h, tokens: scatter_row(p, tokens, words_ref.at[h], out_ref, h))


def slope_sums_kernel(p, peers, follows, *refs):
    stat_refs, refs = refs[: p.chan], refs[p.chan :]
    rows_in_refs, refs = refs[:peers], refs[peers:]
    tokens_ref, affine_ref, table_ref, wide_ref, sum_ref = refs[:5]
    refs = refs[5:]
    before_ref, refs = (refs[0], refs[1:]) if follows else (None, refs)
    sums_ref, total_ref, param_ref, rows_ref, dense_ref = refs
    factor = 1.0 / math.sqrt(p.lon)
    count = 2 * p.stack
    moments(p, stat_refs, rows_ref)

    @pl.when(first_step())
    def _():
        param_ref[...] = jnp.zeros_like(param_ref)

    def fetch(h):
        spectrum = mul(table_ref[...], peer_rows(p, rows_in_refs, h))
        return spectrum, expand(p, rows_ref[h], wide_ref)

    def use(h, fetched):
        folds = (PACK * p.turn_pad // 8, 8, LANES)
        plain, scaled = [], []
        spectrum, pairs = fetched
        for c, (mean, inverse) in enumerate(pairs):
            at = slice(c * LANES, (c + 1) * LANES)
            normed_grad = spectrum[:, at] * factor
            centred = (tokens_ref[0, h, :, at].astype(single) - mean) * inverse
            param_ref[0:8, at] += (normed_grad * centred).reshape(folds).sum(0)
            param_ref[8:16, at] += normed_grad.reshape(folds).sum(0)
            grad = normed_grad * affine_ref[0:1, at]
            plain.append(grad.astype(half))
            scaled.append((grad * centred).astype(half))
        sums = mul(sum_ref[0], jnp.concatenate(plain, axis=1), NT) + mul(
            sum_ref[1], jnp.concatenate(scaled, axis=1), NT
        )
        dense_ref[h * count : (h + 1) * count, :] = sums[:count]

    pipelined(p, fetch, use)
    sums_ref[0] = dense_ref[...].astype(half)

    @pl.when(last_step())
    def _():
        for kind in range(2):
            at = slice(kind, kind + 1)
            total = param_ref[8 * kind : 8 * kind + 8, :].sum(0, keepdims=True)
            if before_ref is not None:
                total = total + before_ref[0, at, :]
            for d in range(p.space):
                total_ref[d, at, :] = total


def input_grad_kernel(p, peers, *refs):
    stat_refs, part_refs, refs = refs[: p.chan], refs[p.chan : 2 * p.chan], refs[2 * p.chan :]
    rows_in_refs, refs = refs[:peers], refs[peers:]
    tokens_ref, affine_ref, table_ref, wide_ref, out_ref, rows_ref, part_ref, words_ref = refs
    factor = 1.0 / math.sqrt(p.lon)
    count = 2 * p.stack
    moments(p, stat_refs, rows_ref)
    total = part_refs[0][0].astype(single)
    for ref in part_refs[1:]:
        total = total + ref[0].astype(single)
    for h in range(p.step):
        part_ref[h, :count, :] = total[h * count : (h + 1) * count] * (1.0 / p.channels)
        if count < 8:
            part_ref[h, count:, :] = jnp.zeros((8 - count, p.turn_pad * PACK), single)

    def fetch(h):
        spectrum = mul(table_ref[...], peer_rows(p, rows_in_refs, h))
        return spectrum, expand(p, rows_ref[h], wide_ref), expand(p, part_ref[h], wide_ref)

    def use(h, fetched):
        spectrum, moment, means = fetched
        tiles = []
        for c in range(p.tiles):
            at = slice(c * LANES, (c + 1) * LANES)
            (mean, inverse), (first, second) = moment[c], means[c]
            centred = (tokens_ref[0, h, :, at].astype(single) - mean) * inverse
            grad = spectrum[:, at] * factor * affine_ref[0:1, at]
            tiles.append(inverse * (grad - first - centred * second))
        grad = jnp.concatenate(tiles, axis=1)
        scatter_row(p, grad, words_ref.at[h], out_ref, h)

    pipelined(p, fetch, use)


def whole_spec(value):
    dims = value.shape
    return pl.BlockSpec(dims, lambda *_: (0,) * len(dims))


def part_spec(p, value):
    dims = (1, value.shape[1] // p.steps) + value.shape[2:]
    return pl.BlockSpec(dims, lambda b, r: (b, r) + (0,) * (len(dims) - 2))


def peer_spec(value, which=0, wide=1):
    dims = (value.shape[0], wide, 1) + value.shape[3:]
    return pl.BlockSpec(dims, lambda b, *_: (0, which, b) + (0,) * (len(dims) - 3))


def peer_part_spec(p, value, which=0):
    dims = (value.shape[0], 1, 1, value.shape[3] // p.steps) + value.shape[4:]
    return pl.BlockSpec(dims, lambda b, r: (0, which, b, r) + (0,) * (len(dims) - 4))


def one_peer_spec(value, which=0):
    dims = (1, 1) + value.shape[2:]
    return pl.BlockSpec(dims, lambda b, *_: (which, b) + (0,) * (len(dims) - 2))


def one_peer_part_spec(p, value):
    dims = (1, 1, value.shape[2] // p.steps) + value.shape[3:]
    return pl.BlockSpec(dims, lambda b, r: (0, b, r) + (0,) * (len(dims) - 3))


def stored_spec(p, offset):
    return pl.BlockSpec((p.stack, p.step, p.groups, p.long), lambda b, r: (b + offset, r, 0, 0))


def call(body, grid, ins, in_specs, outs, out_specs, scratch, flops, aliases=None):
    moved = sum(v.size * v.dtype.itemsize for v in ins) + sum(
        math.prod(o.shape) * o.dtype.itemsize for o in outs
    )
    return _call(body, grid, ins, in_specs, outs, out_specs, scratch, flops, moved, aliases)


def _call(body, grid, ins, in_specs, outs, out_specs, scratch, flops, moved, aliases):
    return pl.pallas_call(
        body,
        grid=grid,
        in_specs=in_specs,
        out_specs=out_specs,
        out_shape=outs,
        scratch_shapes=scratch,
        input_output_aliases=aliases or {},
        compiler_params=pltpu.CompilerParams(vmem_limit_bytes=VMEM_LIMIT),
        cost_estimate=pl.CostEstimate(flops=flops, bytes_accessed=moved, transcendentals=0),
    )(*ins)


def lon_tables(p):
    cos_lon, sin_lon = trig(p.lon, MW)
    wave = np.concatenate([cos_lon, -sin_lon], axis=1)
    turned = np.zeros((PACK, p.turn_pad, 2 * MW), np.float32)
    turned[:, : p.turn] = wave.reshape(p.turn, PACK, 2 * MW).transpose(1, 0, 2)
    turned = turned.reshape(PACK * p.turn_pad, 2 * MW)
    doubling = np.where(np.arange(MW) == 0, 1.0, 2.0).astype(np.float32)
    factor = np.float32(1.0 / math.sqrt(p.lon))
    plain_scale = np.full((2 * MW, 1), factor, np.float32)
    double_scale = (factor * np.tile(doubling, 2))[:, None].astype(np.float32)
    owner = turned.reshape(-1, 2, p.space, p.modes).transpose(0, 2, 1, 3).reshape(-1, 2 * MW)
    twice = np.tile(doubling.reshape(p.space, 1, p.modes), (1, 2, 1)).reshape(1, 2 * MW)
    to_half = lambda value: jnp.asarray(value, half)
    return (
        to_half(turned.T),
        jnp.asarray(plain_scale),
        jnp.asarray(double_scale),
        owner * twice,
        owner,
    )


def by_distance(p, table, inner):
    at = np.arange(p.space * inner, dtype=np.int32)
    source = ((at // inner) ^ lax.axis_index("space").astype(jnp.int32)) * inner + at % inner
    chosen = (at[:, None] == source[None, :]).astype(half)
    return mul(jnp.asarray(table, half), chosen).astype(half)


def lat_tables(p):
    cos_lat, sin_lat = trig(p.lat, p.lat)
    there = np.block([[cos_lat, sin_lat], [-sin_lat, cos_lat]])
    there = there.reshape(2 * p.lat, 2, p.space, p.rows).transpose(0, 2, 1, 3)
    back = np.block([[cos_lat.T, -sin_lat.T], [sin_lat.T, cos_lat.T]])
    return there.reshape(2 * p.lat, 2 * p.lat), jnp.asarray(back, half)


def sum_tables(p):
    owner = np.arange(PACK) // p.groups
    lane_owner = np.repeat(owner, p.width)
    sums = np.zeros((2, 8, p.lanes), np.float32)
    wide = np.zeros((3, 8, 2, p.lanes), np.float32)
    for s in range(p.stack):
        sums[0, s] = lane_owner == s
        sums[1, p.stack + s] = lane_owner == s
        wide[:, s, 0] = lane_owner == s
        wide[:, p.stack + s, 1] = lane_owner == s
    wide = wide.reshape(24, 2, p.tiles, LANES).transpose(0, 2, 1, 3)
    return jnp.asarray(sums, half), jnp.asarray(wide.reshape(24, 2 * p.lanes), half)


def splits(space):
    return (MW // space) % 4 == 0 and space & (space - 1) == 0


def exchange_near(values):
    count = len(values)
    return tuple(
        value if x == 0 else lax.ppermute(value, "space", [(i, i ^ x) for i in range(count)])
        for x, value in enumerate(values)
    )


def exchange(value):
    return lax.all_to_all(value, "space", 0, 0, tiled=True)


def around(value, axis, size):
    gathered = [value]
    for step in range(1, size):
        gathered.append(
            lax.ppermute(value, axis, [(i, (i + step) % size) for i in range(size)])
        )
    return gathered


def reduced(p, value, kind):
    step = 1
    while step < p.space:
        wide = step > 1 and 4 * step <= p.space
        own = value.astype(kind)
        near, far, both = (
            lax.ppermute(own, "space", [(i, i ^ (step * k)) for i in range(p.space)])
            if k == 1 or wide
            else None
            for k in (1, 2, 3)
        )
        value = own.astype(single) + near.astype(single)
        if wide:
            value = value + (far.astype(single) + both.astype(single))
        step *= 4 if wide else 2
    return value


def on_device(space, chan, members, gain, shift, w_first, b_first, w_second, b_second, cotangent):
    p = Plan(members, w_first.shape[-1], space, chan)
    size = p.packs // 2
    grid = (size, p.steps)
    table, _, double_scale, mixed_plain, slope_plain = lon_tables(p)
    there_plain, back_table = lat_tables(p)
    slope_table, there_table = jnp.asarray(slope_plain, half), jnp.asarray(there_plain, half)
    mixed_table = jnp.asarray(mixed_plain, half)
    split = splits(space)
    if split:
        slope_near = by_distance(p, slope_plain, 2 * p.modes)
        mixed_near = by_distance(p, mixed_plain, 2 * p.modes)
        there_near = by_distance(p, there_plain, 2 * p.rows)
        me = lax.axis_index("space").astype(jnp.int32).reshape(1)
    own_spec = pl.BlockSpec(memory_space=pltpu.SMEM)
    sum_table, wide_table = sum_tables(p)
    affine = jnp.concatenate([gain] * p.stack + [shift] * p.stack).reshape(2, p.lanes)
    tokens_rows = PACK * p.turn_pad
    dft_flops = 2 * size * p.rows * tokens_rows * 2 * MW * p.lanes
    words = pltpu.VMEM((p.step, PACK, p.word_pad, LANES), single)
    lines = pltpu.VMEM((p.step, p.stack, p.word_pad * p.groups, LANES), single)
    turn_in = pltpu.VMEM((p.tiles, MW * 2 * p.rows, LANES), single)
    rows_scratch = pltpu.VMEM((p.step, 8, tokens_rows), single)

    def sent(wide):
        return jax.ShapeDtypeStruct((space, wide, size, p.modes, 2 * p.rows, p.lanes), half)

    returned = jax.ShapeDtypeStruct((space, 1, size, p.rows, 2 * p.modes, p.lanes), half)

    count = 2 * p.stack * p.rows
    stored = jax.ShapeDtypeStruct(members.shape, half)

    def out_call(body, ins, specs, outs, out_specs, scratch, flops, before):
        ins, specs = list(ins), list(specs)
        aliases = {}
        inner = body
        if before is not None:
            place, extra = len(ins), len(before)
            inner = lambda *refs: body(*refs[:place], *refs[place + extra :])
            ins += before
            specs += [pl.BlockSpec(memory_space=pl.ANY)] * extra
            aliases = {place + k: k for k in range(extra)}
        return call(inner, grid, tuple(ins), specs, outs, out_specs, scratch, flops, aliases)

    def spectra_out(wide, which, near):
        if near:
            one = jax.ShapeDtypeStruct(sent(wide).shape[1:], half)
            return [one] * space, [one_peer_spec(one, which)] * space
        return [sent(wide)], [peer_spec(sent(wide), which)]

    def cotangent_chunk(c, wide, near):
        outs, out_specs = spectra_out(wide, 0, near)
        ins, specs = (cotangent, table, double_scale), [whole_spec(table), whole_spec(double_scale)]
        if near:
            ins, specs = (*ins, me), [*specs, own_spec]
        return out_call(
            functools.partial(cotangent_kernel, p, near), ins,
            [stored_spec(p, c * size), *specs], outs, out_specs, [words, turn_in], dft_flops, None,
        )

    def stats_chunk(c):
        ins = (members, sum_table)
        outs = [
            jax.ShapeDtypeStruct((size, p.rows, tokens_rows, p.lanes), half),
            jax.ShapeDtypeStruct((size, count, tokens_rows), single),
        ]
        return call(
            functools.partial(stats_kernel, p), grid, ins,
            [stored_spec(p, c * size), whole_spec(sum_table)],
            outs, [part_spec(p, o) for o in outs], [words], dft_flops // 4,
        )

    def normalise_chunk(stats, tokens, before, near):
        tail = (affine, table, wide_table)
        ins = (*stats, tokens, *tail)
        specs = [part_spec(p, s) for s in (*stats, tokens)] + [whole_spec(v) for v in tail]
        if near:
            ins, specs = (*ins, me), [*specs, own_spec]
        which = 0 if before is None else 1
        outs, out_specs = spectra_out(which + 1, which, near)
        return out_call(
            functools.partial(normalise_kernel, p, near), ins, specs,
            outs, out_specs, [rows_scratch, turn_in], dft_flops, before,
        )

    step_modes = 2 if p.modes % 2 == 0 else 1
    wide_lanes = 2 * p.lanes

    def spectral_chunk(x_in, x_which, g_in, before, y_near, x_near):
        peers = len(x_in)
        tail = (there_near if peers > 1 else there_table, back_table)
        tail += (w_first, w_second, b_first, b_second)
        tail += () if before is None else (before,)
        specs = [whole_spec(v) for v in tail]
        if y_near or x_near:
            tail, specs = (*tail, me), [*specs, own_spec]

        def mode_spec(which):
            lead = (1, 1) if peers > 1 else (space, 1, 1)
            at = (which,) if peers > 1 else (0, which)
            return pl.BlockSpec(
                lead + (step_modes, 2 * p.rows, p.lanes), lambda b, m: at + (b, m, 0, 0)
            )

        outs, out_specs = [], []
        one = jax.ShapeDtypeStruct(returned.shape[1:], half)
        for near in (y_near, x_near):
            outs += [one] * space if near else [returned]
            out_specs += [one_peer_spec(one)] * space if near else [peer_spec(returned)]
        bias_rows = -(-4 * p.groups // 8) * 8
        totals = jax.ShapeDtypeStruct(
            (4 * p.groups * p.width + bias_rows, LANES), single if before is None else half
        )
        kept = pltpu.VMEM((p.modes * p.lat, wide_lanes), half)
        held = pltpu.VMEM((step_modes * p.lat, wide_lanes), single)
        brief = pltpu.VMEM((step_modes * p.lat, wide_lanes), half)
        turn_out = pltpu.VMEM((p.tiles, p.lat * 2 * p.modes, LANES), single)
        return call(
            functools.partial(
                spectral_kernel, p, step_modes, peers, y_near, x_near, before is not None
            ),
            (size, p.modes // step_modes), (*x_in, *g_in, *tail),
            [mode_spec(x_which)] * peers + [mode_spec(0)] * peers + specs,
            [*outs, totals],
            [*out_specs, whole_spec(totals)],
            [pltpu.VMEM((16, wide_lanes), single), pltpu.VMEM((2, wide_lanes), single)]
            + [kept] * 4 + [held] + [brief] * 3 + [turn_out] * 2
            + [pltpu.VMEM((wide_lanes, wide_lanes), single)] * 2
            + [pltpu.VMEM((wide_lanes, wide_lanes), half)] * 2,
            12 * size * p.modes * p.lat * wide_lanes * wide_lanes,
        )

    def mixed_chunk(c, rows_in, before):
        table_in = mixed_near if len(rows_in) > 1 else mixed_table
        return out_call(
            functools.partial(mixed_kernel, p, len(rows_in)), (*rows_in, table_in),
            rows_specs(rows_in) + [whole_spec(table_in)],
            [stored], [stored_spec(p, c * size)], [lines], dft_flops, before,
        )

    def rows_specs(rows_in):
        if len(rows_in) == 1:
            return [peer_part_spec(p, rows_in[0])]
        return [one_peer_part_spec(p, value) for value in rows_in]

    def slope_sums_chunk(stats, rows_in, tokens, before):
        near = len(rows_in) > 1
        tail = (affine, slope_near if near else slope_table, wide_table, sum_table)
        tail += () if before is None else (before,)
        outs = [
            jax.ShapeDtypeStruct((size, count, tokens_rows), half),
            jax.ShapeDtypeStruct((space, 2, p.lanes), single),
        ]
        return call(
            functools.partial(slope_sums_kernel, p, len(rows_in), before is not None),
            grid, (*stats, *rows_in, tokens, *tail),
            [part_spec(p, s) for s in stats] + rows_specs(rows_in)
            + [part_spec(p, tokens)] + [whole_spec(v) for v in tail],
            outs, [part_spec(p, outs[0]), whole_spec(outs[1])],
            [
                pltpu.VMEM((16, p.lanes), single), rows_scratch,
                pltpu.VMEM((count // p.steps, tokens_rows), single),
            ],
            dft_flops,
        )

    def input_grad_chunk(c, stats, parts, rows_in, tokens, before):
        near = len(rows_in) > 1
        tail = (affine, slope_near if near else slope_table, wide_table)
        return out_call(
            functools.partial(input_grad_kernel, p, len(rows_in)),
            (*stats, *parts, *rows_in, tokens, *tail),
            [part_spec(p, s) for s in (*stats, *parts)] + rows_specs(rows_in)
            + [part_spec(p, tokens)] + [whole_spec(v) for v in tail],
            [stored], [stored_spec(p, c * size)], [rows_scratch, rows_scratch, lines], dft_flops,
            before,
        )

    def channel_sums(value):
        return around(value, "chan", chan)

    def moved(values, near):
        return exchange_near(values) if near else (exchange(values[0]),)

    g0 = moved(cotangent_chunk(0, 1, False), False)
    tokens0, sums = stats_chunk(0)
    stats0 = channel_sums(sums)
    x0 = moved(normalise_chunk(stats0, tokens0, None, False), False)
    both1 = cotangent_chunk(1, 2, split)
    tokens1, sums = stats_chunk(1)
    stats1 = channel_sums(sums)
    both1 = moved(normalise_chunk(stats1, tokens1, both1, split), split)
    cut = space if split else 1
    *outs, totals = spectral_chunk(x0, 0, g0, None, split, False)
    dx0 = moved(outs[cut:], False)
    y0 = moved(outs[:cut], split)
    *outs, totals = spectral_chunk(both1, 1, both1, totals, False, split)
    dx1 = moved(outs[1:], split)
    y1 = moved(outs[:1], False)
    sums, params = slope_sums_chunk(stats0, dx0, tokens0, None)
    parts = channel_sums(sums)
    grad_input = input_grad_chunk(0, stats0, parts, dx0, tokens0, None)
    mixed = mixed_chunk(0, y0, None)
    sums, params = slope_sums_chunk(stats1, dx1, tokens1, params)
    parts = channel_sums(sums)
    grad_input = input_grad_chunk(1, stats1, parts, dx1, tokens1, grad_input)[0]
    mixed = mixed_chunk(1, y1, mixed)[0]

    size_w = p.groups * p.width
    flat = reduced(p, totals, half)[:, : p.width]
    grads = flat[: 4 * size_w].reshape((2,) + w_first.shape)
    bias_grads = flat[4 * size_w : 4 * size_w + 4 * p.groups].reshape((2,) + b_first.shape)
    params = exchange(params).sum(0)
    params = [
        sum(params[kind, s * size_w : (s + 1) * size_w] for s in range(p.stack)) for kind in range(2)
    ]
    return (
        mixed, grad_input, grads[0], bias_grads[0], grads[1], bias_grads[1], params[0], params[1]
    )


def solution(mesh):
    tokens = P(None, "space", "chan", None)
    weights = P(None, "chan", None, None)
    biases = P(None, "chan", None)
    placed = (tokens, P("chan"), P("chan"), weights, biases, weights, biases, tokens)
    return jax.shard_map(
        functools.partial(on_device, mesh.shape["space"], mesh.shape["chan"]),
        mesh=mesh,
        in_specs=placed,
        out_specs=(tokens, tokens, weights, biases, weights, biases, P("chan"), P("chan")),
        check_vma=False,
    )
```
